32 devices in a mesh: group: 2 (over y), tm: 4 (over z), seq: 2 (over x), mp: 2 (over core).
Axes of the slice: x: 2, y: 2, z: 4, core: 2. Of those that a mesh axis runs over, the one named last changes fastest.
Arguments:
- states: bfloat16 [8, 128, 5120], P(('group', 'tm'), 'seq'), parts along dimension 0, may hold values from -6 to 6
- start_step: int32 [2], P('group'), parts along dimension 0, may hold values from 0 to 96
- w_qkv: bfloat16 [3, 5120, 3072], P(None, 'tm', ('seq', 'mp')), may hold values from -0.078125 to 0.078125
- qk_gain: float32 [2, 3072], P(None, ('seq', 'mp')), may hold values from 0.25 to 1.75
- w_out: bfloat16 [5120, 3072], P('tm', ('seq', 'mp')), may hold values from -0.109375 to 0.109375
- time_proj: bfloat16 [256, 15360], P('tm'), may hold values from -0.375 to 0.375
Outputs:
- displacement: float32 [8, 128, 5120], P(('group', 'tm'), 'seq', 'mp'), parts along dimension 0
The draws below stay inside these ranges and needn't reach their ends.
There are 2 independent parts, one for each index of `group`. The reference program is written for one: setup_inputs(seed, part) draws one part's arguments, and reference() takes and returns one part's arrays. A program takes and returns all parts, laid end to end along the dimension named above; an argument that names none is the same for every part. Nothing has to cross between parts.
Inputs may be any that keep to these rules, and one draw needn't show every extreme that they name: `start_step`: the window lies inside the trajectory.
All inputs are finite; a program needn't handle non-finite values.
Results may differ from the reference program's by a relative error of at most 0.0029.
Values may be sent and summed in bfloat16 or wider, within the bound.
No kernel may reach another device: no remote copies, remote signals or barrier semaphores. Data moves between devices by JAX's collectives and lax.ppermute only.
A program may use at most 128 MiB of HBM per device.

```python
import jax
import jax.numpy as jnp
from jax import lax

D = 5120
HEADS = 24
HEAD_DIM = 128
FREQ = 256
STEPS = 100
W = 4
L = 128


def steps_of(stream_key, extent, pieces, smallest, high):
    loudness, own = 1.0, jax.random.fold_in(stream_key, 6)
    for position, parts in pieces:
        steps = jnp.exp(jax.random.uniform(jax.random.fold_in(own, position), (parts,), jnp.float32, smallest / len(pieces), high / len(pieces)))
        loudness = loudness * jnp.repeat(steps, extent[position] // parts).reshape([-1 if axis == position else 1 for axis in range(len(extent))])
    return loudness


def noise(rng, dims, deviation, reach, split=(), kind=jnp.bfloat16):
    loudness = steps_of(rng, dims, split, -0.22, 0.18) if split else 1.0
    result = jax.random.normal(rng, dims, jnp.float32) * deviation * loudness
    return jnp.minimum(jnp.maximum(result, -reach), reach).astype(kind)


def setup_inputs(seed: int = 0, part: int = 0) -> dict:
    key_list = jax.random.split(jax.random.key(seed), 7)
    own_keys = jax.random.split(jax.random.fold_in(key_list[6], part), 7)
    return {
        "states": noise(own_keys[0], (W, L, D), 1.0, 6.0, ((0, 4), (1, 2))),
        "start_step": jax.random.randint(own_keys[1], (1,), 0, STEPS - W + 1).astype(jnp.int32),
        "w_qkv": noise(key_list[2], (3, D, HEADS * HEAD_DIM), D ** -0.5, 0.078125, ((1, 4), (2, 4))),
        "qk_gain": jnp.clip(1.0 + 0.15 * jax.random.normal(key_list[3], (2, HEADS * HEAD_DIM), jnp.float32), 0.25, 1.75),
        "w_out": noise(key_list[4], (D, HEADS * HEAD_DIM), (HEADS * HEAD_DIM) ** -0.5, 0.109375, ((0, 4), (1, 4))),
        "time_proj": noise(key_list[5], (FREQ, 3 * D), FREQ ** -0.5, 0.375, ((0, 4),)),
    }


sample_shift = 5.0
norm_eps = 1e-06

def sigma_of(index):
    unit = 1.0 - index.astype(jnp.float32) / jnp.float32(STEPS)
    return sample_shift * unit / (1.0 + (sample_shift - 1.0) * unit)

def embed_time(sigma_now):
    half_freq = FREQ // 2
    ranks = jnp.arange(half_freq).astype(jnp.float32)
    freqs = jnp.exp(-jnp.log(jnp.float32(10000.0)) * ranks / jnp.float32(half_freq))
    angles = (1000.0 * sigma_now)[:, None] * freqs[None, :]
    return jnp.concatenate([jnp.cos(angles), jnp.sin(angles)], axis=1).astype(jnp.bfloat16)

def head_norm(values, gain):
    shaped = values.reshape(W, L, HEADS, HEAD_DIM)
    meansq = lax.optimization_barrier(jnp.mean(shaped * shaped, axis=-1, keepdims=True))
    scaled = shaped * lax.rsqrt(meansq + norm_eps) * gain.reshape(HEADS, HEAD_DIM)
    return scaled.astype(jnp.bfloat16)

def reference(states, start_step, w_qkv, qk_gain, w_out, time_proj):
    steps_idx = start_step[0].astype(jnp.int32) + jnp.arange(W).astype(jnp.int32)
    sigma_now = sigma_of(steps_idx)
    step_size = sigma_of(steps_idx + 1) - sigma_now
    emb = embed_time(sigma_now)
    modulation = jnp.dot(emb, time_proj, preferred_element_type=jnp.float32)
    shift = modulation[:, :D]
    scale = modulation[:, D:2 * D]
    gate = modulation[:, 2 * D:]
    field = states.astype(jnp.float32)
    mean = lax.optimization_barrier(jnp.mean(field, axis=-1, keepdims=True))
    centred = field - mean
    var = lax.optimization_barrier(jnp.mean(centred * centred, axis=-1, keepdims=True))
    normed = centred * lax.rsqrt(var + norm_eps)
    hidden = (normed * (1.0 + scale[:, None, :]) + shift[:, None, :]).astype(jnp.bfloat16)
    flat = hidden.reshape(W * L, D)
    query = head_norm(jnp.dot(flat, w_qkv[0], preferred_element_type=jnp.float32), qk_gain[0])
    keys = head_norm(jnp.dot(flat, w_qkv[1], preferred_element_type=jnp.float32), qk_gain[1])
    values = jnp.dot(flat, w_qkv[2], preferred_element_type=jnp.float32).astype(jnp.bfloat16).reshape(W, L, HEADS, HEAD_DIM)
    inv_root = 1.0 / jnp.sqrt(jnp.float32(HEAD_DIM))

    def one_head(operands):
        q_head, k_head, v_head = operands
        scores = jnp.einsum('wqd,wkd->wqk', q_head.astype(jnp.float32), k_head.astype(jnp.float32)) * inv_root
        expo = jnp.exp(scores)
        probs = (expo / lax.optimization_barrier(jnp.sum(expo, axis=-1, keepdims=True))).astype(jnp.bfloat16)
        return jnp.einsum('wqk,wkd->wqd', probs.astype(jnp.float32), v_head.astype(jnp.float32)).astype(jnp.bfloat16)
    heads_out = lax.map(one_head, (jnp.moveaxis(query, 2, 0), jnp.moveaxis(keys, 2, 0), jnp.moveaxis(values, 2, 0)))
    attn = jnp.moveaxis(heads_out, 0, 2).reshape(W * L, HEADS * HEAD_DIM)
    out = jnp.dot(attn, w_out.T, preferred_element_type=jnp.float32).reshape(W, L, D)
    drift = gate[:, None, :] * out
    increments = step_size[:, None, None] * drift
    return jnp.cumsum(increments, axis=0)
```

```python
import jax
import jax.numpy as jnp
from jax import lax
from jax.sharding import PartitionSpec as P

HEAD_DIM = 128
FREQ = 256
STEPS = 100


sample_shift = 5.0
norm_eps = 1e-06


def sigma_of(index):
    unit = 1.0 - index.astype(jnp.float32) / jnp.float32(STEPS)
    return sample_shift * unit / (1.0 + (sample_shift - 1.0) * unit)


def embed_time(sigma_now):
    half_freq = FREQ // 2
    ranks = jnp.arange(half_freq).astype(jnp.float32)
    freqs = jnp.exp(-jnp.log(jnp.float32(10000.0)) * ranks / jnp.float32(half_freq))
    angles = (1000.0 * sigma_now)[:, None] * freqs[None, :]
    return jnp.concatenate([jnp.cos(angles), jnp.sin(angles)], axis=1).astype(jnp.bfloat16)


def turn(block, axis, distance):
    size = lax.axis_size(axis)
    return lax.ppermute(block, axis, [(i, (i + distance) % size) for i in range(size)])


def take(array, index, dim=0):
    return lax.dynamic_index_in_dim(array, index, dim, keepdims=False)


def head_norm(values, gain):
    heads_dev = values.shape[-1] // HEAD_DIM
    shaped = values.reshape(values.shape[:-1] + (heads_dev, HEAD_DIM))
    meansq = jnp.mean(shaped * shaped, axis=-1, keepdims=True)
    scaled = shaped * lax.rsqrt(meansq + norm_eps) * gain.reshape(heads_dev, HEAD_DIM)
    return scaled.astype(jnp.bfloat16)


def attend(query, keys, values):
    inv_root = 1.0 / jnp.sqrt(jnp.float32(query.shape[-1]))
    scores = jnp.einsum("wqhd,wkhd->whqk", query, keys, preferred_element_type=jnp.float32)
    expo = jnp.exp(scores * inv_root)
    probs = (expo / jnp.sum(expo, axis=-1, keepdims=True)).astype(jnp.bfloat16)
    return jnp.einsum(
        "whqk,wkhd->wqhd", probs, values, preferred_element_type=jnp.float32
    ).astype(jnp.bfloat16)


def on_device(states, start_step, w_qkv, qk_gain, w_out, time_proj):
    frames, tok, width = states.shape
    n_tm, n_seq, n_mp = (lax.axis_size(name) for name in ("tm", "seq", "mp"))
    z, m = lax.axis_index("tm"), lax.axis_index("mp")
    part = tok // n_mp
    depth, cols = w_qkv.shape[1:]
    half = depth // n_mp
    window = frames * n_tm
    freq_rows = time_proj.shape[0]

    mine = lax.dynamic_slice_in_dim(states, m * part, part, 1).reshape(frames, part, n_tm, depth)
    raw_tm = [take(mine, z, 2)] + [turn(take(mine, (z + k) % n_tm, 2), "tm", k) for k in range(1, n_tm)]
    raw = jnp.stack(raw_tm)
    raw = jnp.stack([raw] + [turn(raw, "seq", j) for j in range(1, n_seq)], axis=1)
    raw = jnp.stack([raw] + [turn(raw, "mp", i) for i in range(1, n_mp)], axis=1)

    field = states.astype(jnp.float32)
    mean = jnp.mean(field, axis=-1)
    centred = field - mean[..., None]
    var = jnp.mean(centred * centred, axis=-1)
    stats = jnp.stack([mean, lax.rsqrt(var + norm_eps)])
    stats = jnp.stack([stats] + [turn(stats, "tm", k) for k in range(1, n_tm)])
    stats = jnp.stack([stats] + [turn(stats, "seq", j) for j in range(1, n_seq)], axis=1)
    stats = stats.reshape(n_tm, n_seq, 2, frames, n_mp, part)
    stats = jnp.stack([take(stats, (m - i) % n_mp, 4) for i in range(n_mp)], axis=1)

    steps_idx = start_step[0] + jnp.arange(window)
    sigma_now = sigma_of(steps_idx)
    step_size = sigma_of(steps_idx + 1) - sigma_now
    emb = embed_time(sigma_now)
    emb_cols = lax.dynamic_slice_in_dim(emb, z * freq_rows, freq_rows, 1)
    partial = jnp.dot(emb_cols, time_proj, preferred_element_type=jnp.float32)
    partial = partial.reshape(window, 3, n_tm, depth)
    modulation = take(partial, z, 2)
    for k in range(1, n_tm):
        modulation = modulation + turn(take(partial, (z + k) % n_tm, 2), "tm", k)
    modulation = modulation.reshape(n_tm, frames, 3, depth)
    modulation = jnp.stack([take(modulation, (z - k) % n_tm) for k in range(n_tm)])
    sizes = step_size.reshape(n_tm, frames)

    shift, scale, gate = (modulation[:, None, None, :, None, c, :] for c in range(3))
    normed = (raw.astype(jnp.float32) - stats[:, :, :, 0, :, :, None]) * stats[:, :, :, 1, :, :, None]
    hidden = (normed * (1.0 + scale) + shift).astype(jnp.bfloat16)
    rows = n_mp * n_seq * frames * part
    hidden = hidden.reshape(n_tm, rows, depth)

    proj = jnp.einsum("krd,cdh->kcrh", hidden, w_qkv, preferred_element_type=jnp.float32)
    right = left = jnp.zeros((), jnp.float16)
    for t in range(n_tm - 1):
        send_right = (right.astype(jnp.float32) + proj[(t + 1) % n_tm]).astype(jnp.float16)
        send_left = (left.astype(jnp.float32) + proj[n_tm - 1 - t]).astype(jnp.float16)
        right = lax.ppermute(send_right, "tm", [(i, i + 1) for i in range(t + 1)])
        left = lax.ppermute(send_left, "tm", [(n_tm - 1 - i, n_tm - 2 - i) for i in range(t + 1)])
    whole = proj[0] + right.astype(jnp.float32) + left.astype(jnp.float32)
    whole = whole.reshape(3, n_mp * n_seq, frames, part, cols)
    whole = whole.transpose(0, 2, 1, 3, 4).reshape(3, frames, n_mp * n_seq * part, cols)
    query = head_norm(whole[0], qk_gain[0])
    keys = head_norm(whole[1], qk_gain[1])
    values = whole[2].astype(jnp.bfloat16).reshape(query.shape)
    attn = attend(query, keys, values)
    attn = attn.reshape(frames, n_mp, n_seq, part, cols)

    attn = jnp.stack([attn[:, :, 0]] + [turn(attn[:, :, j], "seq", -j) for j in range(1, n_seq)])
    attn = jnp.stack([attn] + [turn(attn, "tm", k) for k in range(1, n_tm)])
    cores = [attn]
    for i in range(1, n_mp):
        cores.append(turn(jnp.roll(attn, i, axis=3), "mp", i))
    attn = jnp.stack(cores)

    share = w_out.reshape(n_mp, half, cols)
    share = jnp.stack([take(share, m)] + [turn(take(share, (m + i) % n_mp), "mp", i) for i in range(1, n_mp)])
    share = jnp.stack([share] + [turn(share, "seq", -j) for j in range(1, n_seq)])
    out = jnp.einsum("lkjfipc,jlec->kfipe", attn, share, preferred_element_type=jnp.float32)

    blocks = [(z - k) % n_tm for k in range(n_tm)]
    gate_own = take(gate.reshape(n_tm, frames, n_mp, half), m, 2)
    local = [
        jnp.cumsum(take(sizes, blocks[k])[:, None, None, None] * (gate_own[k][:, None, None, :] * out[k]), axis=0)
        for k in range(n_tm)
    ]
    moved = []
    for k in range(n_tm):
        total = local[k]
        for other in range(n_tm):
            if other != k:
                total = total + jnp.where(blocks[other] < blocks[k], local[other][-1], 0.0)[None]
        moved.append(total)
    moved = jnp.stack(moved)
    moved = jnp.stack([take(moved, (m - i) % n_mp, 2) for i in range(n_mp)], axis=2)
    arrived = [moved[0]] + [
        turn(moved[k].astype(jnp.bfloat16), "tm", -k).astype(jnp.float32) for k in range(1, n_tm)
    ]
    by_slice = jnp.stack(arrived)
    by_slice = jnp.stack([take(by_slice, (s - z) % n_tm) for s in range(n_tm)])
    by_slice = by_slice.reshape(n_mp, n_tm // n_mp, frames, tok, half)
    final = [take(by_slice, m)]
    for i in range(1, n_mp):
        final.append(turn(take(by_slice, (m + i) % n_mp).astype(jnp.bfloat16), "mp", i).astype(jnp.float32))
    final = jnp.stack(final)
    final = jnp.stack([take(final, (m - i) % n_mp) for i in range(n_mp)])
    return final.transpose(2, 3, 1, 0, 4).reshape(frames, tok, width // n_mp)


def solution(mesh):
    return jax.shard_map(
        on_device,
        mesh=mesh,
        in_specs=(
            P(("group", "tm"), "seq", None),
            P("group"),
            P(None, "tm", ("seq", "mp")),
            P(None, ("seq", "mp")),
            P("tm", ("seq", "mp")),
            P("tm", None),
        ),
        out_specs=P(("group", "tm"), "seq", "mp"),
        check_vma=False,
    )
```

```python
import functools

import jax
import jax.numpy as jnp
from jax import lax
from jax.experimental import pallas as pl
from jax.experimental.pallas import tpu as pltpu
from jax.sharding import PartitionSpec as P


HEAD_DIM = 128
FREQ = 256
STEPS = 100


sample_shift = 5.0
norm_eps = 1e-06


def sigma_of(index):
    unit = 1.0 - index.astype(jnp.float32) / jnp.float32(STEPS)
    return sample_shift * unit / (1.0 + (sample_shift - 1.0) * unit)


def embed_time(sigma_now):
    half_freq = FREQ // 2
    ranks = jnp.arange(half_freq).astype(jnp.float32)
    freqs = jnp.exp(-jnp.log(jnp.float32(10000.0)) * ranks / jnp.float32(half_freq))
    angles = (1000.0 * sigma_now)[:, None] * freqs[None, :]
    return jnp.concatenate([jnp.cos(angles), jnp.sin(angles)], axis=1).astype(jnp.bfloat16)


def turn(block, axis, distance):
    size = lax.axis_size(axis)
    return lax.ppermute(block, axis, [(i, (i + distance) % size) for i in range(size)])


def take(array, index, dim=0):
    return lax.dynamic_index_in_dim(array, index, dim, keepdims=False)


def head_norm(values, gain):
    meansq = jnp.mean(values * values, axis=-1, keepdims=True)
    return (values * lax.rsqrt(meansq + norm_eps) * gain).astype(jnp.bfloat16)


def attend_kernel(n_seq, heads, *refs):
    gain_ref, parts, outs = refs[0], refs[1 : 1 + n_seq], refs[1 + n_seq :]
    inv_root = 1.0 / jnp.sqrt(jnp.float32(HEAD_DIM))
    rows = parts[0].shape[2]
    for h in range(heads):
        lanes = pl.ds(h * HEAD_DIM, HEAD_DIM)
        q, k, v = (
            jnp.concatenate([p[c, 0, :, lanes] for p in parts], axis=0) for c in range(3)
        )
        q = head_norm(q, gain_ref[0:1, lanes])
        k = head_norm(k, gain_ref[1:2, lanes])
        scores = lax.dot_general(
            q, k, (((1,), (1,)), ((), ())), preferred_element_type=jnp.float32
        )
        expo = jnp.exp(scores * inv_root)
        probs = (expo / jnp.sum(expo, axis=-1, keepdims=True)).astype(jnp.bfloat16)
        attn = jnp.dot(
            probs, v.astype(jnp.bfloat16), preferred_element_type=jnp.float32
        ).astype(jnp.bfloat16)
        for j, out in enumerate(outs):
            out[0, :, lanes] = attn[j * rows : (j + 1) * rows]


def attend(parts, gain):
    n_seq = len(parts)
    _, frames, rows, cols = parts[0].shape
    heads = cols // HEAD_DIM
    group = 3 if heads % 3 == 0 else 1
    width = group * HEAD_DIM
    tokens = rows * n_seq
    out = jax.ShapeDtypeStruct((frames, rows, cols), jnp.bfloat16)
    return pl.pallas_call(
        functools.partial(attend_kernel, n_seq, group),
        grid=(frames, heads // group),
        in_specs=[pl.BlockSpec((2, width), lambda f, h: (0, h))]
        + [pl.BlockSpec((3, 1, rows, width), lambda f, h: (0, f, 0, h))] * n_seq,
        out_specs=[pl.BlockSpec((1, rows, width), lambda f, h: (f, 0, h))] * n_seq,
        out_shape=[out] * n_seq,
        cost_estimate=pl.CostEstimate(
            flops=4 * frames * heads * tokens * tokens * HEAD_DIM,
            bytes_accessed=14 * frames * tokens * cols,
            transcendentals=frames * heads * tokens * tokens,
        ),
        name="attend",
    )(gain, *parts)


def out_kernel(dims, place_ref, coef_ref, *refs):
    n_tm, n_seq, n_mp, frames, part, cols = dims
    attn_refs = refs[: n_tm * n_mp]
    w_refs = refs[n_tm * n_mp : n_tm * n_mp + n_seq * n_mp]
    own_ref, moved_ref, rows_scr, sum_scr = refs[n_tm * n_mp + n_seq * n_mp :]
    z, m = place_ref[0], place_ref[1]
    block = n_mp * part
    per = frames * block

    @pl.when(pl.program_id(0) == 0)
    def _():
        for k in range(n_tm):
            for l in range(n_mp):
                piece = attn_refs[k * n_mp + l]
                for j in range(n_seq):
                    for f in range(frames):
                        for i in range(n_mp):
                            source = (i - l) % n_mp * part
                            at = k * per + f * block + i * part
                            lane = (j * n_mp + l) * cols
                            rows_scr[at : at + part, lane : lane + cols] = piece[
                                j, f, source : source + part, :
                            ]

    total = None
    for j in range(n_seq):
        for l in range(n_mp):
            lane = (j * n_mp + l) * cols
            product = lax.dot_general(
                rows_scr[:, lane : lane + cols],
                w_refs[j * n_mp + l][...],
                (((1,), (1,)), ((), ())),
                preferred_element_type=jnp.float32,
            )
            total = product if total is None else total + product
    for k in range(n_tm):
        own = lax.rem(z - k + n_tm, n_tm)
        sum_scr[own] = total[k * per : (k + 1) * per]
    running = None
    for s in range(n_tm):
        k = lax.rem(z - s + n_tm, n_tm)
        for f in range(frames):
            drift = sum_scr[s, f * block : (f + 1) * block] * coef_ref[k, f : f + 1]
            running = drift if running is None else running + drift
            for i in range(n_mp):
                at = pl.multiple_of(lax.rem(m - i + n_mp, n_mp) * part, part)
                piece = running[i * part : (i + 1) * part]
                moved_ref[k, f, pl.ds(at, part), :] = piece.astype(jnp.bfloat16)

                @pl.when(k == 0)
                def _():
                    own_ref[f, pl.ds(at, part), :] = piece


def project(attn, weights, coef, place, dims):
    n_tm, n_seq, n_mp, frames, part, cols = dims
    half = weights[0][0].shape[0]
    step = 128 if half % 128 == 0 else half
    tok = n_mp * part
    rows = n_tm * frames * tok
    deep = n_seq * n_mp * cols
    return pl.pallas_call(
        functools.partial(out_kernel, dims),
        grid_spec=pltpu.PrefetchScalarGridSpec(
            num_scalar_prefetch=1,
            grid=(half // step,),
            in_specs=[pl.BlockSpec((n_tm, frames, step), lambda e, p: (0, 0, e))]
            + [pl.BlockSpec((n_seq, frames, tok, cols), lambda e, p: (0, 0, 0, 0))]
            * (n_tm * n_mp)
            + [pl.BlockSpec((step, cols), lambda e, p: (e, 0))] * (n_seq * n_mp),
            out_specs=[
                pl.BlockSpec((frames, tok, step), lambda e, p: (0, 0, e)),
                pl.BlockSpec((n_tm, frames, tok, step), lambda e, p: (0, 0, 0, e)),
            ],
            scratch_shapes=[
                pltpu.VMEM((rows, deep), jnp.bfloat16),
                pltpu.VMEM((n_tm, frames * tok, step), jnp.float32),
            ],
        ),
        out_shape=[
            jax.ShapeDtypeStruct((frames, tok, half), jnp.float32),
            jax.ShapeDtypeStruct((n_tm, frames, tok, half), jnp.bfloat16),
        ],
        cost_estimate=pl.CostEstimate(
            flops=2 * rows * deep * half, bytes_accessed=2 * (rows + half) * deep, transcendentals=0
        ),
        name="project",
    )(place, coef, *[a for k in attn for a in k], *[w for j in weights for w in j])


def sweep(states, start_step, w_qkv, qk_gain, w_out, time_proj):
    frames, tok, width = states.shape
    n_tm, n_seq, n_mp = (lax.axis_size(name) for name in ("tm", "seq", "mp"))
    z, m = lax.axis_index("tm"), lax.axis_index("mp")
    part = tok // n_mp
    depth, cols = w_qkv.shape[1:]
    half = depth // n_mp
    window = frames * n_tm
    freq_rows = time_proj.shape[0]

    mine = lax.dynamic_slice_in_dim(states, m * part, part, 1).reshape(frames, part, n_tm, depth)
    raw = [take(mine, z, 2)]
    for k in range(1, n_tm):
        raw.append(turn(take(mine, (z + k) % n_tm, 2), "tm", k))
    raw = jnp.stack(raw)
    sides = [raw]
    for j in range(1, n_seq):
        sides.append(turn(raw, "seq", j))
    rows = []
    for side in sides:
        rows.append([side] + [turn(side, "mp", i) for i in range(1, n_mp)])

    field = states.astype(jnp.float32)
    mean = jnp.mean(field, axis=-1)
    centred = field - mean[..., None]
    var = jnp.mean(centred * centred, axis=-1)
    stats = jnp.stack([mean, lax.rsqrt(var + norm_eps)])
    stats = jnp.stack([stats] + [turn(stats, "seq", j) for j in range(1, n_seq)])
    extra = stats.reshape(-1)
    extra_rows = -(-extra.shape[0] // depth)
    extra = jnp.pad(extra, (0, extra_rows * depth - extra.shape[0])).reshape(extra_rows, depth)

    steps_idx = start_step[0] + jnp.arange(window)
    sigma_now = sigma_of(steps_idx)
    step_size = sigma_of(steps_idx + 1) - sigma_now
    emb = embed_time(sigma_now)
    emb_cols = lax.dynamic_slice_in_dim(emb, z * freq_rows, freq_rows, 1)
    partial = jnp.dot(emb_cols, time_proj, preferred_element_type=jnp.float32)
    partial = partial.reshape(window * 3, n_tm, depth)
    modulation = take(partial, z, 1)
    extras = [extra]
    for k in range(1, n_tm):
        block = jnp.concatenate([take(partial, (z + k) % n_tm, 1), extra])
        block = turn(block, "tm", k)
        modulation = modulation + block[: window * 3]
        extras.append(block[window * 3 :])
    modulation = modulation.reshape(n_tm, frames, 3, depth)
    modulation = jnp.stack([take(modulation, (z - k) % n_tm) for k in range(n_tm)])
    sizes = step_size.reshape(n_tm, frames)
    stats = jnp.stack(extras).reshape(n_tm, -1)[:, : n_seq * 2 * frames * tok]
    stats = stats.reshape(n_tm, n_seq, 2, frames, n_mp, part)

    shift, scale, gate = (modulation[:, :, c] for c in range(3))

    def hidden_of(j):
        blocks = []
        for i in range(n_mp):
            stat = take(stats[:, j], (m - i) % n_mp, 3)[..., None]
            normed = (rows[j][i].astype(jnp.float32) - stat[:, 0]) * stat[:, 1]
            blocks.append(normed * (1.0 + scale[:, :, None]) + shift[:, :, None])
        return jnp.stack(blocks, axis=2).astype(jnp.bfloat16)

    proj, right, left = [], [], []
    for j in range(n_seq):
        hidden = hidden_of(j).reshape(n_tm, frames * tok, depth)
        proj.append(jnp.einsum("krd,cdh->kcrh", hidden, w_qkv, preferred_element_type=jnp.float32))
        right.append(None)
        left.append(None)
    for t in range(n_tm - 1):
        for j in range(n_seq):
            send_right, send_left = proj[j][(t + 1) % n_tm], proj[j][n_tm - 1 - t]
            if t:
                right[j], left[j] = lax.optimization_barrier((right[j], left[j]))
                send_right = send_right + right[j].astype(jnp.float32)
                send_left = send_left + left[j].astype(jnp.float32)
            send_right, send_left = send_right.astype(jnp.float16), send_left.astype(jnp.float16)
            right[j] = lax.ppermute(send_right, "tm", [(i, i + 1) for i in range(t + 1)])
            left[j] = lax.ppermute(
                send_left, "tm", [(n_tm - 1 - i, n_tm - 2 - i) for i in range(t + 1)]
            )
    parts = [
        (p[0] + r.astype(jnp.float32) + l.astype(jnp.float32)).reshape(3, frames, tok, cols)
        for p, r, l in zip(proj, right, left)
    ]
    attn = attend(parts, qk_gain)

    attn = jnp.stack([attn[0]] + [turn(attn[j], "seq", -j) for j in range(1, n_seq)])
    gathered = [attn]
    for k in range(1, n_tm):
        gathered.append(turn(attn, "tm", k))
    gathered = [[g] + [turn(g, "mp", i) for i in range(1, n_mp)] for g in gathered]

    share = w_out.reshape(n_mp, half, cols)
    shares = [take(share, m)]
    shares += [turn(take(share, (m + i) % n_mp), "mp", i) for i in range(1, n_mp)]
    weights = [shares]
    for j in range(1, n_seq):
        weights.append([turn(s, "seq", -j) for s in shares])

    gate_own = take(gate.reshape(n_tm, frames, n_mp, half), m, 2)
    coef = jnp.stack([take(sizes, (z - k) % n_tm) for k in range(n_tm)])[..., None] * gate_own
    place = jnp.stack([z, m]).astype(jnp.int32)
    own, moved = project(
        gathered, weights, coef, place, (n_tm, n_seq, n_mp, frames, part, cols)
    )
    arrived = [own]
    for k in range(1, n_tm):
        arrived.append(turn(moved[k], "tm", -k).astype(jnp.float32))
    by_slice = jnp.stack(arrived)
    by_slice = jnp.stack([take(by_slice, (s - z) % n_tm) for s in range(n_tm)])
    by_slice = by_slice.reshape(n_mp, n_tm // n_mp, frames, tok, half)
    final = [take(by_slice, m)]
    for i in range(1, n_mp):
        final.append(turn(take(by_slice, (m + i) % n_mp).astype(jnp.bfloat16), "mp", i).astype(jnp.float32))
    final = jnp.stack(final)
    final = jnp.stack([take(final, (m - i) % n_mp) for i in range(n_mp)])
    return final.transpose(2, 3, 1, 0, 4).reshape(frames, tok, width // n_mp)


def solution(mesh):
    return jax.shard_map(
        sweep,
        mesh=mesh,
        in_specs=(
            P(("group", "tm"), "seq", None),
            P("group"),
            P(None, "tm", ("seq", "mp")),
            P(None, ("seq", "mp")),
            P("tm", ("seq", "mp")),
            P("tm", None),
        ),
        out_specs=P(("group", "tm"), "seq", "mp"),
        check_vma=False,
    )
```

```python
import functools

import jax
import jax.numpy as jnp
from jax import lax
from jax.experimental import pallas as pl
from jax.experimental.pallas import tpu as pltpu
from jax.sharding import PartitionSpec as P


HEAD_DIM = 128
FREQ = 256
STEPS = 100
LANES = 128


sample_shift = 5.0
norm_eps = 1e-06


def sigma_of(index):
    unit = 1.0 - index.astype(jnp.float32) / jnp.float32(STEPS)
    return sample_shift * unit / (1.0 + (sample_shift - 1.0) * unit)


def turn(block, axis, distance):
    size = lax.axis_size(axis)
    return lax.ppermute(block, axis, [(i, (i + distance) % size) for i in range(size)])


def take(array, index, dim=0):
    return lax.dynamic_index_in_dim(array, index, dim, keepdims=False)


def head_norm(values, gain):
    meansq = jnp.mean(values * values, axis=-1, keepdims=True)
    return (values * lax.rsqrt(meansq + norm_eps) * gain).astype(jnp.bfloat16)


def attend_kernel(n_seq, heads, *refs):
    gain_ref, parts, outs = refs[0], refs[1 : 1 + n_seq], refs[1 + n_seq :]
    inv_root = 1.0 / jnp.sqrt(jnp.float32(HEAD_DIM))
    rows = parts[0].shape[2]
    for h in range(heads):
        lanes = pl.ds(h * HEAD_DIM, HEAD_DIM)
        q, k, v = (
            jnp.concatenate([p[c, 0, :, lanes] for p in parts], axis=0) for c in range(3)
        )
        q = head_norm(q, gain_ref[0:1, lanes])
        k = head_norm(k, gain_ref[1:2, lanes])
        scores = lax.dot_general(
            q, k, (((1,), (1,)), ((), ())), preferred_element_type=jnp.float32
        )
        expo = jnp.exp(scores * inv_root)
        probs = (expo / jnp.sum(expo, axis=-1, keepdims=True)).astype(jnp.bfloat16)
        attn = jnp.dot(
            probs, v.astype(jnp.bfloat16), preferred_element_type=jnp.float32
        ).astype(jnp.bfloat16)
        for j, out in enumerate(outs):
            out[0, :, lanes] = attn[j * rows : (j + 1) * rows]


def attend(parts, gain):
    n_seq = len(parts)
    _, frames, rows, cols = parts[0].shape
    heads = cols // HEAD_DIM
    group = 3 if heads % 3 == 0 else 1
    width = group * HEAD_DIM
    tokens = rows * n_seq
    out = jax.ShapeDtypeStruct((frames, rows, cols), jnp.bfloat16)
    return pl.pallas_call(
        functools.partial(attend_kernel, n_seq, group),
        grid=(frames, heads // group),
        in_specs=[pl.BlockSpec((2, width), lambda f, h: (0, h))]
        + [pl.BlockSpec((3, 1, rows, width), lambda f, h: (0, f, 0, h))] * n_seq,
        out_specs=[pl.BlockSpec((1, rows, width), lambda f, h: (f, 0, h))] * n_seq,
        out_shape=[out] * n_seq,
        cost_estimate=pl.CostEstimate(
            flops=4 * frames * heads * tokens * tokens * HEAD_DIM,
            bytes_accessed=14 * frames * tokens * cols,
            transcendentals=frames * heads * tokens * tokens,
        ),
        name="attend",
    )(gain, *parts)


def spread_kernel(n_tm, place_ref, states_ref, *outs):
    z, m = place_ref[0], place_ref[1]
    frames, _, width = states_ref.shape
    part, depth = outs[0].shape[1], width // n_tm
    own = pl.ds(pl.multiple_of(m * part, part), part)
    lane = lax.broadcasted_iota(jnp.int32, (part, LANES), 1)
    for f in range(frames):
        field = states_ref[f, own, :].astype(jnp.float32)
        mean = jnp.mean(field, axis=-1, keepdims=True)
        centred = field - mean
        var = jnp.mean(centred * centred, axis=-1, keepdims=True)
        tail = jnp.zeros((part, LANES), jnp.float32)
        for place, rest in enumerate((mean, lax.rsqrt(var + norm_eps))):
            for term in range(3):
                cut = rest.astype(jnp.bfloat16).astype(jnp.float32)
                tail = jnp.where(lane == 3 * place + term, cut, tail)
                rest = rest - cut
        tail = tail.astype(jnp.bfloat16)
        for k, out in enumerate(outs):
            out[f, :, depth:] = tail
            for s in range(n_tm):

                @pl.when(lax.rem(z + k, n_tm) == s)
                def _():
                    out[f, :, :depth] = states_ref[f, own, s * depth : (s + 1) * depth]


def spread(states, place, n_tm, part):
    frames, _, width = states.shape
    out = jax.ShapeDtypeStruct((frames, part, width // n_tm + LANES), jnp.bfloat16)
    return pl.pallas_call(
        functools.partial(spread_kernel, n_tm),
        in_specs=[pl.BlockSpec(memory_space=pltpu.SMEM), pl.BlockSpec(memory_space=pltpu.VMEM)],
        out_specs=[pl.BlockSpec(memory_space=pltpu.VMEM)] * n_tm,
        out_shape=[out] * n_tm,
        cost_estimate=pl.CostEstimate(
            flops=10 * part * width, bytes_accessed=4 * part * width, transcendentals=0
        ),
        name="spread",
    )(place, states)


def time_kernel(n_tm, place_ref, step_ref, proj_ref, *outs):
    z = place_ref[0]
    freq_rows, wide = proj_ref.shape
    window, depth = outs[0].shape[1:]
    half_freq = FREQ // 2
    index = step_ref[0] + lax.broadcasted_iota(jnp.int32, (window, freq_rows), 0)
    feature = z * freq_rows + lax.broadcasted_iota(jnp.int32, (window, freq_rows), 1)
    late = feature >= half_freq
    rank = jnp.where(late, feature - half_freq, feature).astype(jnp.float32)
    freqs = jnp.exp(-jnp.log(jnp.float32(10000.0)) * rank / jnp.float32(half_freq))
    angles = (1000.0 * sigma_of(index)) * freqs
    emb = jnp.where(late, jnp.sin(angles), jnp.cos(angles)).astype(jnp.bfloat16)
    for k, out in enumerate(outs):
        for s in range(n_tm):

            @pl.when(lax.rem(z + k, n_tm) == s)
            def _():
                for c in range(3):
                    first = c * (wide // 3) + s * depth
                    out[c] = jnp.dot(
                        emb, proj_ref[:, first : first + depth], preferred_element_type=jnp.float32
                    )


def time_shares(start_step, time_proj, place, n_tm, window):
    freq_rows, wide = time_proj.shape
    out = jax.ShapeDtypeStruct((3, window, wide // (3 * n_tm)), jnp.float32)
    smem, vmem = (pl.BlockSpec(memory_space=space) for space in (pltpu.SMEM, pltpu.VMEM))
    return pl.pallas_call(
        functools.partial(time_kernel, n_tm),
        in_specs=[smem, smem, vmem],
        out_specs=[vmem] * n_tm,
        out_shape=[out] * n_tm,
        cost_estimate=pl.CostEstimate(
            flops=2 * window * freq_rows * wide, bytes_accessed=2 * freq_rows * wide, transcendentals=0
        ),
        name="time_shares",
    )(place, start_step, time_proj)


def qkv_kernel(n_tm, n_mp, place_ref, *refs):
    shares, rows, w_ref = refs[:n_tm], refs[n_tm : n_tm + n_mp], refs[n_tm + n_mp]
    proj_ref, mod_scr, hidden_scr = refs[n_tm + n_mp + 1 :]
    z = place_ref[0]
    _, frames, part, wide = rows[0].shape
    depth = wide - LANES

    @pl.when((pl.program_id(0) == 0) & (pl.program_id(1) == 0))
    def _():
        total = shares[0][...]
        for share in shares[1:]:
            total = total + share[...]
        mod_scr[...] = total
        for k in range(n_tm):
            for f in range(frames):
                step = pl.ds(lax.rem(z - k + n_tm, n_tm) * frames + f, 1)
                shift, scale = mod_scr[0, step, :], mod_scr[1, step, :]
                for i in range(n_mp):
                    tail = rows[i][k, f, :, depth:].astype(jnp.float32)
                    mean = tail[:, 0:1] + tail[:, 1:2] + tail[:, 2:3]
                    rstd = tail[:, 3:4] + tail[:, 4:5] + tail[:, 5:6]
                    normed = (rows[i][k, f, :, :depth].astype(jnp.float32) - mean) * rstd
                    at = ((k * frames + f) * n_mp + i) * part
                    hidden_scr[at : at + part, :] = (normed * (1.0 + scale) + shift).astype(
                        jnp.bfloat16
                    )

    product = jnp.dot(hidden_scr[...], w_ref[0], preferred_element_type=jnp.float32)
    proj_ref[:, 0] = product.reshape(proj_ref.shape[0], proj_ref.shape[2], proj_ref.shape[3])


def qkv(shares, rows, w_qkv, place):
    n_tm, n_mp = len(shares), len(rows)
    _, frames, part, _ = rows[0].shape
    three, depth, cols = w_qkv.shape
    window = shares[0].shape[1]
    step = 384 if cols % 384 == 0 else cols
    block = frames * n_mp * part
    return pl.pallas_call(
        functools.partial(qkv_kernel, n_tm, n_mp),
        grid_spec=pltpu.PrefetchScalarGridSpec(
            num_scalar_prefetch=1,
            grid=(three, cols // step),
            in_specs=[pl.BlockSpec(shares[0].shape, lambda c, h, p: (0, 0, 0))] * n_tm
            + [pl.BlockSpec(rows[0].shape, lambda c, h, p: (0, 0, 0, 0))] * n_mp
            + [pl.BlockSpec((1, depth, step), lambda c, h, p: (c, 0, h))],
            out_specs=pl.BlockSpec((n_tm, 1, block, step), lambda c, h, p: (0, c, 0, h)),
            scratch_shapes=[
                pltpu.VMEM((3, window, depth), jnp.float32),
                pltpu.VMEM((n_tm * block, depth), jnp.bfloat16),
            ],
        ),
        out_shape=jax.ShapeDtypeStruct((n_tm, three, block, cols), jnp.float32),
        cost_estimate=pl.CostEstimate(
            flops=2 * n_tm * block * depth * three * cols,
            bytes_accessed=2 * three * depth * cols + 4 * n_tm * block * three * cols,
            transcendentals=0,
        ),
        name="qkv",
    )(place, *shares, *rows, w_qkv)


def project_kernel(dims, place_ref, coef_ref, *refs):
    n_tm, n_seq, n_mp, frames, part, _ = dims
    attn_refs = refs[: n_tm * n_mp]
    w_refs = refs[n_tm * n_mp : n_tm * n_mp + n_seq * n_mp]
    outs = refs[n_tm * n_mp + n_seq * n_mp :]
    own_ref, moved_refs, (rows_scr, w_scr, sum_scr, sems) = outs[0], outs[1:-4], outs[-4:]
    z, m = place_ref[0], place_ref[1]
    block = n_mp * part
    per = frames * block
    copies = []
    for j in range(n_seq):
        for l in range(n_mp):
            at = j * n_mp + l
            group = [pltpu.make_async_copy(w_refs[at], w_scr.at[at], sems.at[at, 0])]
            for k in range(n_tm):
                for f in range(frames):
                    for i in range(n_mp):
                        first = k * per + f * block + i * part
                        source = (i - l) % n_mp * part
                        group.append(
                            pltpu.make_async_copy(
                                attn_refs[k * n_mp + l].at[j, f, pl.ds(source, part)],
                                rows_scr.at[at, pl.ds(first, part)],
                                sems.at[at, len(group)],
                            )
                        )
            for copy in group:
                copy.start()
            copies.append(group)
    total = None
    for at, group in enumerate(copies):
        for copy in group:
            copy.wait()
        product = lax.dot_general(
            rows_scr[at], w_scr[at], (((1,), (1,)), ((), ())), preferred_element_type=jnp.float32
        )
        total = product if total is None else total + product
    for k in range(n_tm):
        for f in range(frames):
            first = k * per + f * block
            drift = total[first : first + block] * coef_ref[k, f : f + 1]
            sum_scr[lax.rem(z - k + n_tm, n_tm), f] = drift
    for s in range(n_tm):
        for f in range(frames):
            if s or f:
                before = sum_scr[s, f - 1] if f else sum_scr[s - 1, frames - 1]
                sum_scr[s, f] = sum_scr[s, f] + before
    for k in range(n_tm):
        own = lax.rem(z - k + n_tm, n_tm)
        for f in range(frames):
            for i in range(n_mp):
                to = pl.ds(pl.multiple_of(lax.rem(m - i + n_mp, n_mp) * part, part), part)
                piece = sum_scr[own, f, i * part : (i + 1) * part, :]
                moved_refs[k][f, to, :] = piece.astype(jnp.bfloat16)
                if k == 0:
                    own_ref[f, to, :] = piece


def project(attn, weights, coef, place, dims):
    n_tm, n_seq, n_mp, frames, part, cols = dims
    half = weights[0][0].shape[0]
    tok = n_mp * part
    rows = n_tm * frames * tok
    deep = n_seq * n_mp * cols
    smem, vmem, anywhere = (
        pl.BlockSpec(memory_space=space) for space in (pltpu.SMEM, pltpu.VMEM, pl.ANY)
    )
    return pl.pallas_call(
        functools.partial(project_kernel, dims),
        in_specs=[smem, vmem] + [anywhere] * (n_tm * n_mp + n_seq * n_mp),
        out_specs=[vmem] * (1 + n_tm),
        scratch_shapes=[
            pltpu.VMEM((n_seq * n_mp, rows, cols), jnp.bfloat16),
            pltpu.VMEM((n_seq * n_mp, half, cols), jnp.bfloat16),
            pltpu.VMEM((n_tm, frames, tok, half), jnp.float32),
            pltpu.SemaphoreType.DMA((n_seq * n_mp, 1 + n_tm * frames * n_mp)),
        ],
        out_shape=[jax.ShapeDtypeStruct((frames, tok, half), jnp.float32)]
        + [jax.ShapeDtypeStruct((frames, tok, half), jnp.bfloat16)] * n_tm,
        cost_estimate=pl.CostEstimate(
            flops=2 * rows * deep * half, bytes_accessed=2 * (rows + half) * deep, transcendentals=0
        ),
        name="project",
    )(place, coef, *[a for k in attn for a in k], *[w for j in weights for w in j])


def finish_kernel(n_tm, n_mp, place_ref, *refs):
    out = refs[-1]
    z, m = place_ref[0], place_ref[1]
    half = refs[0].shape[-1]
    slices = n_tm // n_mp
    for u in range(slices):
        k_here = lax.rem(m * slices + u - z + n_tm, n_tm)
        for h in range(n_mp):
            first = (u * n_mp + h) * half
            for k in range(n_tm):
                for l in range(n_mp):

                    @pl.when((k_here == k) & (lax.rem(m - h + n_mp, n_mp) == l))
                    def _():
                        out[:, :, first : first + half] = refs[k * n_mp + l][...].astype(
                            jnp.float32
                        )


def finish(blocks, place):
    n_tm, n_mp = len(blocks), len(blocks[0])
    frames, tok, half = blocks[0][0].shape
    smem, vmem = (pl.BlockSpec(memory_space=space) for space in (pltpu.SMEM, pltpu.VMEM))
    return pl.pallas_call(
        functools.partial(finish_kernel, n_tm, n_mp),
        in_specs=[smem] + [vmem] * (n_tm * n_mp),
        out_specs=vmem,
        out_shape=jax.ShapeDtypeStruct((frames, tok, n_tm * half), jnp.float32),
        cost_estimate=pl.CostEstimate(
            flops=0, bytes_accessed=8 * frames * tok * n_tm * half, transcendentals=0
        ),
        name="finish",
    )(place, *[b for k in blocks for b in k])


def sweep(states, start_step, w_qkv, qk_gain, w_out, time_proj):
    frames, tok, _ = states.shape
    n_tm, n_seq, n_mp = (lax.axis_size(name) for name in ("tm", "seq", "mp"))
    z, m = lax.axis_index("tm"), lax.axis_index("mp")
    place = jnp.stack([z, m]).astype(jnp.int32)
    part = tok // n_mp
    depth, cols = w_qkv.shape[1:]
    half = depth // n_mp
    window = frames * n_tm

    raw = list(spread(states, place, n_tm, part))
    for k in range(1, n_tm):
        raw[k] = turn(raw[k], "tm", k)
    raw = jnp.stack(raw)
    sides = [raw]
    for j in range(1, n_seq):
        sides.append(turn(raw, "seq", j))
    rows = []
    for side in sides:
        rows.append([side] + [turn(side, "mp", i) for i in range(1, n_mp)])

    shares = list(time_shares(start_step, time_proj, place, n_tm, window))
    for k in range(1, n_tm):
        shares[k] = turn(shares[k], "tm", k)

    share = w_out.reshape(n_mp, half, cols)
    weights = [take(share, m)]
    weights += [turn(take(share, (m + i) % n_mp), "mp", i) for i in range(1, n_mp)]
    weights = [weights]
    for j in range(1, n_seq):
        weights.append([turn(s, "seq", -j) for s in weights[0]])

    steps_idx = start_step[0] + jnp.arange(window)
    step_size = sigma_of(steps_idx + 1) - sigma_of(steps_idx)
    gate = lax.dynamic_slice_in_dim(sum(s[2] for s in shares), m * half, half, 1)
    coef = (step_size[:, None] * gate).reshape(n_tm, frames, half)
    coef = jnp.stack([take(coef, (z - k) % n_tm) for k in range(n_tm)])

    proj = []
    for j in range(n_seq):
        proj.append(qkv(shares, rows[j], w_qkv, place))
    right, left = [None] * n_seq, [None] * n_seq
    for t in range(n_tm - 1):
        for j in range(n_seq):
            send_right, send_left = proj[j][(t + 1) % n_tm], proj[j][n_tm - 1 - t]
            if t:
                right[j], left[j], coef = lax.optimization_barrier((right[j], left[j], coef))
                send_right = send_right + right[j].astype(jnp.float32)
                send_left = send_left + left[j].astype(jnp.float32)
            send_right, send_left = send_right.astype(jnp.float16), send_left.astype(jnp.float16)
            right[j] = lax.ppermute(send_right, "tm", [(i, i + 1) for i in range(t + 1)])
            left[j] = lax.ppermute(
                send_left, "tm", [(n_tm - 1 - i, n_tm - 2 - i) for i in range(t + 1)]
            )
    parts = [
        (p[0] + r.astype(jnp.float32) + l.astype(jnp.float32)).reshape(3, frames, tok, cols)
        for p, r, l in zip(proj, right, left)
    ]
    attn = attend(parts, qk_gain)

    attn = jnp.stack([attn[0]] + [turn(attn[j], "seq", -j) for j in range(1, n_seq)])
    gathered = [attn]
    for k in range(1, n_tm):
        gathered.append(turn(attn, "tm", k))
    gathered = [[g] + [turn(g, "mp", i) for i in range(1, n_mp)] for g in gathered]

    own, *moved = project(
        gathered, weights, coef, place, (n_tm, n_seq, n_mp, frames, part, cols)
    )
    blocks = []
    for k in range(n_tm):
        block = moved[0]
        if k:
            block = turn(moved[k], "tm", -k)
        others = [turn(block, "mp", i) for i in range(1, n_mp)]
        blocks.append([block if k else own] + others)
    return finish(blocks, place)


def solution(mesh):
    return jax.shard_map(
        sweep,
        mesh=mesh,
        in_specs=(
            P(("group", "tm"), "seq", None),
            P("group"),
            P(None, "tm", ("seq", "mp")),
            P(None, ("seq", "mp")),
            P("tm", ("seq", "mp")),
            P("tm", None),
        ),
        out_specs=P(("group", "tm"), "seq", "mp"),
        check_vma=False,
    )
```

```python
import functools

import jax
import jax.numpy as jnp
from jax import lax
from jax.experimental import pallas as pl
from jax.experimental.pallas import tpu as pltpu
from jax.sharding import PartitionSpec as P


HEAD_DIM = 128
FREQ = 256
STEPS = 100
LANES = 128


sample_shift = 5.0
norm_eps = 1e-06


def sigma_of(index):
    unit = 1.0 - index.astype(jnp.float32) / jnp.float32(STEPS)
    return sample_shift * unit / (1.0 + (sample_shift - 1.0) * unit)


def turn(block, axis, distance):
    size = lax.axis_size(axis)
    return lax.ppermute(block, axis, [(i, (i + distance) % size) for i in range(size)])


def take(array, index, dim=0):
    return lax.dynamic_index_in_dim(array, index, dim, keepdims=False)


def head_norm(values, gain):
    meansq = jnp.mean(values * values, axis=-1, keepdims=True)
    return (values * lax.rsqrt(meansq + norm_eps) * gain).astype(jnp.bfloat16)


def head_groups(cols):
    heads = cols // HEAD_DIM
    first = (heads + 1) // 2 * HEAD_DIM
    return ((0, first), (first, cols - first)) if first < cols else ((0, cols),)


def attend_kernel(n_seq, heads, gain_ref, whole_ref, *outs):
    inv_root = 1.0 / jnp.sqrt(jnp.float32(HEAD_DIM))
    rows = whole_ref.shape[3]
    for h in range(heads):
        lanes = pl.ds(h * HEAD_DIM, HEAD_DIM)
        q, k, v = (
            jnp.concatenate([whole_ref[c, j, 0, :, lanes] for j in range(n_seq)], axis=0)
            for c in range(3)
        )
        q = head_norm(q, gain_ref[0:1, lanes])
        k = head_norm(k, gain_ref[1:2, lanes])
        scores = lax.dot_general(
            q, k, (((1,), (1,)), ((), ())), preferred_element_type=jnp.float32
        )
        expo = jnp.exp(scores * inv_root)
        probs = (expo / jnp.sum(expo, axis=-1, keepdims=True)).astype(jnp.bfloat16)
        attn = jnp.dot(
            probs, v.astype(jnp.bfloat16), preferred_element_type=jnp.float32
        ).astype(jnp.bfloat16)
        for j, out in enumerate(outs):
            out[0, :, lanes] = attn[j * rows : (j + 1) * rows]


def attend(whole, gain):
    _, n_seq, frames, rows, cols = whole.shape
    heads = cols // HEAD_DIM
    tokens = rows * n_seq
    out = jax.ShapeDtypeStruct((frames, rows, cols), jnp.bfloat16)
    return pl.pallas_call(
        functools.partial(attend_kernel, n_seq, heads),
        grid=(frames,),
        in_specs=[
            pl.BlockSpec((2, cols), lambda f: (0, 0)),
            pl.BlockSpec((3, n_seq, 1, rows, cols), lambda f: (0, 0, f, 0, 0)),
        ],
        out_specs=[pl.BlockSpec((1, rows, cols), lambda f: (f, 0, 0))] * n_seq,
        out_shape=[out] * n_seq,
        cost_estimate=pl.CostEstimate(
            flops=4 * frames * heads * tokens * tokens * HEAD_DIM,
            bytes_accessed=14 * frames * tokens * cols,
            transcendentals=frames * heads * tokens * tokens,
        ),
        name="attend",
    )(gain, whole)


def spread_kernel(n_tm, states_ref, *outs):
    z, m = lax.axis_index("tm"), lax.axis_index("mp")
    frames, _, width = states_ref.shape
    part, depth = outs[0].shape[1], width // n_tm
    own = pl.ds(pl.multiple_of(m * part, part), part)
    lane = lax.broadcasted_iota(jnp.int32, (part, LANES), 1)
    for f in range(frames):
        field = states_ref[f, own, :].astype(jnp.float32)
        mean = jnp.mean(field, axis=-1, keepdims=True)
        centred = field - mean
        var = jnp.mean(centred * centred, axis=-1, keepdims=True)
        tail = jnp.zeros((part, LANES), jnp.float32)
        for place, rest in enumerate((mean, lax.rsqrt(var + norm_eps))):
            for term in range(3):
                cut = rest.astype(jnp.bfloat16).astype(jnp.float32)
                tail = jnp.where(lane == 3 * place + term, cut, tail)
                rest = rest - cut
        tail = tail.astype(jnp.bfloat16)
        for k, out in enumerate(outs):
            out[f, :, depth:] = tail
            for s in range(n_tm):

                @pl.when(lax.rem(z + k, n_tm) == s)
                def _():
                    out[f, :, :depth] = states_ref[f, own, s * depth : (s + 1) * depth]


def spread(states, n_tm, part):
    frames, _, width = states.shape
    out = jax.ShapeDtypeStruct((frames, part, width // n_tm + LANES), jnp.bfloat16)
    return pl.pallas_call(
        functools.partial(spread_kernel, n_tm),
        in_specs=[pl.BlockSpec(memory_space=pltpu.VMEM)],
        out_specs=[pl.BlockSpec(memory_space=pltpu.VMEM)] * n_tm,
        out_shape=[out] * n_tm,
        cost_estimate=pl.CostEstimate(
            flops=10 * part * width, bytes_accessed=4 * part * width, transcendentals=0
        ),
        name="spread",
    )(states)


def time_kernel(n_tm, step_ref, proj_ref, *outs):
    z = lax.axis_index("tm")
    freq_rows, wide = proj_ref.shape
    window, depth = outs[0].shape[1:]
    half_freq = FREQ // 2
    index = step_ref[0] + lax.broadcasted_iota(jnp.int32, (window, freq_rows), 0)
    feature = z * freq_rows + lax.broadcasted_iota(jnp.int32, (window, freq_rows), 1)
    late = feature >= half_freq
    rank = jnp.where(late, feature - half_freq, feature).astype(jnp.float32)
    freqs = jnp.exp(-jnp.log(jnp.float32(10000.0)) * rank / jnp.float32(half_freq))
    angles = (1000.0 * sigma_of(index)) * freqs
    emb = jnp.where(late, jnp.sin(angles), jnp.cos(angles)).astype(jnp.bfloat16)
    for k, out in enumerate(outs):
        for s in range(n_tm):

            @pl.when(lax.rem(z + k, n_tm) == s)
            def _():
                for c in range(3):
                    first = c * (wide // 3) + s * depth
                    out[c] = jnp.dot(
                        emb, proj_ref[:, first : first + depth], preferred_element_type=jnp.float32
                    )


def time_shares(start_step, time_proj, n_tm, window):
    freq_rows, wide = time_proj.shape
    out = jax.ShapeDtypeStruct((3, window, wide // (3 * n_tm)), jnp.float32)
    smem, vmem = (pl.BlockSpec(memory_space=space) for space in (pltpu.SMEM, pltpu.VMEM))
    return pl.pallas_call(
        functools.partial(time_kernel, n_tm),
        in_specs=[smem, vmem],
        out_specs=[vmem] * n_tm,
        out_shape=[out] * n_tm,
        cost_estimate=pl.CostEstimate(
            flops=2 * window * freq_rows * wide, bytes_accessed=2 * freq_rows * wide, transcendentals=0
        ),
        name="time_shares",
    )(start_step, time_proj)


def modulate_kernel(n_tm, n_seq, n_mp, step_ref, *refs):
    shares, rows, (hidden_ref, coef_ref, mod_scr) = refs[:n_tm], refs[n_tm:-3], refs[-3:]
    z = lax.axis_index("tm")
    _, frames, part, wide = rows[0].shape
    depth = wide - LANES
    total = shares[0][...]
    for share in shares[1:]:
        total = total + share[...]
    mod_scr[...] = total
    for k in range(n_tm):
        for f in range(frames):
            step = pl.ds(lax.rem(z - k + n_tm, n_tm) * frames + f, 1)
            shift, scale = mod_scr[0, step, :], mod_scr[1, step, :]
            index = jnp.full((1, depth), step_ref[0] + step.start, jnp.int32)
            size = sigma_of(index + 1) - sigma_of(index)
            coef_ref[k, f : f + 1, :] = size * mod_scr[2, step, :]
            for j in range(n_seq):
                for i in range(n_mp):
                    row = rows[j * n_mp + i]
                    tail = row[k, f, :, depth:].astype(jnp.float32)
                    mean = tail[:, 0:1] + tail[:, 1:2] + tail[:, 2:3]
                    rstd = tail[:, 3:4] + tail[:, 4:5] + tail[:, 5:6]
                    normed = (row[k, f, :, :depth].astype(jnp.float32) - mean) * rstd
                    hidden_ref[k, j, f, i * part : (i + 1) * part, :] = (
                        normed * (1.0 + scale) + shift
                    ).astype(jnp.bfloat16)


def modulate(start_step, shares, rows):
    n_tm, n_seq, n_mp = len(shares), len(rows), len(rows[0])
    _, frames, part, wide = rows[0][0].shape
    depth = wide - LANES
    window = shares[0].shape[1]
    smem, vmem = (pl.BlockSpec(memory_space=space) for space in (pltpu.SMEM, pltpu.VMEM))
    shape = (n_tm, n_seq, frames, n_mp * part, depth)
    return pl.pallas_call(
        functools.partial(modulate_kernel, n_tm, n_seq, n_mp),
        in_specs=[smem] + [vmem] * (n_tm + n_seq * n_mp),
        out_specs=[vmem] * 2,
        scratch_shapes=[pltpu.VMEM((3, window, depth), jnp.float32)],
        out_shape=[
            jax.ShapeDtypeStruct(shape, jnp.bfloat16),
            jax.ShapeDtypeStruct((n_tm, frames, depth), jnp.float32),
        ],
        cost_estimate=pl.CostEstimate(
            flops=4 * n_tm * n_seq * frames * n_mp * part * depth,
            bytes_accessed=4 * n_tm * n_seq * frames * n_mp * part * depth,
            transcendentals=0,
        ),
        name="modulate",
    )(start_step, *shares, *[r for side in rows for r in side])


def project_kernel(dims, widths, coef_ref, *refs):
    n_tm, n_seq, n_mp, frames, part, _ = dims
    n_attn = len(widths) * n_tm * n_mp
    attn_refs = refs[:n_attn]
    w_refs = refs[n_attn : n_attn + n_seq * n_mp]
    outs = refs[n_attn + n_seq * n_mp :]
    own_ref, moved_refs, (rows_scr, w_scr, sum_scr, sems) = outs[0], outs[1:-4], outs[-4:]
    z, m = lax.axis_index("tm"), lax.axis_index("mp")
    block = n_mp * part
    per = frames * block
    half = own_ref.shape[-1]
    copies = []
    for j in range(n_seq):
        for l in range(n_mp):
            at = j * n_mp + l
            group = [pltpu.make_async_copy(w_refs[at], w_scr.at[at], sems.at[at, 0])]
            for k in range(n_tm):
                for f in range(frames):
                    for i in range(n_mp):
                        first = k * per + f * block + i * part
                        source = (i - l) % n_mp * part
                        for h, (lane, width) in enumerate(widths):
                            piece = attn_refs[(h * n_tm + k) * n_mp + l]
                            group.append(
                                pltpu.make_async_copy(
                                    piece.at[j, f, pl.ds(source, part)],
                                    rows_scr.at[at, pl.ds(first, part), pl.ds(lane, width)],
                                    sems.at[at, len(group)],
                                )
                            )
            for copy in group:
                copy.start()
            copies.append(group)
    total = None
    for at, group in enumerate(copies):
        for copy in group:
            copy.wait()
        product = lax.dot_general(
            rows_scr[at], w_scr[at], (((1,), (1,)), ((), ())), preferred_element_type=jnp.float32
        )
        total = product if total is None else total + product
    for k in range(n_tm):
        for f in range(frames):
            first = k * per + f * block
            factor = coef_ref[k, f : f + 1, :half]
            for mm in range(1, n_mp):
                other = coef_ref[k, f : f + 1, mm * half : (mm + 1) * half]
                factor = jnp.where(m == mm, other, factor)
            drift = total[first : first + block] * factor
            sum_scr[lax.rem(z - k + n_tm, n_tm), f] = drift
    for s in range(n_tm):
        for f in range(frames):
            if s or f:
                before = sum_scr[s, f - 1] if f else sum_scr[s - 1, frames - 1]
                sum_scr[s, f] = sum_scr[s, f] + before
    for k in range(n_tm):
        own = lax.rem(z - k + n_tm, n_tm)
        for f in range(frames):
            for i in range(n_mp):
                to = pl.ds(pl.multiple_of(lax.rem(m - i + n_mp, n_mp) * part, part), part)
                piece = sum_scr[own, f, i * part : (i + 1) * part, :]
                moved_refs[k][f, to, :] = piece.astype(jnp.bfloat16)
                if k == 0:
                    own_ref[f, to, :] = piece


def project(attn, weights, coef, dims, widths):
    n_tm, n_seq, n_mp, frames, part, cols = dims
    half = weights[0][0].shape[0]
    tok = n_mp * part
    rows = n_tm * frames * tok
    deep = n_seq * n_mp * cols
    vmem, anywhere = (pl.BlockSpec(memory_space=space) for space in (pltpu.VMEM, pl.ANY))
    return pl.pallas_call(
        functools.partial(project_kernel, dims, widths),
        in_specs=[vmem] + [anywhere] * (len(widths) * n_tm * n_mp + n_seq * n_mp),
        out_specs=[vmem] * (1 + n_tm),
        scratch_shapes=[
            pltpu.VMEM((n_seq * n_mp, rows, cols), jnp.bfloat16),
            pltpu.VMEM((n_seq * n_mp, half, cols), jnp.bfloat16),
            pltpu.VMEM((n_tm, frames, tok, half), jnp.float32),
            pltpu.SemaphoreType.DMA((n_seq * n_mp, 1 + len(widths) * n_tm * frames * n_mp)),
        ],
        out_shape=[jax.ShapeDtypeStruct((frames, tok, half), jnp.float32)]
        + [jax.ShapeDtypeStruct((frames, tok, half), jnp.bfloat16)] * n_tm,
        cost_estimate=pl.CostEstimate(
            flops=2 * rows * deep * half, bytes_accessed=2 * (rows + half) * deep, transcendentals=0
        ),
        name="project",
    )(coef, *[a for h in attn for k in h for a in k], *[w for j in weights for w in j])


def finish_kernel(n_tm, n_mp, *refs):
    out = refs[-1]
    z, m = lax.axis_index("tm"), lax.axis_index("mp")
    half = refs[0].shape[-1]
    slices = n_tm // n_mp
    for u in range(slices):
        k_here = lax.rem(m * slices + u - z + n_tm, n_tm)
        for h in range(n_mp):
            first = (u * n_mp + h) * half
            for k in range(n_tm):
                for l in range(n_mp):

                    @pl.when((k_here == k) & (lax.rem(m - h + n_mp, n_mp) == l))
                    def _():
                        out[:, :, first : first + half] = refs[k * n_mp + l][...].astype(
                            jnp.float32
                        )


def finish(blocks):
    n_tm, n_mp = len(blocks), len(blocks[0])
    frames, tok, half = blocks[0][0].shape
    vmem = pl.BlockSpec(memory_space=pltpu.VMEM)
    return pl.pallas_call(
        functools.partial(finish_kernel, n_tm, n_mp),
        in_specs=[vmem] * (n_tm * n_mp),
        out_specs=vmem,
        out_shape=jax.ShapeDtypeStruct((frames, tok, n_tm * half), jnp.float32),
        cost_estimate=pl.CostEstimate(
            flops=0, bytes_accessed=8 * frames * tok * n_tm * half, transcendentals=0
        ),
        name="finish",
    )(*[b for k in blocks for b in k])


def sweep(states, start_step, w_qkv, qk_gain, w_out, time_proj):
    frames, tok, _ = states.shape
    n_tm, n_seq, n_mp = (lax.axis_size(name) for name in ("tm", "seq", "mp"))
    m = lax.axis_index("mp")
    part = tok // n_mp
    depth, cols = w_qkv.shape[1:]
    half = depth // n_mp
    window = frames * n_tm

    raw = list(spread(states, n_tm, part))
    for k in range(1, n_tm):
        raw[k] = turn(raw[k], "tm", k)
    raw = jnp.stack(raw)
    sides = [raw]
    for j in range(1, n_seq):
        sides.append(turn(raw, "seq", j))
    rows = []
    for side in sides:
        rows.append([side] + [turn(side, "mp", i) for i in range(1, n_mp)])

    shares = list(time_shares(start_step, time_proj, n_tm, window))
    for k in range(1, n_tm):
        shares[k] = turn(shares[k], "tm", k)

    share = w_out.reshape(n_mp, half, cols)
    weights = [take(share, m)]
    weights += [turn(take(share, (m + i) % n_mp), "mp", i) for i in range(1, n_mp)]
    weights = [weights]
    for j in range(1, n_seq):
        weights.append([turn(s, "seq", -j) for s in weights[0]])

    hidden, coef = modulate(start_step, shares, rows)
    hidden = hidden.reshape(n_tm, n_seq * frames * tok, depth)
    groups = head_groups(cols)
    proj = []
    for lane, size in groups:
        proj.append(
            jnp.einsum(
                "krd,cdh->kcrh",
                hidden,
                w_qkv[:, :, lane : lane + size],
                preferred_element_type=jnp.float32,
            )
        )
    right, left = [None] * len(groups), [None] * len(groups)
    for t in range(n_tm - 1):
        for h in range(len(groups)):
            send_right, send_left = proj[h][(t + 1) % n_tm], proj[h][n_tm - 1 - t]
            if t:
                right[h], left[h] = lax.optimization_barrier((right[h], left[h]))
                send_right = send_right + right[h].astype(jnp.float32)
                send_left = send_left + left[h].astype(jnp.float32)
            send_right, send_left = (send_right.astype(jnp.float16), send_left.astype(jnp.float16))
            right[h] = lax.ppermute(send_right, "tm", [(i, i + 1) for i in range(t + 1)])
            left[h] = lax.ppermute(
                send_left, "tm", [(n_tm - 1 - i, n_tm - 2 - i) for i in range(t + 1)]
            )
    gathered = []
    for h, (lane, size) in enumerate(groups):
        total = proj[h][0] + right[h].astype(jnp.float32) + left[h].astype(jnp.float32)
        total = total.reshape(3, n_seq, frames, tok, size)
        attn = attend(total, qk_gain[:, lane : lane + size])
        attn = jnp.stack([attn[0]] + [turn(attn[j], "seq", -j) for j in range(1, n_seq)])
        pieces = [attn]
        for k in range(1, n_tm):
            pieces.append(turn(attn, "tm", k))
        gathered.append([[g] + [turn(g, "mp", i) for i in range(1, n_mp)] for g in pieces])

    own, *moved = project(
        gathered, weights, coef, (n_tm, n_seq, n_mp, frames, part, cols), groups
    )
    blocks = []
    for k in range(n_tm):
        block = moved[0]
        if k:
            block = turn(moved[k], "tm", -k)
        others = [turn(block, "mp", i) for i in range(1, n_mp)]
        blocks.append([block if k else own] + others)
    return finish(blocks)


def solution(mesh):
    return jax.shard_map(
        sweep,
        mesh=mesh,
        in_specs=(
            P(("group", "tm"), "seq", None),
            P("group"),
            P(None, "tm", ("seq", "mp")),
            P(None, ("seq", "mp")),
            P("tm", ("seq", "mp")),
            P("tm", None),
        ),
        out_specs=P(("group", "tm"), "seq", "mp"),
        check_vma=False,
    )
```

```python
import functools

import jax
import jax.numpy as jnp
from jax import lax
from jax.experimental import pallas as pl
from jax.experimental.pallas import tpu as pltpu
from jax.sharding import PartitionSpec as P


HEAD_DIM = 128
FREQ = 256
STEPS = 100
LANES = 128


sample_shift = 5.0
norm_eps = 1e-06


def sigma_of(index):
    unit = 1.0 - index.astype(jnp.float32) / jnp.float32(STEPS)
    return sample_shift * unit / (1.0 + (sample_shift - 1.0) * unit)


def turn(block, axis, distance):
    size = lax.axis_size(axis)
    return lax.ppermute(block, axis, [(i, (i + distance) % size) for i in range(size)])


def take(array, index, dim=0):
    return lax.dynamic_index_in_dim(array, index, dim, keepdims=False)


def head_norm(values, gain):
    meansq = jnp.mean(values * values, axis=-1, keepdims=True)
    return (values * lax.rsqrt(meansq + norm_eps) * gain).astype(jnp.bfloat16)


def head_groups(cols):
    heads = cols // HEAD_DIM
    first = (heads + 1) // 2 * HEAD_DIM
    return ((0, first), (first, cols - first)) if first < cols else ((0, cols),)


def attend_kernel(n_seq, heads, gain_ref, whole_ref, *outs):
    inv_root = 1.0 / jnp.sqrt(jnp.float32(HEAD_DIM))
    rows = whole_ref.shape[3]
    for h in range(heads):
        lanes = pl.ds(h * HEAD_DIM, HEAD_DIM)
        q, k, v = (
            jnp.concatenate([whole_ref[c, j, 0, :, lanes] for j in range(n_seq)], axis=0)
            for c in range(3)
        )
        q = head_norm(q, gain_ref[0:1, lanes])
        k = head_norm(k, gain_ref[1:2, lanes])
        scores = lax.dot_general(
            q, k, (((1,), (1,)), ((), ())), preferred_element_type=jnp.float32
        )
        expo = jnp.exp(scores * inv_root)
        probs = (expo / jnp.sum(expo, axis=-1, keepdims=True)).astype(jnp.bfloat16)
        attn = jnp.dot(
            probs, v.astype(jnp.bfloat16), preferred_element_type=jnp.float32
        ).astype(jnp.bfloat16)
        for j, out in enumerate(outs):
            out[0, :, lanes] = attn[j * rows : (j + 1) * rows]


def attend(whole, gain):
    _, n_seq, frames, rows, cols = whole.shape
    heads = cols // HEAD_DIM
    tokens = rows * n_seq
    out = jax.ShapeDtypeStruct((frames, rows, cols), jnp.bfloat16)
    return pl.pallas_call(
        functools.partial(attend_kernel, n_seq, heads),
        grid=(frames,),
        in_specs=[
            pl.BlockSpec((2, cols), lambda f: (0, 0)),
            pl.BlockSpec((3, n_seq, 1, rows, cols), lambda f: (0, 0, f, 0, 0)),
        ],
        out_specs=[pl.BlockSpec((1, rows, cols), lambda f: (f, 0, 0))] * n_seq,
        out_shape=[out] * n_seq,
        cost_estimate=pl.CostEstimate(
            flops=4 * frames * heads * tokens * tokens * HEAD_DIM,
            bytes_accessed=14 * frames * tokens * cols,
            transcendentals=frames * heads * tokens * tokens,
        ),
        compiler_params=pltpu.CompilerParams(vmem_limit_bytes=12 << 20),
        name="attend",
    )(gain, whole)


def spread_kernel(n_tm, states_ref, *outs):
    z, m = lax.axis_index("tm"), lax.axis_index("mp")
    frames, _, width = states_ref.shape
    part, depth = outs[0].shape[1], width // n_tm
    own = pl.ds(pl.multiple_of(m * part, part), part)
    lane = lax.broadcasted_iota(jnp.int32, (part, LANES), 1)
    for f in range(frames):
        field = states_ref[f, own, :].astype(jnp.float32)
        mean = jnp.mean(field, axis=-1, keepdims=True)
        centred = field - mean
        var = jnp.mean(centred * centred, axis=-1, keepdims=True)
        tail = jnp.zeros((part, LANES), jnp.float32)
        for place, rest in enumerate((mean, lax.rsqrt(var + norm_eps))):
            for term in range(3):
                cut = rest.astype(jnp.bfloat16).astype(jnp.float32)
                tail = jnp.where(lane == 3 * place + term, cut, tail)
                rest = rest - cut
        tail = tail.astype(jnp.bfloat16)
        for k, out in enumerate(outs):
            out[f, :, depth:] = tail
            for s in range(n_tm):

                @pl.when(lax.rem(z + k, n_tm) == s)
                def _():
                    out[f, :, :depth] = states_ref[f, own, s * depth : (s + 1) * depth]


def spread(states, n_tm, part):
    frames, _, width = states.shape
    out = jax.ShapeDtypeStruct((frames, part, width // n_tm + LANES), jnp.bfloat16)
    return pl.pallas_call(
        functools.partial(spread_kernel, n_tm),
        in_specs=[pl.BlockSpec(memory_space=pltpu.VMEM)],
        out_specs=[pl.BlockSpec(memory_space=pltpu.VMEM)] * n_tm,
        out_shape=[out] * n_tm,
        cost_estimate=pl.CostEstimate(
            flops=10 * part * width, bytes_accessed=4 * part * width, transcendentals=0
        ),
        compiler_params=pltpu.CompilerParams(vmem_limit_bytes=8 << 20),
        name="spread",
    )(states)


def time_kernel(n_tm, step_ref, proj_ref, *outs):
    z = lax.axis_index("tm")
    freq_rows, wide = proj_ref.shape
    window, depth = outs[0].shape[1:]
    half_freq = FREQ // 2
    index = step_ref[0] + lax.broadcasted_iota(jnp.int32, (window, freq_rows), 0)
    feature = z * freq_rows + lax.broadcasted_iota(jnp.int32, (window, freq_rows), 1)
    late = feature >= half_freq
    rank = jnp.where(late, feature - half_freq, feature).astype(jnp.float32)
    freqs = jnp.exp(-jnp.log(jnp.float32(10000.0)) * rank / jnp.float32(half_freq))
    angles = (1000.0 * sigma_of(index)) * freqs
    emb = jnp.where(late, jnp.sin(angles), jnp.cos(angles)).astype(jnp.bfloat16)
    for k, out in enumerate(outs):
        for s in range(n_tm):

            @pl.when(lax.rem(z + k, n_tm) == s)
            def _():
                for c in range(3):
                    first = c * (wide // 3) + s * depth
                    out[c] = jnp.dot(
                        emb, proj_ref[:, first : first + depth], preferred_element_type=jnp.float32
                    )


def time_shares(start_step, time_proj, n_tm, window):
    freq_rows, wide = time_proj.shape
    out = jax.ShapeDtypeStruct((3, window, wide // (3 * n_tm)), jnp.float32)
    smem, vmem = (pl.BlockSpec(memory_space=space) for space in (pltpu.SMEM, pltpu.VMEM))
    return pl.pallas_call(
        functools.partial(time_kernel, n_tm),
        in_specs=[smem, vmem],
        out_specs=[vmem] * n_tm,
        out_shape=[out] * n_tm,
        cost_estimate=pl.CostEstimate(
            flops=2 * window * freq_rows * wide, bytes_accessed=2 * freq_rows * wide, transcendentals=0
        ),
        compiler_params=pltpu.CompilerParams(vmem_limit_bytes=12 << 20),
        name="time_shares",
    )(start_step, time_proj)


def modulate_kernel(n_tm, n_seq, n_mp, step_ref, *refs):
    shares, rows, (hidden_ref, coef_ref, mod_scr) = refs[:n_tm], refs[n_tm:-3], refs[-3:]
    z, k = lax.axis_index("tm"), pl.program_id(0)
    _, frames, part, wide = rows[0].shape
    depth = wide - LANES

    @pl.when(k == 0)
    def _():
        total = shares[0][...]
        for share in shares[1:]:
            total = total + share[...]
        mod_scr[...] = total

    for f in range(frames):
        step = lax.rem(z - k + n_tm, n_tm) * frames + f
        shift, scale, gate = (mod_scr[c, pl.ds(step, 1), :] for c in range(3))
        index = jnp.full((1, depth), step_ref[0] + step, jnp.int32)
        coef_ref[0, f : f + 1, :] = (sigma_of(index + 1) - sigma_of(index)) * gate
        for j in range(n_seq):
            for i in range(n_mp):
                row = rows[j * n_mp + i]
                tail = row[0, f, :, depth:].astype(jnp.float32)
                mean = tail[:, 0:1] + tail[:, 1:2] + tail[:, 2:3]
                rstd = tail[:, 3:4] + tail[:, 4:5] + tail[:, 5:6]
                normed = (row[0, f, :, :depth].astype(jnp.float32) - mean) * rstd
                hidden_ref[0, j, f, i * part : (i + 1) * part, :] = (
                    normed * (1.0 + scale) + shift
                ).astype(jnp.bfloat16)


def modulate(start_step, shares, rows):
    n_tm, n_seq, n_mp = len(shares), len(rows), len(rows[0])
    _, frames, part, wide = rows[0][0].shape
    depth = wide - LANES
    window = shares[0].shape[1]
    shape = (n_tm, n_seq, frames, n_mp * part, depth)
    return pl.pallas_call(
        functools.partial(modulate_kernel, n_tm, n_seq, n_mp),
        grid=(n_tm,),
        in_specs=[pl.BlockSpec(memory_space=pltpu.SMEM)]
        + [pl.BlockSpec((3, window, depth), lambda k: (0, 0, 0))] * n_tm
        + [pl.BlockSpec((1, frames, part, wide), lambda k: (k, 0, 0, 0))] * (n_seq * n_mp),
        out_specs=[
            pl.BlockSpec((1,) + shape[1:], lambda k: (k, 0, 0, 0, 0)),
            pl.BlockSpec((1, frames, depth), lambda k: (k, 0, 0)),
        ],
        scratch_shapes=[pltpu.VMEM((3, window, depth), jnp.float32)],
        out_shape=[
            jax.ShapeDtypeStruct(shape, jnp.bfloat16),
            jax.ShapeDtypeStruct((n_tm, frames, depth), jnp.float32),
        ],
        cost_estimate=pl.CostEstimate(
            flops=4 * n_tm * n_seq * frames * n_mp * part * depth,
            bytes_accessed=4 * n_tm * n_seq * frames * n_mp * part * depth,
            transcendentals=0,
        ),
        compiler_params=pltpu.CompilerParams(vmem_limit_bytes=24 << 20),
        name="modulate",
    )(start_step, *shares, *[r for side in rows for r in side])


def project_kernel(dims, widths, coef_ref, *refs):
    n_tm, n_seq, n_mp, frames, part, _ = dims
    n_attn = len(widths) * n_tm * n_mp
    attn_refs = refs[:n_attn]
    w_refs = refs[n_attn : n_attn + n_seq * n_mp]
    outs = refs[n_attn + n_seq * n_mp :]
    own_ref, moved_refs, (rows_scr, sum_scr) = outs[0], outs[1:-2], outs[-2:]
    z, m = lax.axis_index("tm"), lax.axis_index("mp")
    block = n_mp * part
    per = frames * block
    half = own_ref.shape[-1]
    total = None
    for j in range(n_seq):
        for l in range(n_mp):
            at = j * n_mp + l
            for k in range(n_tm):
                for f in range(frames):
                    for i in range(n_mp):
                        first = k * per + f * block + i * part
                        source = (i - l) % n_mp * part
                        for h, (lane, width) in enumerate(widths):
                            piece = attn_refs[(h * n_tm + k) * n_mp + l]
                            rows_scr[at, first : first + part, lane : lane + width] = piece[
                                j, f, source : source + part, :
                            ]
            product = lax.dot_general(
                rows_scr[at],
                w_refs[at][...],
                (((1,), (1,)), ((), ())),
                preferred_element_type=jnp.float32,
            )
            total = product if total is None else total + product
    for k in range(n_tm):
        for f in range(frames):
            first = k * per + f * block
            factor = coef_ref[k, f : f + 1, :half]
            for mm in range(1, n_mp):
                other = coef_ref[k, f : f + 1, mm * half : (mm + 1) * half]
                factor = jnp.where(m == mm, other, factor)
            drift = total[first : first + block] * factor
            sum_scr[lax.rem(z - k + n_tm, n_tm), f] = drift
    for s in range(n_tm):
        for f in range(frames):
            if s or f:
                before = sum_scr[s, f - 1] if f else sum_scr[s - 1, frames - 1]
                sum_scr[s, f] = sum_scr[s, f] + before
    for k in range(n_tm):
        own = lax.rem(z - k + n_tm, n_tm)
        for f in range(frames):
            for i in range(n_mp):
                to = pl.ds(pl.multiple_of(lax.rem(m - i + n_mp, n_mp) * part, part), part)
                piece = sum_scr[own, f, i * part : (i + 1) * part, :]
                moved_refs[k][f, to, :] = piece.astype(jnp.bfloat16)
                if k == 0:
                    own_ref[f, to, :] = piece


def project(attn, weights, coef, dims, widths):
    n_tm, n_seq, n_mp, frames, part, cols = dims
    half = weights[0][0].shape[0]
    tok = n_mp * part
    rows = n_tm * frames * tok
    deep = n_seq * n_mp * cols
    vmem = pl.BlockSpec(memory_space=pltpu.VMEM)
    return pl.pallas_call(
        functools.partial(project_kernel, dims, widths),
        in_specs=[vmem] * (1 + len(widths) * n_tm * n_mp + n_seq * n_mp),
        out_specs=[vmem] * (1 + n_tm),
        scratch_shapes=[
            pltpu.VMEM((n_seq * n_mp, rows, cols), jnp.bfloat16),
            pltpu.VMEM((n_tm, frames, tok, half), jnp.float32),
        ],
        out_shape=[jax.ShapeDtypeStruct((frames, tok, half), jnp.float32)]
        + [jax.ShapeDtypeStruct((frames, tok, half), jnp.bfloat16)] * n_tm,
        cost_estimate=pl.CostEstimate(
            flops=2 * rows * deep * half, bytes_accessed=2 * (rows + half) * deep, transcendentals=0
        ),
        compiler_params=pltpu.CompilerParams(vmem_limit_bytes=32 << 20),
        name="project",
    )(coef, *[a for h in attn for k in h for a in k], *[w for j in weights for w in j])


def finish_kernel(n_tm, n_mp, *refs):
    out = refs[-1]
    z, m = lax.axis_index("tm"), lax.axis_index("mp")
    half = refs[0].shape[-1]
    slices = n_tm // n_mp
    for u in range(slices):
        k_here = lax.rem(m * slices + u - z + n_tm, n_tm)
        for h in range(n_mp):
            first = (u * n_mp + h) * half
            for k in range(n_tm):
                for l in range(n_mp):

                    @pl.when((k_here == k) & (lax.rem(m - h + n_mp, n_mp) == l))
                    def _():
                        out[:, :, first : first + half] = refs[k * n_mp + l][...].astype(
                            jnp.float32
                        )


def finish(blocks):
    n_tm, n_mp = len(blocks), len(blocks[0])
    frames, tok, half = blocks[0][0].shape
    vmem = pl.BlockSpec(memory_space=pltpu.VMEM)
    return pl.pallas_call(
        functools.partial(finish_kernel, n_tm, n_mp),
        in_specs=[vmem] * (n_tm * n_mp),
        out_specs=vmem,
        out_shape=jax.ShapeDtypeStruct((frames, tok, n_tm * half), jnp.float32),
        cost_estimate=pl.CostEstimate(
            flops=0, bytes_accessed=8 * frames * tok * n_tm * half, transcendentals=0
        ),
        compiler_params=pltpu.CompilerParams(vmem_limit_bytes=8 << 20),
        name="finish",
    )(*[b for k in blocks for b in k])


def sweep(states, start_step, w_qkv, qk_gain, w_out, time_proj):
    frames, tok, _ = states.shape
    n_tm, n_seq, n_mp = (lax.axis_size(name) for name in ("tm", "seq", "mp"))
    z, m = lax.axis_index("tm"), lax.axis_index("mp")
    part = tok // n_mp
    depth, cols = w_qkv.shape[1:]
    half = depth // n_mp
    window = frames * n_tm

    raw = list(spread(states, n_tm, part))
    for k in range(1, n_tm):
        raw[k] = turn(raw[k], "tm", k)
    raw = jnp.stack(raw)
    sides = [raw]
    for j in range(1, n_seq):
        sides.append(turn(raw, "seq", j))
    rows = []
    for side in sides:
        rows.append([side] + [turn(side, "mp", i) for i in range(1, n_mp)])

    shares = list(time_shares(start_step, time_proj, n_tm, window))
    for k in range(1, n_tm):
        shares[k] = turn(shares[k], "tm", k)

    share = w_out.reshape(n_mp, half, cols)
    weights = [take(share, m)]
    weights += [turn(take(share, (m + i) % n_mp), "mp", i) for i in range(1, n_mp)]
    weights = [weights]
    for j in range(1, n_seq):
        weights.append([turn(s, "seq", -j) for s in weights[0]])

    hidden, coef = modulate(start_step, shares, rows)
    hidden = hidden.reshape(n_tm, n_seq * frames * tok, depth)
    groups = head_groups(cols)
    proj = []
    for lane, size in groups:
        proj.append(
            jnp.einsum(
                "krd,cdh->kcrh",
                hidden,
                w_qkv[:, :, lane : lane + size],
                preferred_element_type=jnp.float32,
            )
        )
    even = z % 2 == 0
    evens = [(i, i ^ 1) for i in range(n_tm)]
    odds = []
    for i in range(n_tm):
        for c in range(n_mp):
            other = i + 1 if i % 2 else i - 1
            inside = 0 <= other < n_tm
            to = other * n_mp + c if inside else i * n_mp + (c + 1) % n_mp
            odds.append((i * n_mp + c, to))

    def incoming(pair):
        first, second = (0.0 if p is None else p.astype(jnp.float32) for p in pair)
        right = jnp.where(z > 0, jnp.where(even, second, first), 0.0)
        return right, jnp.where(z < n_tm - 1, jnp.where(even, first, second), 0.0)

    flows = [(None, None)] * len(groups)
    for t in range(n_tm - 1):
        for h in range(len(groups)):
            right, left = proj[h][(t + 1) % n_tm], proj[h][n_tm - 1 - t]
            if t:
                more_right, more_left = incoming(flows[h])
                right, left = right + more_right, left + more_left
            first = jnp.where(even, right, left).astype(jnp.float16)
            second = jnp.where(even, left, right).astype(jnp.float16)
            first = lax.ppermute(first, "tm", evens)
            if t:
                second = lax.ppermute(second, ("tm", "mp"), odds)
                first, second = lax.optimization_barrier((first, second))
            flows[h] = (first, second if t else None)
    gathered = []
    for h, (lane, size) in enumerate(groups):
        right, left = incoming(flows[h])
        total = proj[h][0] + right + left
        total = total.reshape(3, n_seq, frames, tok, size)
        attn = attend(total, qk_gain[:, lane : lane + size])
        attn = jnp.stack([attn[0]] + [turn(attn[j], "seq", -j) for j in range(1, n_seq)])
        pieces = [attn]
        for k in range(1, n_tm):
            pieces.append(turn(attn, "tm", k))
        gathered.append([[g] + [turn(g, "mp", i) for i in range(1, n_mp)] for g in pieces])

    own, *moved = project(
        gathered, weights, coef, (n_tm, n_seq, n_mp, frames, part, cols), groups
    )
    blocks = []
    for k in range(n_tm):
        block = moved[0]
        if k:
            block = turn(moved[k], "tm", -k)
        others = [turn(block, "mp", i) for i in range(1, n_mp)]
        blocks.append([block if k else own] + others)
    return finish(blocks)


def solution(mesh):
    return jax.shard_map(
        sweep,
        mesh=mesh,
        in_specs=(
            P(("group", "tm"), "seq", None),
            P("group"),
            P(None, "tm", ("seq", "mp")),
            P(None, ("seq", "mp")),
            P("tm", ("seq", "mp")),
            P("tm", None),
        ),
        out_specs=P(("group", "tm"), "seq", "mp"),
        check_vma=False,
    )
```

```python
import functools

import jax
import jax.numpy as jnp
from jax import lax
from jax.experimental import pallas as pl
from jax.experimental.pallas import tpu as pltpu
from jax.sharding import PartitionSpec as P


HEAD_DIM = 128
FREQ = 256
STEPS = 100
LANES = 128


sample_shift = 5.0
norm_eps = 1e-06


def sigma_of(index):
    unit = 1.0 - index.astype(jnp.float32) / jnp.float32(STEPS)
    return sample_shift * unit / (1.0 + (sample_shift - 1.0) * unit)


def turn(block, axis, distance):
    size = lax.axis_size(axis)
    return lax.ppermute(block, axis, [(i, (i + distance) % size) for i in range(size)])


def head_norm(values, gain):
    meansq = jnp.mean(values * values, axis=-1, keepdims=True)
    return (values * lax.rsqrt(meansq + norm_eps) * gain).astype(jnp.bfloat16)


def head_groups(cols):
    heads = cols // HEAD_DIM
    first = (heads + 1) // 2 * HEAD_DIM
    return ((0, first), (first, cols - first)) if first < cols else ((0, cols),)


def attend_kernel(n_seq, heads, gain_ref, whole_ref, *outs):
    inv_root = 1.0 / jnp.sqrt(jnp.float32(HEAD_DIM))
    rows = whole_ref.shape[3]
    for h in range(heads):
        lanes = pl.ds(h * HEAD_DIM, HEAD_DIM)
        q, k, v = (
            jnp.concatenate([whole_ref[c, j, 0, :, lanes] for j in range(n_seq)], axis=0)
            for c in range(3)
        )
        q = head_norm(q, gain_ref[0:1, lanes])
        k = head_norm(k, gain_ref[1:2, lanes])
        scores = lax.dot_general(
            q, k, (((1,), (1,)), ((), ())), preferred_element_type=jnp.float32
        )
        expo = jnp.exp(scores * inv_root)
        probs = (expo / jnp.sum(expo, axis=-1, keepdims=True)).astype(jnp.bfloat16)
        attn = jnp.dot(
            probs, v.astype(jnp.bfloat16), preferred_element_type=jnp.float32
        ).astype(jnp.bfloat16)
        for j, out in enumerate(outs):
            out[0, :, lanes] = attn[j * rows : (j + 1) * rows]


def attend(whole, gain):
    _, n_seq, frames, rows, cols = whole.shape
    heads = cols // HEAD_DIM
    tokens = rows * n_seq
    out = jax.ShapeDtypeStruct((frames, rows, cols), jnp.bfloat16)
    return pl.pallas_call(
        functools.partial(attend_kernel, n_seq, heads),
        grid=(frames,),
        in_specs=[
            pl.BlockSpec((2, cols), lambda f: (0, 0)),
            pl.BlockSpec((3, n_seq, 1, rows, cols), lambda f: (0, 0, f, 0, 0)),
        ],
        out_specs=[pl.BlockSpec((1, rows, cols), lambda f: (f, 0, 0))] * n_seq,
        out_shape=[out] * n_seq,
        cost_estimate=pl.CostEstimate(
            flops=4 * frames * heads * tokens * tokens * HEAD_DIM,
            bytes_accessed=14 * frames * tokens * cols,
            transcendentals=frames * heads * tokens * tokens,
        ),
        compiler_params=pltpu.CompilerParams(vmem_limit_bytes=6 << 20),
        name="attend",
    )(gain, whole)


def spread_kernel(n_tm, states_ref, *outs):
    z, m = lax.axis_index("tm"), lax.axis_index("mp")
    frames, _, width = states_ref.shape
    part, depth = outs[0].shape[1], width // n_tm
    own = pl.ds(pl.multiple_of(m * part, part), part)
    lane = lax.broadcasted_iota(jnp.int32, (part, LANES), 1)
    for f in range(frames):
        field = states_ref[f, own, :].astype(jnp.float32)
        mean = jnp.mean(field, axis=-1, keepdims=True)
        centred = field - mean
        var = jnp.mean(centred * centred, axis=-1, keepdims=True)
        tail = jnp.zeros((part, LANES), jnp.float32)
        for place, rest in enumerate((mean, lax.rsqrt(var + norm_eps))):
            for term in range(3):
                cut = rest.astype(jnp.bfloat16).astype(jnp.float32)
                tail = jnp.where(lane == 3 * place + term, cut, tail)
                rest = rest - cut
        tail = tail.astype(jnp.bfloat16)
        for k, out in enumerate(outs):
            out[f, :, depth:] = tail
            for s in range(n_tm):

                @pl.when(lax.rem(z + k, n_tm) == s)
                def _():
                    out[f, :, :depth] = states_ref[f, own, s * depth : (s + 1) * depth]


def spread(states, n_tm, part):
    frames, _, width = states.shape
    out = jax.ShapeDtypeStruct((frames, part, width // n_tm + LANES), jnp.bfloat16)
    return pl.pallas_call(
        functools.partial(spread_kernel, n_tm),
        in_specs=[pl.BlockSpec(memory_space=pltpu.VMEM)],
        out_specs=[pl.BlockSpec(memory_space=pltpu.VMEM)] * n_tm,
        out_shape=[out] * n_tm,
        cost_estimate=pl.CostEstimate(
            flops=10 * part * width, bytes_accessed=4 * part * width, transcendentals=0
        ),
        compiler_params=pltpu.CompilerParams(vmem_limit_bytes=4 << 20),
        name="spread",
    )(states)


def time_kernel(n_tm, step_ref, proj_ref, *outs):
    z = lax.axis_index("tm")
    freq_rows, wide = proj_ref.shape
    window, depth = outs[0].shape[1:]
    half_freq = FREQ // 2
    index = step_ref[0] + lax.broadcasted_iota(jnp.int32, (window, freq_rows), 0)
    feature = z * freq_rows + lax.broadcasted_iota(jnp.int32, (window, freq_rows), 1)
    late = feature >= half_freq
    rank = jnp.where(late, feature - half_freq, feature).astype(jnp.float32)
    freqs = jnp.exp(-jnp.log(jnp.float32(10000.0)) * rank / jnp.float32(half_freq))
    angles = (1000.0 * sigma_of(index)) * freqs
    emb = jnp.where(late, jnp.sin(angles), jnp.cos(angles)).astype(jnp.bfloat16)
    for k, out in enumerate(outs):
        for s in range(n_tm):

            @pl.when(lax.rem(z + k, n_tm) == s)
            def _():
                for c in range(3):
                    first = c * (wide // 3) + s * depth
                    out[c] = jnp.dot(
                        emb, proj_ref[:, first : first + depth], preferred_element_type=jnp.float32
                    )


def time_shares(start_step, time_proj, n_tm, window):
    freq_rows, wide = time_proj.shape
    out = jax.ShapeDtypeStruct((3, window, wide // (3 * n_tm)), jnp.float32)
    smem, vmem = (pl.BlockSpec(memory_space=space) for space in (pltpu.SMEM, pltpu.VMEM))
    return pl.pallas_call(
        functools.partial(time_kernel, n_tm),
        in_specs=[smem, vmem],
        out_specs=[vmem] * n_tm,
        out_shape=[out] * n_tm,
        cost_estimate=pl.CostEstimate(
            flops=2 * window * freq_rows * wide, bytes_accessed=2 * freq_rows * wide, transcendentals=0
        ),
        compiler_params=pltpu.CompilerParams(vmem_limit_bytes=6 << 20),
        name="time_shares",
    )(start_step, time_proj)


def load_kernel(n_mp, w_ref, *refs):
    outs, sems = refs[:-1], refs[-1]
    copies = []
    for i, out in enumerate(outs):
        rows = out.shape[0]
        share = lax.rem(lax.axis_index("mp") + i, n_mp)
        source = w_ref.at[pl.ds(pl.multiple_of(share * rows, rows), rows)]
        copies.append(pltpu.make_async_copy(source, out, sems.at[i]))
    for copy in copies:
        copy.start()
    for copy in copies:
        copy.wait()


def load_out(weights, n_mp):
    share = jax.ShapeDtypeStruct((weights.shape[0] // n_mp, weights.shape[1]), weights.dtype)
    return pl.pallas_call(
        functools.partial(load_kernel, n_mp),
        in_specs=[pl.BlockSpec(memory_space=pl.ANY)],
        out_specs=[pl.BlockSpec(memory_space=pltpu.VMEM)] * n_mp,
        out_shape=[share] * n_mp,
        scratch_shapes=[pltpu.SemaphoreType.DMA((n_mp,))],
        cost_estimate=pl.CostEstimate(flops=0, bytes_accessed=2 * weights.size, transcendentals=0),
        compiler_params=pltpu.CompilerParams(vmem_limit_bytes=8 << 20),
        name="load_out",
    )(weights)


def modulate_kernel(n_tm, n_seq, n_mp, cuts, step_ref, w_ref, *refs):
    shares, rows = refs[:n_tm], refs[n_tm : n_tm + n_seq * n_mp]
    hidden_ref, coef_ref, *w_outs, mod_scr, sems = refs[n_tm + n_seq * n_mp :]
    copies = [
        pltpu.make_async_copy(w_ref.at[:, :, pl.ds(lane, size)], out, sems.at[h])
        for h, ((lane, size), out) in enumerate(zip(cuts, w_outs))
    ]
    z, k = lax.axis_index("tm"), pl.program_id(0)
    _, frames, part, wide = rows[0].shape
    depth = wide - LANES

    @pl.when(k == 0)
    def _():
        for copy in copies:
            copy.start()
        total = shares[0][...]
        for share in shares[1:]:
            total = total + share[...]
        mod_scr[...] = total

    for f in range(frames):
        step = lax.rem(z - k + n_tm, n_tm) * frames + f
        shift, scale, gate = (mod_scr[c, pl.ds(step, 1), :] for c in range(3))
        index = jnp.full((1, depth), step_ref[0] + step, jnp.int32)
        coef_ref[0, f : f + 1, :] = (sigma_of(index + 1) - sigma_of(index)) * gate
        for j in range(n_seq):
            for i in range(n_mp):
                row = rows[j * n_mp + i]
                tail = row[0, f, :, depth:].astype(jnp.float32)
                mean = tail[:, 0:1] + tail[:, 1:2] + tail[:, 2:3]
                rstd = tail[:, 3:4] + tail[:, 4:5] + tail[:, 5:6]
                normed = (row[0, f, :, :depth].astype(jnp.float32) - mean) * rstd
                hidden_ref[0, j, f, i * part : (i + 1) * part, :] = (
                    normed * (1.0 + scale) + shift
                ).astype(jnp.bfloat16)

    @pl.when(k == n_tm - 1)
    def _():
        for copy in copies:
            copy.wait()


def modulate(start_step, w_qkv, cuts, shares, rows):
    n_tm, n_seq, n_mp = len(shares), len(rows), len(rows[0])
    _, frames, part, wide = rows[0][0].shape
    depth = wide - LANES
    window = shares[0].shape[1]
    shape = (n_tm, n_seq, frames, n_mp * part, depth)
    return pl.pallas_call(
        functools.partial(modulate_kernel, n_tm, n_seq, n_mp, cuts),
        grid=(n_tm,),
        in_specs=[pl.BlockSpec(memory_space=pltpu.SMEM), pl.BlockSpec(memory_space=pl.ANY)]
        + [pl.BlockSpec((3, window, depth), lambda k: (0, 0, 0))] * n_tm
        + [pl.BlockSpec((1, frames, part, wide), lambda k: (k, 0, 0, 0))] * (n_seq * n_mp),
        out_specs=[
            pl.BlockSpec((1,) + shape[1:], lambda k: (k, 0, 0, 0, 0)),
            pl.BlockSpec((1, frames, depth), lambda k: (k, 0, 0)),
        ]
        + [pl.BlockSpec(memory_space=pl.ANY)] * len(cuts),
        scratch_shapes=[
            pltpu.VMEM((3, window, depth), jnp.float32),
            pltpu.SemaphoreType.DMA((len(cuts),)),
        ],
        out_shape=[
            jax.ShapeDtypeStruct(shape, jnp.bfloat16),
            jax.ShapeDtypeStruct((n_tm, frames, depth), jnp.float32),
        ]
        + [jax.ShapeDtypeStruct(w_qkv.shape[:2] + (size,), w_qkv.dtype) for _, size in cuts],
        cost_estimate=pl.CostEstimate(
            flops=4 * n_tm * n_seq * frames * n_mp * part * depth,
            bytes_accessed=4 * n_tm * n_seq * frames * n_mp * part * depth,
            transcendentals=0,
        ),
        compiler_params=pltpu.CompilerParams(vmem_limit_bytes=8 << 20),
        name="modulate",
    )(start_step, w_qkv, *shares, *[r for side in rows for r in side])


def project_kernel(dims, widths, coef_ref, *refs):
    n_tm, n_seq, n_mp, frames, part, _ = dims
    n_attn = len(widths) * n_tm * n_mp
    attn_refs = refs[:n_attn]
    w_refs = refs[n_attn : n_attn + n_seq * n_mp]
    outs = refs[n_attn + n_seq * n_mp :]
    own_ref, moved_refs, (rows_scr, sum_scr) = outs[0], outs[1:-2], outs[-2:]
    z, m = lax.axis_index("tm"), lax.axis_index("mp")
    block = n_mp * part
    per = frames * block
    half = own_ref.shape[-1]
    total = None
    for j in range(n_seq):
        for l in range(n_mp):
            at = j * n_mp + l
            for k in range(n_tm):
                for f in range(frames):
                    for i in range(n_mp):
                        first = k * per + f * block + i * part
                        source = (i - l) % n_mp * part
                        for h, (lane, width) in enumerate(widths):
                            piece = attn_refs[(h * n_tm + k) * n_mp + l]
                            rows_scr[at, first : first + part, lane : lane + width] = piece[
                                j, f, source : source + part, :
                            ]
            product = lax.dot_general(
                rows_scr[at],
                w_refs[at][...],
                (((1,), (1,)), ((), ())),
                preferred_element_type=jnp.float32,
            )
            total = product if total is None else total + product
    for k in range(n_tm):
        for f in range(frames):
            first = k * per + f * block
            factor = coef_ref[k, f : f + 1, :half]
            for mm in range(1, n_mp):
                other = coef_ref[k, f : f + 1, mm * half : (mm + 1) * half]
                factor = jnp.where(m == mm, other, factor)
            drift = total[first : first + block] * factor
            sum_scr[lax.rem(z - k + n_tm, n_tm), f] = drift
    for s in range(n_tm):
        for f in range(frames):
            if s or f:
                before = sum_scr[s, f - 1] if f else sum_scr[s - 1, frames - 1]
                sum_scr[s, f] = sum_scr[s, f] + before
    for k in range(n_tm):
        own = lax.rem(z - k + n_tm, n_tm)
        for f in range(frames):
            for i in range(n_mp):
                to = pl.ds(pl.multiple_of(lax.rem(m - i + n_mp, n_mp) * part, part), part)
                piece = sum_scr[own, f, i * part : (i + 1) * part, :]
                moved_refs[k][f, to, :] = piece.astype(jnp.bfloat16)
                if k == 0:
                    own_ref[f, to, :] = piece


def project(attn, weights, coef, dims, widths):
    n_tm, n_seq, n_mp, frames, part, cols = dims
    half = weights[0][0].shape[0]
    tok = n_mp * part
    rows = n_tm * frames * tok
    deep = n_seq * n_mp * cols
    vmem = pl.BlockSpec(memory_space=pltpu.VMEM)
    return pl.pallas_call(
        functools.partial(project_kernel, dims, widths),
        in_specs=[vmem] * (1 + len(widths) * n_tm * n_mp + n_seq * n_mp),
        out_specs=[vmem] * (1 + n_tm),
        scratch_shapes=[
            pltpu.VMEM((n_seq * n_mp, rows, cols), jnp.bfloat16),
            pltpu.VMEM((n_tm, frames, tok, half), jnp.float32),
        ],
        out_shape=[jax.ShapeDtypeStruct((frames, tok, half), jnp.float32)]
        + [jax.ShapeDtypeStruct((frames, tok, half), jnp.bfloat16)] * n_tm,
        cost_estimate=pl.CostEstimate(
            flops=2 * rows * deep * half, bytes_accessed=2 * (rows + half) * deep, transcendentals=0
        ),
        compiler_params=pltpu.CompilerParams(vmem_limit_bytes=24 << 20),
        name="project",
    )(coef, *[a for h in attn for k in h for a in k], *[w for j in weights for w in j])


def finish_kernel(n_tm, n_mp, *refs):
    out = refs[-1]
    z, m = lax.axis_index("tm"), lax.axis_index("mp")
    half = refs[0].shape[-1]
    slices = n_tm // n_mp
    for u in range(slices):
        k_here = lax.rem(m * slices + u - z + n_tm, n_tm)
        for h in range(n_mp):
            first = (u * n_mp + h) * half
            for k in range(n_tm):
                for l in range(n_mp):

                    @pl.when((k_here == k) & (lax.rem(m - h + n_mp, n_mp) == l))
                    def _():
                        out[:, :, first : first + half] = refs[k * n_mp + l][...].astype(
                            jnp.float32
                        )


def finish(blocks):
    n_tm, n_mp = len(blocks), len(blocks[0])
    frames, tok, half = blocks[0][0].shape
    vmem = pl.BlockSpec(memory_space=pltpu.VMEM)
    return pl.pallas_call(
        functools.partial(finish_kernel, n_tm, n_mp),
        in_specs=[vmem] * (n_tm * n_mp),
        out_specs=vmem,
        out_shape=jax.ShapeDtypeStruct((frames, tok, n_tm * half), jnp.float32),
        cost_estimate=pl.CostEstimate(
            flops=0, bytes_accessed=8 * frames * tok * n_tm * half, transcendentals=0
        ),
        compiler_params=pltpu.CompilerParams(vmem_limit_bytes=6 << 20),
        name="finish",
    )(*[b for k in blocks for b in k])


def sweep(states, start_step, w_qkv, qk_gain, w_out, time_proj):
    frames, tok, _ = states.shape
    n_tm, n_seq, n_mp = (lax.axis_size(name) for name in ("tm", "seq", "mp"))
    z = lax.axis_index("tm")
    part = tok // n_mp
    depth, cols = w_qkv.shape[1:]
    window = frames * n_tm

    raw = list(spread(states, n_tm, part))
    for k in range(1, n_tm):
        raw[k] = turn(raw[k], "tm", k)
    raw = jnp.stack(raw)
    sides = [raw]
    for j in range(1, n_seq):
        sides.append(turn(raw, "seq", j))
    rows = []
    for side in sides:
        rows.append([side] + [turn(side, "mp", i) for i in range(1, n_mp)])

    shares = list(time_shares(start_step, time_proj, n_tm, window))
    for k in range(1, n_tm):
        shares[k] = turn(shares[k], "tm", k)

    shares_out = load_out(w_out, n_mp)
    weights = [turn(share, "mp", i) if i else share for i, share in enumerate(shares_out)]
    weights = [weights]
    for j in range(1, n_seq):
        weights.append([turn(s, "seq", -j) for s in weights[0]])

    groups = head_groups(cols)
    hidden, coef, *parts_qkv = modulate(start_step, w_qkv, groups, shares, rows)
    hidden = hidden.reshape(n_tm, n_seq * frames * tok, depth)
    proj = []
    for part_qkv in parts_qkv:
        proj.append(
            jnp.einsum(
                "krd,cdh->kcrh",
                hidden,
                part_qkv,
                preferred_element_type=jnp.float32,
            )
        )
    even = z % 2 == 0
    evens = [(i, i ^ 1) for i in range(n_tm)]
    odds = []
    for i in range(n_tm):
        for c in range(n_mp):
            other = i + 1 if i % 2 else i - 1
            inside = 0 <= other < n_tm
            to = other * n_mp + c if inside else i * n_mp + (c + 1) % n_mp
            odds.append((i * n_mp + c, to))

    def incoming(pair):
        first, second = (0.0 if p is None else p.astype(jnp.float32) for p in pair)
        right = jnp.where(z > 0, jnp.where(even, second, first), 0.0)
        return right, jnp.where(z < n_tm - 1, jnp.where(even, first, second), 0.0)

    flows = [(None, None)] * len(groups)
    for t in range(n_tm - 1):
        for h in range(len(groups)):
            right, left = proj[h][(t + 1) % n_tm], proj[h][n_tm - 1 - t]
            if t:
                more_right, more_left = incoming(flows[h])
                right, left = right + more_right, left + more_left
            first = jnp.where(even, right, left).astype(jnp.float16)
            second = jnp.where(even, left, right).astype(jnp.float16)
            first = lax.ppermute(first, "tm", evens)
            if t:
                second = lax.ppermute(second, ("tm", "mp"), odds)
                first, second = lax.optimization_barrier((first, second))
            flows[h] = (first, second if t else None)
    gathered = []
    for h, (lane, size) in enumerate(groups):
        right, left = incoming(flows[h])
        total = proj[h][0] + right + left
        total = total.reshape(3, n_seq, frames, tok, size)
        attn = attend(total, qk_gain[:, lane : lane + size])
        attn = jnp.stack([attn[0]] + [turn(attn[j], "seq", -j) for j in range(1, n_seq)])
        pieces = [attn]
        for k in range(1, n_tm):
            pieces.append(turn(attn, "tm", k))
        gathered.append([[g] + [turn(g, "mp", i) for i in range(1, n_mp)] for g in pieces])

    own, *moved = project(
        gathered, weights, coef, (n_tm, n_seq, n_mp, frames, part, cols), groups
    )
    blocks = []
    for k in range(n_tm):
        block = moved[0]
        if k:
            block = turn(moved[k], "tm", -k)
        others = [turn(block, "mp", i) for i in range(1, n_mp)]
        blocks.append([block if k else own] + others)
    return finish(blocks)


def solution(mesh):
    return jax.shard_map(
        sweep,
        mesh=mesh,
        in_specs=(
            P(("group", "tm"), "seq", None),
            P("group"),
            P(None, "tm", ("seq", "mp")),
            P(None, ("seq", "mp")),
            P("tm", ("seq", "mp")),
            P("tm", None),
        ),
        out_specs=P(("group", "tm"), "seq", "mp"),
        check_vma=False,
    )
```

```python
import functools

import jax
import jax.numpy as jnp
from jax import lax
from jax.experimental import pallas as pl
from jax.experimental.pallas import tpu as pltpu
from jax.sharding import PartitionSpec as P


HEAD_DIM = 128
FREQ = 256
STEPS = 100
LANES = 128


sample_shift = 5.0
norm_eps = 1e-06


def sigma_of(index):
    unit = 1.0 - index.astype(jnp.float32) / jnp.float32(STEPS)
    return sample_shift * unit / (1.0 + (sample_shift - 1.0) * unit)


def turn(block, axis, distance):
    size = lax.axis_size(axis)
    return lax.ppermute(block, axis, [(i, (i + distance) % size) for i in range(size)])


def head_norm(values, gain):
    meansq = jnp.mean(values * values, axis=-1, keepdims=True)
    return (values * lax.rsqrt(meansq + norm_eps) * gain).astype(jnp.bfloat16)


def head_groups(cols):
    heads = cols // HEAD_DIM
    first = (heads + 1) // 2 * HEAD_DIM
    return ((0, first), (first, cols - first)) if first < cols else ((0, cols),)


def attend_kernel(n_seq, heads, gain_ref, whole_ref, *outs):
    inv_root = 1.0 / jnp.sqrt(jnp.float32(HEAD_DIM))
    rows = whole_ref.shape[3]
    for h in range(heads):
        lanes = pl.ds(h * HEAD_DIM, HEAD_DIM)
        q, k, v = (
            jnp.concatenate([whole_ref[c, j, 0, :, lanes] for j in range(n_seq)], axis=0)
            for c in range(3)
        )
        q = head_norm(q, gain_ref[0:1, lanes])
        k = head_norm(k, gain_ref[1:2, lanes])
        scores = lax.dot_general(
            q, k, (((1,), (1,)), ((), ())), preferred_element_type=jnp.float32
        )
        expo = jnp.exp(scores * inv_root)
        probs = (expo / jnp.sum(expo, axis=-1, keepdims=True)).astype(jnp.bfloat16)
        attn = jnp.dot(
            probs, v.astype(jnp.bfloat16), preferred_element_type=jnp.float32
        ).astype(jnp.bfloat16)
        for j, out in enumerate(outs):
            out[0, :, lanes] = attn[j * rows : (j + 1) * rows]


def attend(whole, gain):
    _, n_seq, frames, rows, cols = whole.shape
    heads = cols // HEAD_DIM
    tokens = rows * n_seq
    out = jax.ShapeDtypeStruct((frames, rows, cols), jnp.bfloat16)
    return pl.pallas_call(
        functools.partial(attend_kernel, n_seq, heads),
        grid=(frames,),
        in_specs=[
            pl.BlockSpec((2, cols), lambda f: (0, 0)),
            pl.BlockSpec((3, n_seq, 1, rows, cols), lambda f: (0, 0, f, 0, 0)),
        ],
        out_specs=[pl.BlockSpec((1, rows, cols), lambda f: (f, 0, 0))] * n_seq,
        out_shape=[out] * n_seq,
        cost_estimate=pl.CostEstimate(
            flops=4 * frames * heads * tokens * tokens * HEAD_DIM,
            bytes_accessed=14 * frames * tokens * cols,
            transcendentals=frames * heads * tokens * tokens,
        ),
        compiler_params=pltpu.CompilerParams(vmem_limit_bytes=6 << 20),
        name="attend",
    )(gain, whole)


def spread_kernel(n_tm, states_ref, *outs):
    z, m = lax.axis_index("tm"), lax.axis_index("mp")
    frames, _, width = states_ref.shape
    part, depth = outs[0].shape[1], width // n_tm
    own = pl.ds(pl.multiple_of(m * part, part), part)
    lane = lax.broadcasted_iota(jnp.int32, (part, LANES), 1)
    for f in range(frames):
        field = states_ref[f, own, :].astype(jnp.float32)
        mean = jnp.mean(field, axis=-1, keepdims=True)
        centred = field - mean
        var = jnp.mean(centred * centred, axis=-1, keepdims=True)
        tail = jnp.zeros((part, LANES), jnp.float32)
        for place, rest in enumerate((mean, lax.rsqrt(var + norm_eps))):
            for term in range(3):
                cut = rest.astype(jnp.bfloat16).astype(jnp.float32)
                tail = jnp.where(lane == 3 * place + term, cut, tail)
                rest = rest - cut
        tail = tail.astype(jnp.bfloat16)
        for k, out in enumerate(outs):
            out[f, :, depth:] = tail
            for s in range(n_tm):

                @pl.when(lax.rem(z + k, n_tm) == s)
                def _():
                    out[f, :, :depth] = states_ref[f, own, s * depth : (s + 1) * depth]


def spread(states, n_tm, part):
    frames, _, width = states.shape
    out = jax.ShapeDtypeStruct((frames, part, width // n_tm + LANES), jnp.bfloat16)
    return pl.pallas_call(
        functools.partial(spread_kernel, n_tm),
        in_specs=[pl.BlockSpec(memory_space=pltpu.VMEM)],
        out_specs=[pl.BlockSpec(memory_space=pltpu.VMEM)] * n_tm,
        out_shape=[out] * n_tm,
        cost_estimate=pl.CostEstimate(
            flops=10 * part * width, bytes_accessed=4 * part * width, transcendentals=0
        ),
        compiler_params=pltpu.CompilerParams(vmem_limit_bytes=4 << 20),
        name="spread",
    )(states)


def time_kernel(n_tm, step_ref, proj_ref, *outs):
    z = lax.axis_index("tm")
    freq_rows, wide = proj_ref.shape
    window, depth = outs[0].shape[1:]
    half_freq = FREQ // 2
    index = step_ref[0] + lax.broadcasted_iota(jnp.int32, (window, freq_rows), 0)
    feature = z * freq_rows + lax.broadcasted_iota(jnp.int32, (window, freq_rows), 1)
    late = feature >= half_freq
    rank = jnp.where(late, feature - half_freq, feature).astype(jnp.float32)
    freqs = jnp.exp(-jnp.log(jnp.float32(10000.0)) * rank / jnp.float32(half_freq))
    angles = (1000.0 * sigma_of(index)) * freqs
    emb = jnp.where(late, jnp.sin(angles), jnp.cos(angles)).astype(jnp.bfloat16)
    for k, out in enumerate(outs):
        for s in range(n_tm):

            @pl.when(lax.rem(z + k, n_tm) == s)
            def _():
                for c in range(3):
                    first = c * (wide // 3) + s * depth
                    out[c] = jnp.dot(
                        emb, proj_ref[:, first : first + depth], preferred_element_type=jnp.float32
                    )


def time_shares(start_step, time_proj, n_tm, window):
    freq_rows, wide = time_proj.shape
    out = jax.ShapeDtypeStruct((3, window, wide // (3 * n_tm)), jnp.float32)
    smem, vmem = (pl.BlockSpec(memory_space=space) for space in (pltpu.SMEM, pltpu.VMEM))
    return pl.pallas_call(
        functools.partial(time_kernel, n_tm),
        in_specs=[smem, vmem],
        out_specs=[vmem] * n_tm,
        out_shape=[out] * n_tm,
        cost_estimate=pl.CostEstimate(
            flops=2 * window * freq_rows * wide, bytes_accessed=2 * freq_rows * wide, transcendentals=0
        ),
        compiler_params=pltpu.CompilerParams(vmem_limit_bytes=6 << 20),
        name="time_shares",
    )(start_step, time_proj)


def load_kernel(n_mp, w_ref, *refs):
    outs, sems = refs[:-1], refs[-1]
    copies = []
    for i, out in enumerate(outs):
        rows = out.shape[0]
        share = lax.rem(lax.axis_index("mp") + i, n_mp)
        source = w_ref.at[pl.ds(pl.multiple_of(share * rows, rows), rows)]
        copies.append(pltpu.make_async_copy(source, out, sems.at[i]))
    for copy in copies:
        copy.start()
    for copy in copies:
        copy.wait()


def load_out(weights, n_mp):
    share = jax.ShapeDtypeStruct((weights.shape[0] // n_mp, weights.shape[1]), weights.dtype)
    return pl.pallas_call(
        functools.partial(load_kernel, n_mp),
        in_specs=[pl.BlockSpec(memory_space=pltpu.HBM)],
        out_specs=[pl.BlockSpec(memory_space=pltpu.VMEM)] * n_mp,
        out_shape=[share] * n_mp,
        scratch_shapes=[pltpu.SemaphoreType.DMA((n_mp,))],
        cost_estimate=pl.CostEstimate(flops=0, bytes_accessed=2 * weights.size, transcendentals=0),
        compiler_params=pltpu.CompilerParams(vmem_limit_bytes=8 << 20),
        name="load_out",
    )(weights)


def modulate_kernel(n_tm, n_seq, n_mp, cuts, step_ref, w_ref, *refs):
    shares, rows = refs[:n_tm], refs[n_tm : n_tm + n_seq * n_mp]
    hidden_ref, coef_ref, *w_outs, mod_scr, sems = refs[n_tm + n_seq * n_mp :]
    copies = [
        pltpu.make_async_copy(w_ref.at[:, :, pl.ds(lane, size)], out, sems.at[h])
        for h, ((lane, size), out) in enumerate(zip(cuts, w_outs))
    ]
    z, k = lax.axis_index("tm"), pl.program_id(0)
    _, frames, part, wide = rows[0].shape
    depth = wide - LANES

    @pl.when(k == 0)
    def _():
        for copy in copies:
            copy.start()
        total = shares[0][...]
        for share in shares[1:]:
            total = total + share[...]
        mod_scr[...] = total

    for f in range(frames):
        step = lax.rem(z - k + n_tm, n_tm) * frames + f
        shift, scale, gate = (mod_scr[c, pl.ds(step, 1), :] for c in range(3))
        index = jnp.full((1, depth), step_ref[0] + step, jnp.int32)
        coef_ref[0, f : f + 1, :] = (sigma_of(index + 1) - sigma_of(index)) * gate
        for j in range(n_seq):
            for i in range(n_mp):
                row = rows[j * n_mp + i]
                tail = row[0, f, :, depth:].astype(jnp.float32)
                mean = tail[:, 0:1] + tail[:, 1:2] + tail[:, 2:3]
                rstd = tail[:, 3:4] + tail[:, 4:5] + tail[:, 5:6]
                normed = (row[0, f, :, :depth].astype(jnp.float32) - mean) * rstd
                hidden_ref[0, j, f, i * part : (i + 1) * part, :] = (
                    normed * (1.0 + scale) + shift
                ).astype(jnp.bfloat16)

    @pl.when(k == n_tm - 1)
    def _():
        for copy in copies:
            copy.wait()


def modulate(start_step, w_qkv, cuts, shares, rows):
    n_tm, n_seq, n_mp = len(shares), len(rows), len(rows[0])
    _, frames, part, wide = rows[0][0].shape
    depth = wide - LANES
    window = shares[0].shape[1]
    shape = (n_tm, n_seq, frames, n_mp * part, depth)
    return pl.pallas_call(
        functools.partial(modulate_kernel, n_tm, n_seq, n_mp, cuts),
        grid=(n_tm,),
        in_specs=[pl.BlockSpec(memory_space=pltpu.SMEM), pl.BlockSpec(memory_space=pltpu.HBM)]
        + [pl.BlockSpec((3, window, depth), lambda k: (0, 0, 0))] * n_tm
        + [pl.BlockSpec((1, frames, part, wide), lambda k: (k, 0, 0, 0))] * (n_seq * n_mp),
        out_specs=[
            pl.BlockSpec((1,) + shape[1:], lambda k: (k, 0, 0, 0, 0)),
            pl.BlockSpec((1, frames, depth), lambda k: (k, 0, 0)),
        ]
        + [pl.BlockSpec(memory_space=pl.ANY)] * len(cuts),
        scratch_shapes=[
            pltpu.VMEM((3, window, depth), jnp.float32),
            pltpu.SemaphoreType.DMA((len(cuts),)),
        ],
        out_shape=[
            jax.ShapeDtypeStruct(shape, jnp.bfloat16),
            jax.ShapeDtypeStruct((n_tm, frames, depth), jnp.float32),
        ]
        + [jax.ShapeDtypeStruct(w_qkv.shape[:2] + (size,), w_qkv.dtype) for _, size in cuts],
        cost_estimate=pl.CostEstimate(
            flops=4 * n_tm * n_seq * frames * n_mp * part * depth,
            bytes_accessed=4 * n_tm * n_seq * frames * n_mp * part * depth,
            transcendentals=0,
        ),
        compiler_params=pltpu.CompilerParams(vmem_limit_bytes=48 << 20),
        name="modulate",
    )(start_step, w_qkv, *shares, *[r for side in rows for r in side])


def project_kernel(dims, widths, coef_ref, *refs):
    n_tm, n_seq, n_mp, frames, part, _ = dims
    n_attn = len(widths) * n_tm * n_mp
    attn_refs = refs[:n_attn]
    w_refs = refs[n_attn : n_attn + n_seq * n_mp]
    outs = refs[n_attn + n_seq * n_mp :]
    own_ref, moved_refs, (rows_scr, sum_scr) = outs[0], outs[1:-2], outs[-2:]
    z, m = lax.axis_index("tm"), lax.axis_index("mp")
    block = n_mp * part
    per = frames * block
    half = own_ref.shape[-1]
    total = None
    for j in range(n_seq):
        for l in range(n_mp):
            at = j * n_mp + l
            for k in range(n_tm):
                for f in range(frames):
                    for i in range(n_mp):
                        first = k * per + f * block + i * part
                        source = (i - l) % n_mp * part
                        for h, (lane, width) in enumerate(widths):
                            piece = attn_refs[(h * n_tm + k) * n_mp + l]
                            rows_scr[at, first : first + part, lane : lane + width] = piece[
                                j, f, source : source + part, :
                            ]
            product = lax.dot_general(
                rows_scr[at],
                w_refs[at][...],
                (((1,), (1,)), ((), ())),
                preferred_element_type=jnp.float32,
            )
            total = product if total is None else total + product
    for k in range(n_tm):
        for f in range(frames):
            first = k * per + f * block
            factor = coef_ref[k, f : f + 1, :half]
            for mm in range(1, n_mp):
                other = coef_ref[k, f : f + 1, mm * half : (mm + 1) * half]
                factor = jnp.where(m == mm, other, factor)
            drift = total[first : first + block] * factor
            sum_scr[lax.rem(z - k + n_tm, n_tm), f] = drift
    for s in range(n_tm):
        for f in range(frames):
            if s or f:
                before = sum_scr[s, f - 1] if f else sum_scr[s - 1, frames - 1]
                sum_scr[s, f] = sum_scr[s, f] + before
    for k in range(n_tm):
        own = lax.rem(z - k + n_tm, n_tm)
        for f in range(frames):
            for i in range(n_mp):
                to = pl.ds(pl.multiple_of(lax.rem(m - i + n_mp, n_mp) * part, part), part)
                piece = sum_scr[own, f, i * part : (i + 1) * part, :]
                moved_refs[k][f, to, :] = piece.astype(jnp.bfloat16)
                if k == 0:
                    own_ref[f, to, :] = piece


def project(attn, weights, coef, dims, widths):
    n_tm, n_seq, n_mp, frames, part, cols = dims
    half = weights[0][0].shape[0]
    tok = n_mp * part
    rows = n_tm * frames * tok
    deep = n_seq * n_mp * cols
    vmem = pl.BlockSpec(memory_space=pltpu.VMEM)
    return pl.pallas_call(
        functools.partial(project_kernel, dims, widths),
        in_specs=[vmem] * (1 + len(widths) * n_tm * n_mp + n_seq * n_mp),
        out_specs=[vmem] * (1 + n_tm),
        scratch_shapes=[
            pltpu.VMEM((n_seq * n_mp, rows, cols), jnp.bfloat16),
            pltpu.VMEM((n_tm, frames, tok, half), jnp.float32),
        ],
        out_shape=[jax.ShapeDtypeStruct((frames, tok, half), jnp.float32)]
        + [jax.ShapeDtypeStruct((frames, tok, half), jnp.bfloat16)] * n_tm,
        cost_estimate=pl.CostEstimate(
            flops=2 * rows * deep * half, bytes_accessed=2 * (rows + half) * deep, transcendentals=0
        ),
        compiler_params=pltpu.CompilerParams(vmem_limit_bytes=24 << 20),
        name="project",
    )(coef, *[a for h in attn for k in h for a in k], *[w for j in weights for w in j])


def finish_kernel(n_tm, n_mp, *refs):
    out = refs[-1]
    z, m = lax.axis_index("tm"), lax.axis_index("mp")
    half = refs[0].shape[-1]
    slices = n_tm // n_mp
    for u in range(slices):
        k_here = lax.rem(m * slices + u - z + n_tm, n_tm)
        for h in range(n_mp):
            first = (u * n_mp + h) * half
            for k in range(n_tm):
                for l in range(n_mp):

                    @pl.when((k_here == k) & (lax.rem(m - h + n_mp, n_mp) == l))
                    def _():
                        out[:, :, first : first + half] = refs[k * n_mp + l][...].astype(
                            jnp.float32
                        )


def finish(blocks):
    n_tm, n_mp = len(blocks), len(blocks[0])
    frames, tok, half = blocks[0][0].shape
    vmem = pl.BlockSpec(memory_space=pltpu.VMEM)
    return pl.pallas_call(
        functools.partial(finish_kernel, n_tm, n_mp),
        in_specs=[vmem] * (n_tm * n_mp),
        out_specs=vmem,
        out_shape=jax.ShapeDtypeStruct((frames, tok, n_tm * half), jnp.float32),
        cost_estimate=pl.CostEstimate(
            flops=0, bytes_accessed=8 * frames * tok * n_tm * half, transcendentals=0
        ),
        compiler_params=pltpu.CompilerParams(vmem_limit_bytes=6 << 20),
        name="finish",
    )(*[b for k in blocks for b in k])


def sweep(states, start_step, w_qkv, qk_gain, w_out, time_proj):
    frames, tok, _ = states.shape
    n_tm, n_seq, n_mp = (lax.axis_size(name) for name in ("tm", "seq", "mp"))
    z = lax.axis_index("tm")
    part = tok // n_mp
    depth, cols = w_qkv.shape[1:]
    window = frames * n_tm

    raw = list(spread(states, n_tm, part))
    for k in range(1, n_tm):
        raw[k] = turn(raw[k], "tm", k)
    raw = jnp.stack(raw)
    sides = [raw]
    for j in range(1, n_seq):
        sides.append(turn(raw, "seq", j))
    rows = []
    for side in sides:
        rows.append([side] + [turn(side, "mp", i) for i in range(1, n_mp)])

    shares = list(time_shares(start_step, time_proj, n_tm, window))
    for k in range(1, n_tm):
        shares[k] = turn(shares[k], "tm", k)

    shares_out = load_out(w_out, n_mp)
    weights = [turn(share, "mp", i) if i else share for i, share in enumerate(shares_out)]
    weights = [weights]
    for j in range(1, n_seq):
        weights.append([turn(s, "seq", -j) for s in weights[0]])

    groups = head_groups(cols)
    hidden, coef, first_qkv = modulate(start_step, w_qkv, groups[:1], shares, rows)
    hidden = hidden.reshape(n_tm, n_seq * frames * tok, depth)
    proj = []
    for h, (lane, size) in enumerate(groups):
        part_qkv = w_qkv[:, :, lane : lane + size] if h else first_qkv
        proj.append(
            jnp.einsum(
                "krd,cdh->kcrh",
                hidden,
                part_qkv,
                preferred_element_type=jnp.float32,
            )
        )
    even = z % 2 == 0
    evens = [(i, i ^ 1) for i in range(n_tm)]
    odds = []
    for i in range(n_tm):
        for c in range(n_mp):
            other = i + 1 if i % 2 else i - 1
            inside = 0 <= other < n_tm
            to = other * n_mp + c if inside else i * n_mp + (c + 1) % n_mp
            odds.append((i * n_mp + c, to))

    def incoming(pair):
        first, second = (0.0 if p is None else p.astype(jnp.float32) for p in pair)
        right = jnp.where(z > 0, jnp.where(even, second, first), 0.0)
        return right, jnp.where(z < n_tm - 1, jnp.where(even, first, second), 0.0)

    flows = [(None, None)] * len(groups)
    for t in range(n_tm - 1):
        for h in range(len(groups)):
            right, left = proj[h][(t + 1) % n_tm], proj[h][n_tm - 1 - t]
            if t:
                more_right, more_left = incoming(flows[h])
                right, left = right + more_right, left + more_left
            first = jnp.where(even, right, left).astype(jnp.float16)
            second = jnp.where(even, left, right).astype(jnp.float16)
            first = lax.ppermute(first, "tm", evens)
            if t:
                second = lax.ppermute(second, ("tm", "mp"), odds)
                first, second = lax.optimization_barrier((first, second))
            flows[h] = (first, second if t else None)
    gathered = []
    for h, (lane, size) in enumerate(groups):
        right, left = incoming(flows[h])
        total = proj[h][0] + right + left
        total = total.reshape(3, n_seq, frames, tok, size)
        attn = attend(total, qk_gain[:, lane : lane + size])
        attn = jnp.stack([attn[0]] + [turn(attn[j], "seq", -j) for j in range(1, n_seq)])
        pieces = [attn]
        for k in range(1, n_tm):
            pieces.append(turn(attn, "tm", k))
        gathered.append([[g] + [turn(g, "mp", i) for i in range(1, n_mp)] for g in pieces])

    own, *moved = project(
        gathered, weights, coef, (n_tm, n_seq, n_mp, frames, part, cols), groups
    )
    blocks = []
    for k in range(n_tm):
        block = moved[0]
        if k:
            block = turn(moved[k], "tm", -k)
        others = [turn(block, "mp", i) for i in range(1, n_mp)]
        blocks.append([block if k else own] + others)
    return finish(blocks)


def solution(mesh):
    return jax.shard_map(
        sweep,
        mesh=mesh,
        in_specs=(
            P(("group", "tm"), "seq", None),
            P("group"),
            P(None, "tm", ("seq", "mp")),
            P(None, ("seq", "mp")),
            P("tm", ("seq", "mp")),
            P("tm", None),
        ),
        out_specs=P(("group", "tm"), "seq", "mp"),
        check_vma=False,
    )
```

```python
import functools

import jax
import jax.numpy as jnp
from jax import lax
from jax.experimental import pallas as pl
from jax.experimental.pallas import tpu as pltpu
from jax.sharding import PartitionSpec as P


HEAD_DIM = 128
FREQ = 256
STEPS = 100
LANES = 128
DMA_PIECES = 4


sample_shift = 5.0
norm_eps = 1e-06


def sigma_of(index):
    unit = 1.0 - index.astype(jnp.float32) / jnp.float32(STEPS)
    return sample_shift * unit / (1.0 + (sample_shift - 1.0) * unit)


def turn(block, axis, distance):
    size = lax.axis_size(axis)
    return lax.ppermute(block, axis, [(i, (i + distance) % size) for i in range(size)])


def head_norm(values, gain):
    meansq = jnp.mean(values * values, axis=-1, keepdims=True)
    return (values * lax.rsqrt(meansq + norm_eps) * gain).astype(jnp.bfloat16)


def head_groups(cols):
    heads = cols // HEAD_DIM
    first = (heads + 1) // 2 * HEAD_DIM
    return ((0, first), (first, cols - first)) if first < cols else ((0, cols),)


def attend_kernel(n_seq, heads, gain_ref, whole_ref, *outs):
    inv_root = 1.0 / jnp.sqrt(jnp.float32(HEAD_DIM))
    rows = whole_ref.shape[3]
    for h in range(heads):
        lanes = pl.ds(h * HEAD_DIM, HEAD_DIM)
        q, k, v = (
            jnp.concatenate([whole_ref[c, j, 0, :, lanes] for j in range(n_seq)], axis=0)
            for c in range(3)
        )
        q = head_norm(q, gain_ref[0:1, lanes])
        k = head_norm(k, gain_ref[1:2, lanes])
        scores = lax.dot_general(
            q, k, (((1,), (1,)), ((), ())), preferred_element_type=jnp.float32
        )
        expo = jnp.exp(scores * inv_root)
        probs = (expo / jnp.sum(expo, axis=-1, keepdims=True)).astype(jnp.bfloat16)
        attn = jnp.dot(
            probs, v.astype(jnp.bfloat16), preferred_element_type=jnp.float32
        ).astype(jnp.bfloat16)
        for j, out in enumerate(outs):
            out[0, :, lanes] = attn[j * rows : (j + 1) * rows]


def attend(whole, gain):
    _, n_seq, frames, rows, cols = whole.shape
    heads = cols // HEAD_DIM
    tokens = rows * n_seq
    out = jax.ShapeDtypeStruct((frames, rows, cols), jnp.bfloat16)
    return pl.pallas_call(
        functools.partial(attend_kernel, n_seq, heads),
        grid=(frames,),
        in_specs=[
            pl.BlockSpec((2, cols), lambda f: (0, 0)),
            pl.BlockSpec((3, n_seq, 1, rows, cols), lambda f: (0, 0, f, 0, 0)),
        ],
        out_specs=[pl.BlockSpec((1, rows, cols), lambda f: (f, 0, 0))] * n_seq,
        out_shape=[out] * n_seq,
        cost_estimate=pl.CostEstimate(
            flops=4 * frames * heads * tokens * tokens * HEAD_DIM,
            bytes_accessed=14 * frames * tokens * cols,
            transcendentals=frames * heads * tokens * tokens,
        ),
        compiler_params=pltpu.CompilerParams(vmem_limit_bytes=6 << 20),
        name="attend",
    )(gain, whole)


def spread_kernel(n_tm, states_ref, *outs):
    z, m = lax.axis_index("tm"), lax.axis_index("mp")
    frames, _, width = states_ref.shape
    part, depth = outs[0].shape[1], width // n_tm
    own = pl.ds(pl.multiple_of(m * part, part), part)
    lane = lax.broadcasted_iota(jnp.int32, (part, LANES), 1)
    for f in range(frames):
        field = states_ref[f, own, :].astype(jnp.float32)
        mean = jnp.mean(field, axis=-1, keepdims=True)
        centred = field - mean
        var = jnp.mean(centred * centred, axis=-1, keepdims=True)
        tail = jnp.zeros((part, LANES), jnp.float32)
        for place, rest in enumerate((mean, lax.rsqrt(var + norm_eps))):
            for term in range(3):
                cut = rest.astype(jnp.bfloat16).astype(jnp.float32)
                tail = jnp.where(lane == 3 * place + term, cut, tail)
                rest = rest - cut
        tail = tail.astype(jnp.bfloat16)
        for k, out in enumerate(outs):
            out[f, :, depth:] = tail
            for s in range(n_tm):

                @pl.when(lax.rem(z + k, n_tm) == s)
                def _():
                    out[f, :, :depth] = states_ref[f, own, s * depth : (s + 1) * depth]


def spread(states, n_tm, part):
    frames, _, width = states.shape
    out = jax.ShapeDtypeStruct((frames, part, width // n_tm + LANES), jnp.bfloat16)
    return pl.pallas_call(
        functools.partial(spread_kernel, n_tm),
        in_specs=[pl.BlockSpec(memory_space=pltpu.VMEM)],
        out_specs=[pl.BlockSpec(memory_space=pltpu.VMEM)] * n_tm,
        out_shape=[out] * n_tm,
        cost_estimate=pl.CostEstimate(
            flops=10 * part * width, bytes_accessed=4 * part * width, transcendentals=0
        ),
        compiler_params=pltpu.CompilerParams(vmem_limit_bytes=4 << 20),
        name="spread",
    )(states)


def time_kernel(n_tm, step_ref, proj_ref, *outs):
    z = lax.axis_index("tm")
    freq_rows, wide = proj_ref.shape
    window, depth = outs[0].shape[1:]
    half_freq = FREQ // 2
    index = step_ref[0] + lax.broadcasted_iota(jnp.int32, (window, freq_rows), 0)
    feature = z * freq_rows + lax.broadcasted_iota(jnp.int32, (window, freq_rows), 1)
    late = feature >= half_freq
    rank = jnp.where(late, feature - half_freq, feature).astype(jnp.float32)
    freqs = jnp.exp(-jnp.log(jnp.float32(10000.0)) * rank / jnp.float32(half_freq))
    angles = (1000.0 * sigma_of(index)) * freqs
    emb = jnp.where(late, jnp.sin(angles), jnp.cos(angles)).astype(jnp.bfloat16)
    for k, out in enumerate(outs):
        for s in range(n_tm):

            @pl.when(lax.rem(z + k, n_tm) == s)
            def _():
                for c in range(3):
                    first = c * (wide // 3) + s * depth
                    out[c] = jnp.dot(
                        emb, proj_ref[:, first : first + depth], preferred_element_type=jnp.float32
                    )


def time_shares(start_step, time_proj, n_tm, window):
    freq_rows, wide = time_proj.shape
    out = jax.ShapeDtypeStruct((3, window, wide // (3 * n_tm)), jnp.float32)
    smem, vmem = (pl.BlockSpec(memory_space=space) for space in (pltpu.SMEM, pltpu.VMEM))
    return pl.pallas_call(
        functools.partial(time_kernel, n_tm),
        in_specs=[smem, vmem],
        out_specs=[vmem] * n_tm,
        out_shape=[out] * n_tm,
        cost_estimate=pl.CostEstimate(
            flops=2 * window * freq_rows * wide, bytes_accessed=2 * freq_rows * wide, transcendentals=0
        ),
        compiler_params=pltpu.CompilerParams(vmem_limit_bytes=6 << 20),
        name="time_shares",
    )(start_step, time_proj)


def load_kernel(n_mp, w_ref, *refs):
    outs, sems = refs[:-1], refs[-1]
    copies = []
    for i, out in enumerate(outs):
        rows = out.shape[0]
        share = lax.rem(lax.axis_index("mp") + i, n_mp)
        source = w_ref.at[pl.ds(pl.multiple_of(share * rows, rows), rows)]
        copies.append(pltpu.make_async_copy(source, out, sems.at[i]))
    for copy in copies:
        copy.start()
    for copy in copies:
        copy.wait()


def load_out(weights, n_mp):
    share = jax.ShapeDtypeStruct((weights.shape[0] // n_mp, weights.shape[1]), weights.dtype)
    return pl.pallas_call(
        functools.partial(load_kernel, n_mp),
        in_specs=[pl.BlockSpec(memory_space=pltpu.HBM)],
        out_specs=[pl.BlockSpec(memory_space=pltpu.VMEM)] * n_mp,
        out_shape=[share] * n_mp,
        scratch_shapes=[pltpu.SemaphoreType.DMA((n_mp,))],
        cost_estimate=pl.CostEstimate(flops=0, bytes_accessed=2 * weights.size, transcendentals=0),
        compiler_params=pltpu.CompilerParams(vmem_limit_bytes=8 << 20),
        name="load_out",
    )(weights)


def modulate_kernel(n_tm, n_seq, n_mp, cuts, step_ref, w_ref, *refs):
    shares, rows = refs[:n_tm], refs[n_tm : n_tm + n_seq * n_mp]
    hidden_ref, coef_ref, *w_outs, mod_scr, sems = refs[n_tm + n_seq * n_mp :]
    stride = w_ref.shape[1] // DMA_PIECES
    copies = []
    for (lane, size), out in zip(cuts, w_outs):
        for c in range(w_ref.shape[0]):
            for piece in range(DMA_PIECES):
                rows_here = pl.ds(piece * stride, stride)
                copies.append(
                    pltpu.make_async_copy(
                        w_ref.at[c, rows_here, pl.ds(lane, size)],
                        out.at[c, rows_here],
                        sems.at[len(copies)],
                    )
                )
    z, k = lax.axis_index("tm"), pl.program_id(0)
    _, frames, part, wide = rows[0].shape
    depth = wide - LANES

    @pl.when(k == 0)
    def _():
        for copy in copies:
            copy.start()
        total = shares[0][...]
        for share in shares[1:]:
            total = total + share[...]
        mod_scr[...] = total

    for f in range(frames):
        step = lax.rem(z - k + n_tm, n_tm) * frames + f
        shift, scale, gate = (mod_scr[c, pl.ds(step, 1), :] for c in range(3))
        index = jnp.full((1, depth), step_ref[0] + step, jnp.int32)
        coef_ref[0, f : f + 1, :] = (sigma_of(index + 1) - sigma_of(index)) * gate
        for j in range(n_seq):
            for i in range(n_mp):
                row = rows[j * n_mp + i]
                tail = row[0, f, :, depth:].astype(jnp.float32)
                mean = tail[:, 0:1] + tail[:, 1:2] + tail[:, 2:3]
                rstd = tail[:, 3:4] + tail[:, 4:5] + tail[:, 5:6]
                normed = (row[0, f, :, :depth].astype(jnp.float32) - mean) * rstd
                hidden_ref[0, j, f, i * part : (i + 1) * part, :] = (
                    normed * (1.0 + scale) + shift
                ).astype(jnp.bfloat16)

    @pl.when(k == n_tm - 1)
    def _():
        for copy in copies:
            copy.wait()


def modulate(start_step, w_qkv, cuts, shares, rows):
    n_tm, n_seq, n_mp = len(shares), len(rows), len(rows[0])
    _, frames, part, wide = rows[0][0].shape
    three = w_qkv.shape[0]
    depth = wide - LANES
    window = shares[0].shape[1]
    shape = (n_tm, n_seq, frames, n_mp * part, depth)
    return pl.pallas_call(
        functools.partial(modulate_kernel, n_tm, n_seq, n_mp, cuts),
        grid=(n_tm,),
        in_specs=[pl.BlockSpec(memory_space=pltpu.SMEM), pl.BlockSpec(memory_space=pltpu.HBM)]
        + [pl.BlockSpec((3, window, depth), lambda k: (0, 0, 0))] * n_tm
        + [pl.BlockSpec((1, frames, part, wide), lambda k: (k, 0, 0, 0))] * (n_seq * n_mp),
        out_specs=[
            pl.BlockSpec((1,) + shape[1:], lambda k: (k, 0, 0, 0, 0)),
            pl.BlockSpec((1, frames, depth), lambda k: (k, 0, 0)),
        ]
        + [pl.BlockSpec(memory_space=pl.ANY)] * len(cuts),
        scratch_shapes=[
            pltpu.VMEM((3, window, depth), jnp.float32),
            pltpu.SemaphoreType.DMA((len(cuts) * three * DMA_PIECES,)),
        ],
        out_shape=[
            jax.ShapeDtypeStruct(shape, jnp.bfloat16),
            jax.ShapeDtypeStruct((n_tm, frames, depth), jnp.float32),
        ]
        + [jax.ShapeDtypeStruct(w_qkv.shape[:2] + (size,), w_qkv.dtype) for _, size in cuts],
        cost_estimate=pl.CostEstimate(
            flops=4 * n_tm * n_seq * frames * n_mp * part * depth,
            bytes_accessed=4 * n_tm * n_seq * frames * n_mp * part * depth,
            transcendentals=0,
        ),
        compiler_params=pltpu.CompilerParams(vmem_limit_bytes=48 << 20),
        name="modulate",
    )(start_step, w_qkv, *shares, *[r for side in rows for r in side])


def project_kernel(dims, widths, coef_ref, *refs):
    n_tm, n_seq, n_mp, frames, part, _ = dims
    n_attn = len(widths) * n_tm * n_mp
    attn_refs = refs[:n_attn]
    w_refs = refs[n_attn : n_attn + n_seq * n_mp]
    outs = refs[n_attn + n_seq * n_mp :]
    own_ref, moved_refs, (rows_scr, sum_scr) = outs[0], outs[1:-2], outs[-2:]
    z, m = lax.axis_index("tm"), lax.axis_index("mp")
    block = n_mp * part
    per = frames * block
    half = own_ref.shape[-1]
    total = None
    for j in range(n_seq):
        for l in range(n_mp):
            at = j * n_mp + l
            for k in range(n_tm):
                for f in range(frames):
                    for i in range(n_mp):
                        first = k * per + f * block + i * part
                        source = (i - l) % n_mp * part
                        for h, (lane, width) in enumerate(widths):
                            piece = attn_refs[(h * n_tm + k) * n_mp + l]
                            rows_scr[at, first : first + part, lane : lane + width] = piece[
                                j, f, source : source + part, :
                            ]
            product = lax.dot_general(
                rows_scr[at],
                w_refs[at][...],
                (((1,), (1,)), ((), ())),
                preferred_element_type=jnp.float32,
            )
            total = product if total is None else total + product
    for k in range(n_tm):
        for f in range(frames):
            first = k * per + f * block
            factor = coef_ref[k, f : f + 1, :half]
            for mm in range(1, n_mp):
                other = coef_ref[k, f : f + 1, mm * half : (mm + 1) * half]
                factor = jnp.where(m == mm, other, factor)
            drift = total[first : first + block] * factor
            sum_scr[lax.rem(z - k + n_tm, n_tm), f] = drift
    for s in range(n_tm):
        for f in range(frames):
            if s or f:
                before = sum_scr[s, f - 1] if f else sum_scr[s - 1, frames - 1]
                sum_scr[s, f] = sum_scr[s, f] + before
    for k in range(n_tm):
        own = lax.rem(z - k + n_tm, n_tm)
        for f in range(frames):
            for i in range(n_mp):
                to = pl.ds(pl.multiple_of(lax.rem(m - i + n_mp, n_mp) * part, part), part)
                piece = sum_scr[own, f, i * part : (i + 1) * part, :]
                moved_refs[k][f, to, :] = piece.astype(jnp.bfloat16)
                if k == 0:
                    own_ref[f, to, :] = piece


def project(attn, weights, coef, dims, widths):
    n_tm, n_seq, n_mp, frames, part, cols = dims
    half = weights[0][0].shape[0]
    tok = n_mp * part
    rows = n_tm * frames * tok
    deep = n_seq * n_mp * cols
    vmem = pl.BlockSpec(memory_space=pltpu.VMEM)
    return pl.pallas_call(
        functools.partial(project_kernel, dims, widths),
        in_specs=[vmem] * (1 + len(widths) * n_tm * n_mp + n_seq * n_mp),
        out_specs=[vmem] * (1 + n_tm),
        scratch_shapes=[
            pltpu.VMEM((n_seq * n_mp, rows, cols), jnp.bfloat16),
            pltpu.VMEM((n_tm, frames, tok, half), jnp.float32),
        ],
        out_shape=[jax.ShapeDtypeStruct((frames, tok, half), jnp.float32)]
        + [jax.ShapeDtypeStruct((frames, tok, half), jnp.bfloat16)] * n_tm,
        cost_estimate=pl.CostEstimate(
            flops=2 * rows * deep * half, bytes_accessed=2 * (rows + half) * deep, transcendentals=0
        ),
        compiler_params=pltpu.CompilerParams(vmem_limit_bytes=24 << 20),
        name="project",
    )(coef, *[a for h in attn for k in h for a in k], *[w for j in weights for w in j])


def finish_kernel(n_tm, n_mp, *refs):
    out = refs[-1]
    z, m = lax.axis_index("tm"), lax.axis_index("mp")
    half = refs[0].shape[-1]
    slices = n_tm // n_mp
    for u in range(slices):
        k_here = lax.rem(m * slices + u - z + n_tm, n_tm)
        for h in range(n_mp):
            first = (u * n_mp + h) * half
            for k in range(n_tm):
                for l in range(n_mp):

                    @pl.when((k_here == k) & (lax.rem(m - h + n_mp, n_mp) == l))
                    def _():
                        out[:, :, first : first + half] = refs[k * n_mp + l][...].astype(
                            jnp.float32
                        )


def finish(blocks):
    n_tm, n_mp = len(blocks), len(blocks[0])
    frames, tok, half = blocks[0][0].shape
    vmem = pl.BlockSpec(memory_space=pltpu.VMEM)
    return pl.pallas_call(
        functools.partial(finish_kernel, n_tm, n_mp),
        in_specs=[vmem] * (n_tm * n_mp),
        out_specs=vmem,
        out_shape=jax.ShapeDtypeStruct((frames, tok, n_tm * half), jnp.float32),
        cost_estimate=pl.CostEstimate(
            flops=0, bytes_accessed=8 * frames * tok * n_tm * half, transcendentals=0
        ),
        compiler_params=pltpu.CompilerParams(vmem_limit_bytes=6 << 20),
        name="finish",
    )(*[b for k in blocks for b in k])


def sweep(states, start_step, w_qkv, qk_gain, w_out, time_proj):
    frames, tok, _ = states.shape
    n_tm, n_seq, n_mp = (lax.axis_size(name) for name in ("tm", "seq", "mp"))
    z = lax.axis_index("tm")
    part = tok // n_mp
    depth, cols = w_qkv.shape[1:]
    window = frames * n_tm

    raw = list(spread(states, n_tm, part))
    for k in range(1, n_tm):
        raw[k] = turn(raw[k], "tm", k)
    raw = jnp.stack(raw)
    sides = [raw]
    for j in range(1, n_seq):
        sides.append(turn(raw, "seq", j))
    rows = []
    for side in sides:
        rows.append([side] + [turn(side, "mp", i) for i in range(1, n_mp)])

    shares = list(time_shares(start_step, time_proj, n_tm, window))
    for k in range(1, n_tm):
        shares[k] = turn(shares[k], "tm", k)

    shares_out = load_out(w_out, n_mp)
    weights = [turn(share, "mp", i) if i else share for i, share in enumerate(shares_out)]
    weights = [weights]
    for j in range(1, n_seq):
        weights.append([turn(s, "seq", -j) for s in weights[0]])

    groups = head_groups(cols)
    hidden, coef, first_qkv = modulate(start_step, w_qkv, groups[:1], shares, rows)
    hidden = hidden.reshape(n_tm, n_seq * frames * tok, depth)
    proj = []
    for h, (lane, size) in enumerate(groups):
        part_qkv = w_qkv[:, :, lane : lane + size] if h else first_qkv
        proj.append(
            jnp.einsum(
                "krd,cdh->kcrh",
                hidden,
                part_qkv,
                preferred_element_type=jnp.float32,
            )
        )
    even = z % 2 == 0
    evens = [(i, i ^ 1) for i in range(n_tm)]
    odds = []
    for i in range(n_tm):
        for c in range(n_mp):
            other = i + 1 if i % 2 else i - 1
            inside = 0 <= other < n_tm
            to = other * n_mp + c if inside else i * n_mp + (c + 1) % n_mp
            odds.append((i * n_mp + c, to))

    def incoming(pair):
        first, second = (0.0 if p is None else p.astype(jnp.float32) for p in pair)
        right = jnp.where(z > 0, jnp.where(even, second, first), 0.0)
        return right, jnp.where(z < n_tm - 1, jnp.where(even, first, second), 0.0)

    flows = [(None, None)] * len(groups)
    for t in range(n_tm - 1):
        for h in range(len(groups)):
            right, left = proj[h][(t + 1) % n_tm], proj[h][n_tm - 1 - t]
            if t:
                more_right, more_left = incoming(flows[h])
                right, left = right + more_right, left + more_left
            first = jnp.where(even, right, left).astype(jnp.float16)
            second = jnp.where(even, left, right).astype(jnp.float16)
            first = lax.ppermute(first, "tm", evens)
            if t:
                second = lax.ppermute(second, ("tm", "mp"), odds)
                first, second = lax.optimization_barrier((first, second))
            flows[h] = (first, second if t else None)
    gathered = []
    for h, (lane, size) in enumerate(groups):
        right, left = incoming(flows[h])
        total = proj[h][0] + right + left
        total = total.reshape(3, n_seq, frames, tok, size)
        attn = attend(total, qk_gain[:, lane : lane + size])
        attn = jnp.stack([attn[0]] + [turn(attn[j], "seq", -j) for j in range(1, n_seq)])
        pieces = [attn]
        for k in range(1, n_tm):
            pieces.append(turn(attn, "tm", k))
        gathered.append([[g] + [turn(g, "mp", i) for i in range(1, n_mp)] for g in pieces])

    own, *moved = project(
        gathered, weights, coef, (n_tm, n_seq, n_mp, frames, part, cols), groups
    )
    blocks = []
    for k in range(n_tm):
        block = moved[0]
        if k:
            block = turn(moved[k], "tm", -k)
        others = [turn(block, "mp", i) for i in range(1, n_mp)]
        blocks.append([block if k else own] + others)
    return finish(blocks)


def solution(mesh):
    return jax.shard_map(
        sweep,
        mesh=mesh,
        in_specs=(
            P(("group", "tm"), "seq", None),
            P("group"),
            P(None, "tm", ("seq", "mp")),
            P(None, ("seq", "mp")),
            P("tm", ("seq", "mp")),
            P("tm", None),
        ),
        out_specs=P(("group", "tm"), "seq", "mp"),
        check_vma=False,
    )
```

```python
import functools

import jax
import jax.numpy as jnp
from jax import lax
from jax.experimental import pallas as pl
from jax.experimental.pallas import tpu as pltpu
from jax.sharding import PartitionSpec as P


HEAD_DIM = 128
FREQ = 256
STEPS = 100
LANES = 128
DMA_PIECES = 4


sample_shift = 5.0
norm_eps = 1e-06


def sigma_of(index):
    unit = 1.0 - index.astype(jnp.float32) / jnp.float32(STEPS)
    return sample_shift * unit / (1.0 + (sample_shift - 1.0) * unit)


def turn(block, axis, distance):
    size = lax.axis_size(axis)
    return lax.ppermute(block, axis, [(i, (i + distance) % size) for i in range(size)])


def head_norm(values, gain):
    meansq = jnp.mean(values * values, axis=-1, keepdims=True)
    return (values * lax.rsqrt(meansq + norm_eps) * gain).astype(jnp.bfloat16)


def head_groups(cols):
    heads = cols // HEAD_DIM
    first = (heads + 1) // 2 * HEAD_DIM
    return ((0, first), (first, cols - first)) if first < cols else ((0, cols),)


def attend_kernel(n_seq, heads, gain_ref, whole_ref, *outs):
    inv_root = 1.0 / jnp.sqrt(jnp.float32(HEAD_DIM))
    rows = whole_ref.shape[3]
    for h in range(heads):
        lanes = pl.ds(h * HEAD_DIM, HEAD_DIM)
        q, k, v = (
            jnp.concatenate([whole_ref[c, j, 0, :, lanes] for j in range(n_seq)], axis=0)
            for c in range(3)
        )
        q = head_norm(q, gain_ref[0:1, lanes])
        k = head_norm(k, gain_ref[1:2, lanes])
        scores = lax.dot_general(
            q, k, (((1,), (1,)), ((), ())), preferred_element_type=jnp.float32
        )
        expo = jnp.exp(scores * inv_root)
        probs = (expo / jnp.sum(expo, axis=-1, keepdims=True)).astype(jnp.bfloat16)
        attn = jnp.dot(
            probs, v.astype(jnp.bfloat16), preferred_element_type=jnp.float32
        ).astype(jnp.bfloat16)
        for j, out in enumerate(outs):
            out[0, :, lanes] = attn[j * rows : (j + 1) * rows]


def attend(whole, gain):
    _, n_seq, frames, rows, cols = whole.shape
    heads = cols // HEAD_DIM
    tokens = rows * n_seq
    out = jax.ShapeDtypeStruct((frames, rows, cols), jnp.bfloat16)
    return pl.pallas_call(
        functools.partial(attend_kernel, n_seq, heads),
        grid=(frames,),
        in_specs=[
            pl.BlockSpec((2, cols), lambda f: (0, 0)),
            pl.BlockSpec((3, n_seq, 1, rows, cols), lambda f: (0, 0, f, 0, 0)),
        ],
        out_specs=[pl.BlockSpec((1, rows, cols), lambda f: (f, 0, 0))] * n_seq,
        out_shape=[out] * n_seq,
        cost_estimate=pl.CostEstimate(
            flops=4 * frames * heads * tokens * tokens * HEAD_DIM,
            bytes_accessed=14 * frames * tokens * cols,
            transcendentals=frames * heads * tokens * tokens,
        ),
        compiler_params=pltpu.CompilerParams(vmem_limit_bytes=6 << 20),
        name="attend",
    )(gain, whole)


def spread_kernel(n_tm, states_ref, *outs):
    z, m = lax.axis_index("tm"), lax.axis_index("mp")
    frames, _, width = states_ref.shape
    part, depth = outs[0].shape[1], width // n_tm
    own = pl.ds(pl.multiple_of(m * part, part), part)
    lane = lax.broadcasted_iota(jnp.int32, (part, LANES), 1)
    for f in range(frames):
        field = states_ref[f, own, :].astype(jnp.float32)
        mean = jnp.mean(field, axis=-1, keepdims=True)
        centred = field - mean
        var = jnp.mean(centred * centred, axis=-1, keepdims=True)
        tail = jnp.zeros((part, LANES), jnp.float32)
        for place, rest in enumerate((mean, lax.rsqrt(var + norm_eps))):
            for term in range(3):
                cut = rest.astype(jnp.bfloat16).astype(jnp.float32)
                tail = jnp.where(lane == 3 * place + term, cut, tail)
                rest = rest - cut
        tail = tail.astype(jnp.bfloat16)
        for k, out in enumerate(outs):
            out[f, :, depth:] = tail
            for s in range(n_tm):

                @pl.when(lax.rem(z + k, n_tm) == s)
                def _():
                    out[f, :, :depth] = states_ref[f, own, s * depth : (s + 1) * depth]


def spread(states, n_tm, part):
    frames, _, width = states.shape
    out = jax.ShapeDtypeStruct((frames, part, width // n_tm + LANES), jnp.bfloat16)
    return pl.pallas_call(
        functools.partial(spread_kernel, n_tm),
        in_specs=[pl.BlockSpec(memory_space=pltpu.VMEM)],
        out_specs=[pl.BlockSpec(memory_space=pltpu.VMEM)] * n_tm,
        out_shape=[out] * n_tm,
        cost_estimate=pl.CostEstimate(
            flops=10 * part * width, bytes_accessed=4 * part * width, transcendentals=0
        ),
        compiler_params=pltpu.CompilerParams(vmem_limit_bytes=4 << 20),
        name="spread",
    )(states)


def time_kernel(n_tm, step_ref, proj_ref, *outs):
    z = lax.axis_index("tm")
    freq_rows, wide = proj_ref.shape
    window, depth = outs[0].shape[1:]
    half_freq = FREQ // 2
    index = step_ref[0] + lax.broadcasted_iota(jnp.int32, (window, freq_rows), 0)
    feature = z * freq_rows + lax.broadcasted_iota(jnp.int32, (window, freq_rows), 1)
    late = feature >= half_freq
    rank = jnp.where(late, feature - half_freq, feature).astype(jnp.float32)
    freqs = jnp.exp(-jnp.log(jnp.float32(10000.0)) * rank / jnp.float32(half_freq))
    angles = (1000.0 * sigma_of(index)) * freqs
    emb = jnp.where(late, jnp.sin(angles), jnp.cos(angles)).astype(jnp.bfloat16)
    for k, out in enumerate(outs):
        for s in range(n_tm):

            @pl.when(lax.rem(z + k, n_tm) == s)
            def _():
                for c in range(3):
                    first = c * (wide // 3) + s * depth
                    out[c] = jnp.dot(
                        emb, proj_ref[:, first : first + depth], preferred_element_type=jnp.float32
                    )


def time_shares(start_step, time_proj, n_tm, window):
    freq_rows, wide = time_proj.shape
    out = jax.ShapeDtypeStruct((3, window, wide // (3 * n_tm)), jnp.float32)
    smem, vmem = (pl.BlockSpec(memory_space=space) for space in (pltpu.SMEM, pltpu.VMEM))
    return pl.pallas_call(
        functools.partial(time_kernel, n_tm),
        in_specs=[smem, vmem],
        out_specs=[vmem] * n_tm,
        out_shape=[out] * n_tm,
        cost_estimate=pl.CostEstimate(
            flops=2 * window * freq_rows * wide, bytes_accessed=2 * freq_rows * wide, transcendentals=0
        ),
        compiler_params=pltpu.CompilerParams(vmem_limit_bytes=6 << 20),
        name="time_shares",
    )(start_step, time_proj)


def load_kernel(n_mp, w_ref, *refs):
    outs, sems = refs[:-1], refs[-1]
    copies = []
    for i, out in enumerate(outs):
        rows = out.shape[0]
        share = lax.rem(lax.axis_index("mp") + i, n_mp)
        source = w_ref.at[pl.ds(pl.multiple_of(share * rows, rows), rows)]
        copies.append(pltpu.make_async_copy(source, out, sems.at[i]))
    for copy in copies:
        copy.start()
    for copy in copies:
        copy.wait()


def load_out(weights, n_mp):
    share = jax.ShapeDtypeStruct((weights.shape[0] // n_mp, weights.shape[1]), weights.dtype)
    return pl.pallas_call(
        functools.partial(load_kernel, n_mp),
        in_specs=[pl.BlockSpec(memory_space=pltpu.HBM)],
        out_specs=[pl.BlockSpec(memory_space=pltpu.VMEM)] * n_mp,
        out_shape=[share] * n_mp,
        scratch_shapes=[pltpu.SemaphoreType.DMA((n_mp,))],
        cost_estimate=pl.CostEstimate(flops=0, bytes_accessed=2 * weights.size, transcendentals=0),
        compiler_params=pltpu.CompilerParams(vmem_limit_bytes=8 << 20),
        name="load_out",
    )(weights)


def modulate_kernel(n_tm, n_seq, n_mp, cuts, step_ref, w_ref, *refs):
    sides = n_seq * n_mp
    shares, near, far = refs[:n_tm], refs[n_tm : n_tm + sides], refs[n_tm + sides :][:sides]
    hidden_ref, coef_ref, *w_outs, mod_scr, sems = refs[n_tm + 2 * sides :]
    stride = w_ref.shape[1] // DMA_PIECES
    copies = []
    for (lane, size), out in zip(cuts, w_outs):
        for c in range(w_ref.shape[0]):
            for piece in range(DMA_PIECES):
                rows_here = pl.ds(piece * stride, stride)
                copies.append(
                    pltpu.make_async_copy(
                        w_ref.at[c, rows_here, pl.ds(lane, size)],
                        out.at[c, rows_here],
                        sems.at[len(copies)],
                    )
                )
    z, k = lax.axis_index("tm"), pl.program_id(0)
    frames, part, wide = near[0].shape
    depth = wide - LANES

    @pl.when(k == 0)
    def _():
        for copy in copies:
            copy.start()
        total = shares[0][...]
        for share in shares[1:]:
            total = total + share[...]
        mod_scr[...] = total

    for f in range(frames):
        step = lax.rem(z - k + n_tm, n_tm) * frames + f
        shift, scale, gate = (mod_scr[c, pl.ds(step, 1), :] for c in range(3))
        index = jnp.full((1, depth), step_ref[0] + step, jnp.int32)
        coef_ref[0, f : f + 1, :] = (sigma_of(index + 1) - sigma_of(index)) * gate

        def modulated(block):
            tail = block[:, depth:].astype(jnp.float32)
            mean = tail[:, 0:1] + tail[:, 1:2] + tail[:, 2:3]
            rstd = tail[:, 3:4] + tail[:, 4:5] + tail[:, 5:6]
            normed = (block[:, :depth].astype(jnp.float32) - mean) * rstd
            return (normed * (1.0 + scale) + shift).astype(jnp.bfloat16)

        for j in range(n_seq):
            for i in range(n_mp):
                to = slice(i * part, (i + 1) * part)

                @pl.when(k == 0)
                def _():
                    hidden_ref[0, j, f, to, :] = modulated(near[j * n_mp + i][f])

                @pl.when(k > 0)
                def _():
                    hidden_ref[0, j, f, to, :] = modulated(far[j * n_mp + i][0, f])

    @pl.when(k == n_tm - 1)
    def _():
        for copy in copies:
            copy.wait()


def modulate(start_step, w_qkv, cuts, shares, near, far):
    n_tm, n_seq, n_mp = len(shares), len(near), len(near[0])
    frames, part, wide = near[0][0].shape
    three = w_qkv.shape[0]
    depth = wide - LANES
    window = shares[0].shape[1]
    shape = (n_tm, n_seq, frames, n_mp * part, depth)
    return pl.pallas_call(
        functools.partial(modulate_kernel, n_tm, n_seq, n_mp, cuts),
        grid=(n_tm,),
        in_specs=[pl.BlockSpec(memory_space=pltpu.SMEM), pl.BlockSpec(memory_space=pltpu.HBM)]
        + [pl.BlockSpec((3, window, depth), lambda k: (0, 0, 0))] * n_tm
        + [pl.BlockSpec((frames, part, wide), lambda k: (0, 0, 0))] * (n_seq * n_mp)
        + [pl.BlockSpec((1, frames, part, wide), lambda k: (jnp.maximum(k - 1, 0), 0, 0, 0))]
        * (n_seq * n_mp),
        out_specs=[
            pl.BlockSpec((1,) + shape[1:], lambda k: (k, 0, 0, 0, 0)),
            pl.BlockSpec((1, frames, depth), lambda k: (k, 0, 0)),
        ]
        + [pl.BlockSpec(memory_space=pl.ANY)] * len(cuts),
        scratch_shapes=[
            pltpu.VMEM((3, window, depth), jnp.float32),
            pltpu.SemaphoreType.DMA((len(cuts) * three * DMA_PIECES,)),
        ],
        out_shape=[
            jax.ShapeDtypeStruct(shape, jnp.bfloat16),
            jax.ShapeDtypeStruct((n_tm, frames, depth), jnp.float32),
        ]
        + [jax.ShapeDtypeStruct(w_qkv.shape[:2] + (size,), w_qkv.dtype) for _, size in cuts],
        cost_estimate=pl.CostEstimate(
            flops=4 * n_tm * n_seq * frames * n_mp * part * depth,
            bytes_accessed=4 * n_tm * n_seq * frames * n_mp * part * depth,
            transcendentals=0,
        ),
        compiler_params=pltpu.CompilerParams(vmem_limit_bytes=42 << 20),
        name="modulate",
    )(start_step, w_qkv, *shares, *[r for rows in (near, far) for side in rows for r in side])


def project_kernel(dims, widths, coef_ref, *refs):
    n_tm, n_seq, n_mp, frames, part, _ = dims
    n_attn = len(widths) * n_tm * n_mp
    attn_refs = refs[:n_attn]
    w_refs = refs[n_attn : n_attn + n_seq * n_mp]
    outs = refs[n_attn + n_seq * n_mp :]
    own_ref, moved_refs, (rows_scr, sum_scr) = outs[0], outs[1:-2], outs[-2:]
    z, m = lax.axis_index("tm"), lax.axis_index("mp")
    block = n_mp * part
    per = frames * block
    half = own_ref.shape[-1]
    total = None
    for j in range(n_seq):
        for l in range(n_mp):
            at = j * n_mp + l
            for k in range(n_tm):
                for f in range(frames):
                    for i in range(n_mp):
                        first = k * per + f * block + i * part
                        source = (i - l) % n_mp * part
                        for h, (lane, width) in enumerate(widths):
                            piece = attn_refs[(h * n_tm + k) * n_mp + l]
                            rows_scr[at, first : first + part, lane : lane + width] = piece[
                                j, f, source : source + part, :
                            ]
            product = lax.dot_general(
                rows_scr[at],
                w_refs[at][...],
                (((1,), (1,)), ((), ())),
                preferred_element_type=jnp.float32,
            )
            total = product if total is None else total + product
    for k in range(n_tm):
        for f in range(frames):
            first = k * per + f * block
            factor = coef_ref[k, f : f + 1, :half]
            for mm in range(1, n_mp):
                other = coef_ref[k, f : f + 1, mm * half : (mm + 1) * half]
                factor = jnp.where(m == mm, other, factor)
            drift = total[first : first + block] * factor
            sum_scr[lax.rem(z - k + n_tm, n_tm), f] = drift
    for s in range(n_tm):
        for f in range(frames):
            if s or f:
                before = sum_scr[s, f - 1] if f else sum_scr[s - 1, frames - 1]
                sum_scr[s, f] = sum_scr[s, f] + before
    for k in range(n_tm):
        own = lax.rem(z - k + n_tm, n_tm)
        for f in range(frames):
            for i in range(n_mp):
                to = pl.ds(pl.multiple_of(lax.rem(m - i + n_mp, n_mp) * part, part), part)
                piece = sum_scr[own, f, i * part : (i + 1) * part, :]
                moved_refs[k][f, to, :] = piece.astype(jnp.bfloat16)
                if k == 0:
                    own_ref[f, to, :] = piece


def project(attn, weights, coef, dims, widths):
    n_tm, n_seq, n_mp, frames, part, cols = dims
    half = weights[0][0].shape[0]
    tok = n_mp * part
    rows = n_tm * frames * tok
    deep = n_seq * n_mp * cols
    vmem = pl.BlockSpec(memory_space=pltpu.VMEM)
    return pl.pallas_call(
        functools.partial(project_kernel, dims, widths),
        in_specs=[vmem] * (1 + len(widths) * n_tm * n_mp + n_seq * n_mp),
        out_specs=[vmem] * (1 + n_tm),
        scratch_shapes=[
            pltpu.VMEM((n_seq * n_mp, rows, cols), jnp.bfloat16),
            pltpu.VMEM((n_tm, frames, tok, half), jnp.float32),
        ],
        out_shape=[jax.ShapeDtypeStruct((frames, tok, half), jnp.float32)]
        + [jax.ShapeDtypeStruct((frames, tok, half), jnp.bfloat16)] * n_tm,
        cost_estimate=pl.CostEstimate(
            flops=2 * rows * deep * half, bytes_accessed=2 * (rows + half) * deep, transcendentals=0
        ),
        compiler_params=pltpu.CompilerParams(vmem_limit_bytes=24 << 20),
        name="project",
    )(coef, *[a for h in attn for k in h for a in k], *[w for j in weights for w in j])


def finish_kernel(n_tm, n_mp, *refs):
    out = refs[-1]
    z, m = lax.axis_index("tm"), lax.axis_index("mp")
    half = refs[0].shape[-1]
    slices = n_tm // n_mp
    for u in range(slices):
        k_here = lax.rem(m * slices + u - z + n_tm, n_tm)
        for h in range(n_mp):
            first = (u * n_mp + h) * half
            for k in range(n_tm):
                for l in range(n_mp):

                    @pl.when((k_here == k) & (lax.rem(m - h + n_mp, n_mp) == l))
                    def _():
                        out[:, :, first : first + half] = refs[k * n_mp + l][...].astype(
                            jnp.float32
                        )


def finish(blocks):
    n_tm, n_mp = len(blocks), len(blocks[0])
    frames, tok, half = blocks[0][0].shape
    vmem = pl.BlockSpec(memory_space=pltpu.VMEM)
    return pl.pallas_call(
        functools.partial(finish_kernel, n_tm, n_mp),
        in_specs=[vmem] * (n_tm * n_mp),
        out_specs=vmem,
        out_shape=jax.ShapeDtypeStruct((frames, tok, n_tm * half), jnp.float32),
        cost_estimate=pl.CostEstimate(
            flops=0, bytes_accessed=8 * frames * tok * n_tm * half, transcendentals=0
        ),
        compiler_params=pltpu.CompilerParams(vmem_limit_bytes=6 << 20),
        name="finish",
    )(*[b for k in blocks for b in k])


def sweep(states, start_step, w_qkv, qk_gain, w_out, time_proj):
    frames, tok, _ = states.shape
    n_tm, n_seq, n_mp = (lax.axis_size(name) for name in ("tm", "seq", "mp"))
    z = lax.axis_index("tm")
    part = tok // n_mp
    depth, cols = w_qkv.shape[1:]
    window = frames * n_tm

    raw = list(spread(states, n_tm, part))
    for k in range(1, n_tm):
        raw[k] = turn(raw[k], "tm", k)
    near, far = [], []
    for blocks, kept in ((raw[0], near), (jnp.stack(raw[1:]), far)):
        for j in range(n_seq):
            side = turn(blocks, "seq", j) if j else blocks
            kept.append([side] + [turn(side, "mp", i) for i in range(1, n_mp)])

    shares = list(time_shares(start_step, time_proj, n_tm, window))
    for k in range(1, n_tm):
        shares[k] = turn(shares[k], "tm", k)

    shares_out = load_out(w_out, n_mp)
    weights = [turn(share, "mp", i) if i else share for i, share in enumerate(shares_out)]
    weights = [weights]
    for j in range(1, n_seq):
        weights.append([])
        for share in weights[0]:
            weights[j].append(turn(share, "seq", -j))

    groups = head_groups(cols)
    hidden, coef, *parts_qkv = modulate(start_step, w_qkv, groups, shares, near, far)
    hidden = hidden.reshape(n_tm, n_seq * frames * tok, depth)
    proj = []
    for part_qkv in parts_qkv:
        proj.append(
            jnp.einsum(
                "krd,cdh->kcrh",
                hidden,
                part_qkv,
                preferred_element_type=jnp.float32,
            )
        )
    even = z % 2 == 0
    evens = [(i, i ^ 1) for i in range(n_tm)]
    odds = []
    for i in range(n_tm):
        for c in range(n_mp):
            other = i + 1 if i % 2 else i - 1
            inside = 0 <= other < n_tm
            to = other * n_mp + c if inside else i * n_mp + (c + 1) % n_mp
            odds.append((i * n_mp + c, to))

    def incoming(pair):
        first, second = (0.0 if p is None else p.astype(jnp.float32) for p in pair)
        right = jnp.where(z > 0, jnp.where(even, second, first), 0.0)
        return right, jnp.where(z < n_tm - 1, jnp.where(even, first, second), 0.0)

    flows = [(None, None)] * len(groups)
    for t in range(n_tm - 1):
        for h in range(len(groups)):
            right, left = proj[h][(t + 1) % n_tm], proj[h][n_tm - 1 - t]
            if t:
                more_right, more_left = incoming(flows[h])
                right, left = right + more_right, left + more_left
            first = jnp.where(even, right, left).astype(jnp.float16)
            second = jnp.where(even, left, right).astype(jnp.float16)
            first = lax.ppermute(first, "tm", evens)
            if t:
                second = lax.ppermute(second, ("tm", "mp"), odds)
                first, second = lax.optimization_barrier((first, second))
            flows[h] = (first, second if t else None)
    gathered = []
    for h, (lane, size) in enumerate(groups):
        right, left = incoming(flows[h])
        total = proj[h][0] + right + left
        total = total.reshape(3, n_seq, frames, tok, size)
        attn = attend(total, qk_gain[:, lane : lane + size])
        attn = jnp.stack([attn[0]] + [turn(attn[j], "seq", -j) for j in range(1, n_seq)])
        pieces = [attn]
        for k in range(1, n_tm):
            pieces.append(turn(attn, "tm", k))
        gathered.append([[g] + [turn(g, "mp", i) for i in range(1, n_mp)] for g in pieces])

    own, *moved = project(
        gathered, weights, coef, (n_tm, n_seq, n_mp, frames, part, cols), groups
    )
    blocks = []
    for k in range(n_tm):
        block = moved[0]
        if k:
            block = turn(moved[k], "tm", -k)
        others = [turn(block, "mp", i) for i in range(1, n_mp)]
        blocks.append([block if k else own] + others)
    return finish(blocks)


def solution(mesh):
    return jax.shard_map(
        sweep,
        mesh=mesh,
        in_specs=(
            P(("group", "tm"), "seq", None),
            P("group"),
            P(None, "tm", ("seq", "mp")),
            P(None, ("seq", "mp")),
            P("tm", ("seq", "mp")),
            P("tm", None),
        ),
        out_specs=P(("group", "tm"), "seq", "mp"),
        check_vma=False,
    )
```

```python
import functools

import jax
import jax.numpy as jnp
from jax import lax
from jax.experimental import pallas as pl
from jax.experimental.pallas import tpu as pltpu
from jax.sharding import PartitionSpec as P


HEAD_DIM = 128
FREQ = 256
STEPS = 100
LANES = 128
DMA_PIECES = 4


sample_shift = 5.0
norm_eps = 1e-06


def sigma_of(index):
    unit = 1.0 - index.astype(jnp.float32) / jnp.float32(STEPS)
    return sample_shift * unit / (1.0 + (sample_shift - 1.0) * unit)


def turn(block, axis, distance):
    size = lax.axis_size(axis)
    return lax.ppermute(block, axis, [(i, (i + distance) % size) for i in range(size)])


def head_norm(values, gain):
    meansq = jnp.mean(values * values, axis=-1, keepdims=True)
    return (values * lax.rsqrt(meansq + norm_eps) * gain).astype(jnp.bfloat16)


def head_groups(cols):
    heads = cols // HEAD_DIM
    first = (heads + 1) // 2 * HEAD_DIM
    return ((0, first), (first, cols - first)) if first < cols else ((0, cols),)


def attend_kernel(n_seq, heads, gain_ref, whole_ref, *outs):
    inv_root = 1.0 / jnp.sqrt(jnp.float32(HEAD_DIM))
    rows = whole_ref.shape[3]
    for h in range(heads):
        lanes = pl.ds(h * HEAD_DIM, HEAD_DIM)
        q, k, v = (
            jnp.concatenate([whole_ref[c, j, 0, :, lanes] for j in range(n_seq)], axis=0)
            for c in range(3)
        )
        q = head_norm(q, gain_ref[0:1, lanes])
        k = head_norm(k, gain_ref[1:2, lanes])
        scores = lax.dot_general(
            q, k, (((1,), (1,)), ((), ())), preferred_element_type=jnp.float32
        )
        expo = jnp.exp(scores * inv_root)
        probs = (expo / jnp.sum(expo, axis=-1, keepdims=True)).astype(jnp.bfloat16)
        attn = jnp.dot(
            probs, v.astype(jnp.bfloat16), preferred_element_type=jnp.float32
        ).astype(jnp.bfloat16)
        for j, out in enumerate(outs):
            out[0, :, lanes] = attn[j * rows : (j + 1) * rows]


def attend(whole, gain):
    _, n_seq, frames, rows, cols = whole.shape
    heads = cols // HEAD_DIM
    tokens = rows * n_seq
    out = jax.ShapeDtypeStruct((frames, rows, cols), jnp.bfloat16)
    return pl.pallas_call(
        functools.partial(attend_kernel, n_seq, heads),
        grid=(frames,),
        in_specs=[
            pl.BlockSpec((2, cols), lambda f: (0, 0)),
            pl.BlockSpec((3, n_seq, 1, rows, cols), lambda f: (0, 0, f, 0, 0)),
        ],
        out_specs=[pl.BlockSpec((1, rows, cols), lambda f: (f, 0, 0))] * n_seq,
        out_shape=[out] * n_seq,
        cost_estimate=pl.CostEstimate(
            flops=4 * frames * heads * tokens * tokens * HEAD_DIM,
            bytes_accessed=14 * frames * tokens * cols,
            transcendentals=frames * heads * tokens * tokens,
        ),
        compiler_params=pltpu.CompilerParams(vmem_limit_bytes=6 << 20),
        name="attend",
    )(gain, whole)


def spread_kernel(n_tm, states_ref, *outs):
    z, m = lax.axis_index("tm"), lax.axis_index("mp")
    frames, _, width = states_ref.shape
    part, depth = outs[0].shape[1], width // n_tm
    own = pl.ds(pl.multiple_of(m * part, part), part)
    lane = lax.broadcasted_iota(jnp.int32, (part, LANES), 1)
    for f in range(frames):
        field = states_ref[f, own, :].astype(jnp.float32)
        mean = jnp.mean(field, axis=-1, keepdims=True)
        centred = field - mean
        var = jnp.mean(centred * centred, axis=-1, keepdims=True)
        tail = jnp.zeros((part, LANES), jnp.float32)
        for place, rest in enumerate((mean, lax.rsqrt(var + norm_eps))):
            for term in range(3):
                cut = rest.astype(jnp.bfloat16).astype(jnp.float32)
                tail = jnp.where(lane == 3 * place + term, cut, tail)
                rest = rest - cut
        tail = tail.astype(jnp.bfloat16)
        for k, out in enumerate(outs):
            out[f, :, depth:] = tail
            for s in range(n_tm):

                @pl.when(lax.rem(z + k, n_tm) == s)
                def _():
                    out[f, :, :depth] = states_ref[f, own, s * depth : (s + 1) * depth]


def spread(states, n_tm, part):
    frames, _, width = states.shape
    out = jax.ShapeDtypeStruct((frames, part, width // n_tm + LANES), jnp.bfloat16)
    return pl.pallas_call(
        functools.partial(spread_kernel, n_tm),
        in_specs=[pl.BlockSpec(memory_space=pltpu.VMEM)],
        out_specs=[pl.BlockSpec(memory_space=pltpu.VMEM)] * n_tm,
        out_shape=[out] * n_tm,
        cost_estimate=pl.CostEstimate(
            flops=10 * part * width, bytes_accessed=4 * part * width, transcendentals=0
        ),
        compiler_params=pltpu.CompilerParams(vmem_limit_bytes=4 << 20),
        name="spread",
    )(states)


def time_kernel(n_tm, step_ref, proj_ref, *outs):
    z = lax.axis_index("tm")
    freq_rows, wide = proj_ref.shape
    window, depth = outs[0].shape[1:]
    half_freq = FREQ // 2
    index = step_ref[0] + lax.broadcasted_iota(jnp.int32, (window, freq_rows), 0)
    feature = z * freq_rows + lax.broadcasted_iota(jnp.int32, (window, freq_rows), 1)
    late = feature >= half_freq
    rank = jnp.where(late, feature - half_freq, feature).astype(jnp.float32)
    freqs = jnp.exp(-jnp.log(jnp.float32(10000.0)) * rank / jnp.float32(half_freq))
    angles = (1000.0 * sigma_of(index)) * freqs
    emb = jnp.where(late, jnp.sin(angles), jnp.cos(angles)).astype(jnp.bfloat16)
    for k, out in enumerate(outs):
        for s in range(n_tm):

            @pl.when(lax.rem(z + k, n_tm) == s)
            def _():
                for c in range(3):
                    first = c * (wide // 3) + s * depth
                    out[c] = jnp.dot(
                        emb, proj_ref[:, first : first + depth], preferred_element_type=jnp.float32
                    )


def time_shares(start_step, time_proj, n_tm, window):
    freq_rows, wide = time_proj.shape
    out = jax.ShapeDtypeStruct((3, window, wide // (3 * n_tm)), jnp.float32)
    smem, vmem = (pl.BlockSpec(memory_space=space) for space in (pltpu.SMEM, pltpu.VMEM))
    return pl.pallas_call(
        functools.partial(time_kernel, n_tm),
        in_specs=[smem, vmem],
        out_specs=[vmem] * n_tm,
        out_shape=[out] * n_tm,
        cost_estimate=pl.CostEstimate(
            flops=2 * window * freq_rows * wide, bytes_accessed=2 * freq_rows * wide, transcendentals=0
        ),
        compiler_params=pltpu.CompilerParams(vmem_limit_bytes=6 << 20),
        name="time_shares",
    )(start_step, time_proj)


def load_kernel(n_mp, w_ref, *refs):
    outs, sems = refs[:-1], refs[-1]
    copies = []
    for i, out in enumerate(outs):
        rows = out.shape[0]
        share = lax.rem(lax.axis_index("mp") + i, n_mp)
        source = w_ref.at[pl.ds(pl.multiple_of(share * rows, rows), rows)]
        copies.append(pltpu.make_async_copy(source, out, sems.at[i]))
    for copy in copies:
        copy.start()
    for copy in copies:
        copy.wait()


def load_out(weights, n_mp):
    share = jax.ShapeDtypeStruct((weights.shape[0] // n_mp, weights.shape[1]), weights.dtype)
    return pl.pallas_call(
        functools.partial(load_kernel, n_mp),
        in_specs=[pl.BlockSpec(memory_space=pltpu.HBM)],
        out_specs=[pl.BlockSpec(memory_space=pltpu.VMEM)] * n_mp,
        out_shape=[share] * n_mp,
        scratch_shapes=[pltpu.SemaphoreType.DMA((n_mp,))],
        cost_estimate=pl.CostEstimate(flops=0, bytes_accessed=2 * weights.size, transcendentals=0),
        compiler_params=pltpu.CompilerParams(vmem_limit_bytes=8 << 20),
        name="load_out",
    )(weights)


def modulate_kernel(n_tm, n_seq, n_mp, step_ref, w_ref, *refs):
    sides = n_seq * n_mp
    shares, near, far = refs[:n_tm], refs[n_tm : n_tm + sides], refs[n_tm + sides :][:sides]
    hidden_ref, coef_ref, w_out, mod_scr, sems = refs[n_tm + 2 * sides :]
    stride = w_ref.shape[1] // DMA_PIECES
    copies = []
    for c in range(w_ref.shape[0]):
        for piece in range(DMA_PIECES):
            at = c, pl.ds(piece * stride, stride)
            copies.append(
                pltpu.make_async_copy(w_ref.at[at], w_out.at[at], sems.at[len(copies)])
            )
    z, k = lax.axis_index("tm"), pl.program_id(0)
    frames, part, wide = near[0].shape
    depth = wide - LANES

    @pl.when(k == 0)
    def _():
        for copy in copies:
            copy.start()
        total = shares[0][...]
        for share in shares[1:]:
            total = total + share[...]
        mod_scr[...] = total

    for f in range(frames):
        step = lax.rem(z - k + n_tm, n_tm) * frames + f
        shift, scale, gate = (mod_scr[c, pl.ds(step, 1), :] for c in range(3))
        index = jnp.full((1, depth), step_ref[0] + step, jnp.int32)
        coef_ref[0, f : f + 1, :] = (sigma_of(index + 1) - sigma_of(index)) * gate

        def modulated(block):
            tail = block[:, depth:].astype(jnp.float32)
            mean = tail[:, 0:1] + tail[:, 1:2] + tail[:, 2:3]
            rstd = tail[:, 3:4] + tail[:, 4:5] + tail[:, 5:6]
            normed = (block[:, :depth].astype(jnp.float32) - mean) * rstd
            return (normed * (1.0 + scale) + shift).astype(jnp.bfloat16)

        for j in range(n_seq):
            for i in range(n_mp):
                to = slice(i * part, (i + 1) * part)

                @pl.when(k == 0)
                def _():
                    hidden_ref[0, j, f, to, :] = modulated(near[j * n_mp + i][f])

                @pl.when(k > 0)
                def _():
                    hidden_ref[0, j, f, to, :] = modulated(far[j * n_mp + i][0, f])

    @pl.when(k == n_tm - 1)
    def _():
        for copy in copies:
            copy.wait()


def modulate(start_step, w_qkv, shares, near, far):
    n_tm, n_seq, n_mp = len(shares), len(near), len(near[0])
    frames, part, wide = near[0][0].shape
    three = w_qkv.shape[0]
    depth = wide - LANES
    window = shares[0].shape[1]
    shape = (n_tm, n_seq, frames, n_mp * part, depth)
    return pl.pallas_call(
        functools.partial(modulate_kernel, n_tm, n_seq, n_mp),
        grid=(n_tm,),
        in_specs=[pl.BlockSpec(memory_space=pltpu.SMEM), pl.BlockSpec(memory_space=pltpu.HBM)]
        + [pl.BlockSpec((3, window, depth), lambda k: (0, 0, 0))] * n_tm
        + [pl.BlockSpec((frames, part, wide), lambda k: (0, 0, 0))] * (n_seq * n_mp)
        + [pl.BlockSpec((1, frames, part, wide), lambda k: (jnp.maximum(k - 1, 0), 0, 0, 0))]
        * (n_seq * n_mp),
        out_specs=[
            pl.BlockSpec((1,) + shape[1:], lambda k: (k, 0, 0, 0, 0)),
            pl.BlockSpec((1, frames, depth), lambda k: (k, 0, 0)),
        ]
        + [pl.BlockSpec(memory_space=pl.ANY)],
        scratch_shapes=[
            pltpu.VMEM((3, window, depth), jnp.float32),
            pltpu.SemaphoreType.DMA((three * DMA_PIECES,)),
        ],
        out_shape=[
            jax.ShapeDtypeStruct(shape, jnp.bfloat16),
            jax.ShapeDtypeStruct((n_tm, frames, depth), jnp.float32),
        ]
        + [jax.ShapeDtypeStruct(w_qkv.shape, w_qkv.dtype)],
        cost_estimate=pl.CostEstimate(
            flops=4 * n_tm * n_seq * frames * n_mp * part * depth,
            bytes_accessed=4 * n_tm * n_seq * frames * n_mp * part * depth,
            transcendentals=0,
        ),
        compiler_params=pltpu.CompilerParams(vmem_limit_bytes=42 << 20),
        name="modulate",
    )(start_step, w_qkv, *shares, *[r for rows in (near, far) for side in rows for r in side])


def project_kernel(dims, widths, coef_ref, *refs):
    n_tm, n_seq, n_mp, frames, part, _ = dims
    n_attn = len(widths) * n_tm * n_mp
    attn_refs = refs[:n_attn]
    w_refs = refs[n_attn : n_attn + n_seq * n_mp]
    outs = refs[n_attn + n_seq * n_mp :]
    own_ref, moved_refs, (rows_scr, sum_scr) = outs[0], outs[1:-2], outs[-2:]
    z, m = lax.axis_index("tm"), lax.axis_index("mp")
    block = n_mp * part
    per = frames * block
    half = own_ref.shape[-1]
    total = None
    for j in range(n_seq):
        for l in range(n_mp):
            at = j * n_mp + l
            for k in range(n_tm):
                for f in range(frames):
                    for i in range(n_mp):
                        first = k * per + f * block + i * part
                        source = (i - l) % n_mp * part
                        for h, (lane, width) in enumerate(widths):
                            piece = attn_refs[(h * n_tm + k) * n_mp + l]
                            rows_scr[at, first : first + part, lane : lane + width] = piece[
                                j, f, source : source + part, :
                            ]
            product = lax.dot_general(
                rows_scr[at],
                w_refs[at][...],
                (((1,), (1,)), ((), ())),
                preferred_element_type=jnp.float32,
            )
            total = product if total is None else total + product
    for k in range(n_tm):
        for f in range(frames):
            first = k * per + f * block
            factor = coef_ref[k, f : f + 1, :half]
            for mm in range(1, n_mp):
                other = coef_ref[k, f : f + 1, mm * half : (mm + 1) * half]
                factor = jnp.where(m == mm, other, factor)
            drift = total[first : first + block] * factor
            sum_scr[lax.rem(z - k + n_tm, n_tm), f] = drift
    for s in range(n_tm):
        for f in range(frames):
            if s or f:
                before = sum_scr[s, f - 1] if f else sum_scr[s - 1, frames - 1]
                sum_scr[s, f] = sum_scr[s, f] + before
    for k in range(n_tm):
        own = lax.rem(z - k + n_tm, n_tm)
        for f in range(frames):
            for i in range(n_mp):
                to = pl.ds(pl.multiple_of(lax.rem(m - i + n_mp, n_mp) * part, part), part)
                piece = sum_scr[own, f, i * part : (i + 1) * part, :]
                moved_refs[k][f, to, :] = piece.astype(jnp.bfloat16)
                if k == 0:
                    own_ref[f, to, :] = piece


def project(attn, weights, coef, dims, widths):
    n_tm, n_seq, n_mp, frames, part, cols = dims
    half = weights[0][0].shape[0]
    tok = n_mp * part
    rows = n_tm * frames * tok
    deep = n_seq * n_mp * cols
    vmem = pl.BlockSpec(memory_space=pltpu.VMEM)
    return pl.pallas_call(
        functools.partial(project_kernel, dims, widths),
        in_specs=[vmem] * (1 + len(widths) * n_tm * n_mp + n_seq * n_mp),
        out_specs=[vmem] * (1 + n_tm),
        scratch_shapes=[
            pltpu.VMEM((n_seq * n_mp, rows, cols), jnp.bfloat16),
            pltpu.VMEM((n_tm, frames, tok, half), jnp.float32),
        ],
        out_shape=[jax.ShapeDtypeStruct((frames, tok, half), jnp.float32)]
        + [jax.ShapeDtypeStruct((frames, tok, half), jnp.bfloat16)] * n_tm,
        cost_estimate=pl.CostEstimate(
            flops=2 * rows * deep * half, bytes_accessed=2 * (rows + half) * deep, transcendentals=0
        ),
        compiler_params=pltpu.CompilerParams(vmem_limit_bytes=24 << 20),
        name="project",
    )(coef, *[a for h in attn for k in h for a in k], *[w for j in weights for w in j])


def finish_kernel(n_tm, n_mp, *refs):
    out = refs[-1]
    z, m = lax.axis_index("tm"), lax.axis_index("mp")
    half = refs[0].shape[-1]
    slices = n_tm // n_mp
    for u in range(slices):
        k_here = lax.rem(m * slices + u - z + n_tm, n_tm)
        for h in range(n_mp):
            first = (u * n_mp + h) * half
            for k in range(n_tm):
                for l in range(n_mp):

                    @pl.when((k_here == k) & (lax.rem(m - h + n_mp, n_mp) == l))
                    def _():
                        out[:, :, first : first + half] = refs[k * n_mp + l][...].astype(
                            jnp.float32
                        )


def finish(blocks):
    n_tm, n_mp = len(blocks), len(blocks[0])
    frames, tok, half = blocks[0][0].shape
    vmem = pl.BlockSpec(memory_space=pltpu.VMEM)
    return pl.pallas_call(
        functools.partial(finish_kernel, n_tm, n_mp),
        in_specs=[vmem] * (n_tm * n_mp),
        out_specs=vmem,
        out_shape=jax.ShapeDtypeStruct((frames, tok, n_tm * half), jnp.float32),
        cost_estimate=pl.CostEstimate(
            flops=0, bytes_accessed=8 * frames * tok * n_tm * half, transcendentals=0
        ),
        compiler_params=pltpu.CompilerParams(vmem_limit_bytes=6 << 20),
        name="finish",
    )(*[b for k in blocks for b in k])


def sweep(states, start_step, w_qkv, qk_gain, w_out, time_proj):
    frames, tok, _ = states.shape
    n_tm, n_seq, n_mp = (lax.axis_size(name) for name in ("tm", "seq", "mp"))
    z = lax.axis_index("tm")
    part = tok // n_mp
    depth, cols = w_qkv.shape[1:]
    window = frames * n_tm

    raw = list(spread(states, n_tm, part))
    for k in range(1, n_tm):
        raw[k] = turn(raw[k], "tm", k)
    near, far = [], []
    for blocks, kept in ((raw[0], near), (jnp.stack(raw[1:]), far)):
        for j in range(n_seq):
            side = turn(blocks, "seq", j) if j else blocks
            kept.append([side] + [turn(side, "mp", i) for i in range(1, n_mp)])

    shares = list(time_shares(start_step, time_proj, n_tm, window))
    for k in range(1, n_tm):
        shares[k] = turn(shares[k], "tm", k)

    shares_out = load_out(w_out, n_mp)
    weights = [turn(share, "mp", i) if i else share for i, share in enumerate(shares_out)]
    weights = [weights]
    for j in range(1, n_seq):
        weights.append([])
        for share in weights[0]:
            weights[j].append(turn(share, "seq", -j))

    groups = head_groups(cols)
    hidden, coef, held_qkv = modulate(start_step, w_qkv, shares, near, far)
    hidden = hidden.reshape(n_tm, n_seq * frames * tok, depth)
    proj = []
    for lane, size in groups:
        proj.append(
            jnp.einsum(
                "krd,cdh->kcrh",
                hidden,
                held_qkv[:, :, lane : lane + size],
                preferred_element_type=jnp.float32,
            )
        )
    even = z % 2 == 0
    ev = [(i, i ^ 1) for i in range(n_tm)]
    od = []
    for i in range(n_tm):
        for c in range(n_mp):
            other = i + 1 if i % 2 else i - 1
            inside = 0 <= other < n_tm
            to = other * n_mp + c if inside else i * n_mp + (c + 1) % n_mp
            od.append((i * n_mp + c, to))

    def incoming(pair):
        first, second = (0.0 if p is None else p.astype(jnp.float32) for p in pair)
        right = jnp.where(z > 0, jnp.where(even, second, first), 0.0)
        return right, jnp.where(z < n_tm - 1, jnp.where(even, first, second), 0.0)

    flows = [(None, None)] * len(groups)
    for t in range(n_tm - 1):
        for h in range(len(groups)):
            right, left = proj[h][(t + 1) % n_tm], proj[h][n_tm - 1 - t]
            if t:
                more_right, more_left = incoming(flows[h])
                right, left = right + more_right, left + more_left
            first = jnp.where(even, right, left).astype(jnp.float16)
            second = jnp.where(even, left, right).astype(jnp.float16)
            first = lax.ppermute(first, "tm", ev)
            if t:
                second = lax.ppermute(second, ("tm", "mp"), od)
                first, second = lax.optimization_barrier((first, second))
            flows[h] = (first, second if t else None)
    gathered = []
    for h, (lane, size) in enumerate(groups):
        right, left = incoming(flows[h])
        total = proj[h][0] + right + left
        total = total.reshape(3, n_seq, frames, tok, size)
        attn = attend(total, qk_gain[:, lane : lane + size])
        attn = jnp.stack([attn[0]] + [turn(attn[j], "seq", -j) for j in range(1, n_seq)])
        pieces = [attn]
        for k in range(1, n_tm):
            pieces.append(turn(attn, "tm", k))
        gathered.append([[g] + [turn(g, "mp", i) for i in range(1, n_mp)] for g in pieces])

    own, *moved = project(
        gathered, weights, coef, (n_tm, n_seq, n_mp, frames, part, cols), groups
    )
    blocks = []
    for k in range(n_tm):
        block = moved[0]
        if k:
            block = turn(moved[k], "tm", -k)
        others = [turn(block, "mp", i) for i in range(1, n_mp)]
        blocks.append([block if k else own] + others)
    return finish(blocks)


def solution(mesh):
    return jax.shard_map(
        sweep,
        mesh=mesh,
        in_specs=(
            P(("group", "tm"), "seq", None),
            P("group"),
            P(None, "tm", ("seq", "mp")),
            P(None, ("seq", "mp")),
            P("tm", ("seq", "mp")),
            P("tm", None),
        ),
        out_specs=P(("group", "tm"), "seq", "mp"),
        check_vma=False,
    )
```

```python
import functools

import jax
import jax.numpy as jnp
from jax import lax
from jax.experimental import pallas as pl
from jax.experimental.pallas import tpu as pltpu
from jax.sharding import PartitionSpec as P


HEAD_DIM = 128
FREQ = 256
STEPS = 100
LANES = 128


sample_shift = 5.0
norm_eps = 1e-06


def sigma_of(index):
    unit = 1.0 - index.astype(jnp.float32) / jnp.float32(STEPS)
    return sample_shift * unit / (1.0 + (sample_shift - 1.0) * unit)


def turn(block, axis, distance):
    size = lax.axis_size(axis)
    return lax.ppermute(block, axis, [(i, (i + distance) % size) for i in range(size)])


def head_norm(values, gain):
    meansq = jnp.mean(values * values, axis=-1, keepdims=True)
    return (values * lax.rsqrt(meansq + norm_eps) * gain).astype(jnp.bfloat16)


def head_groups(cols):
    heads = cols // HEAD_DIM
    first = (heads + 1) // 2 * HEAD_DIM
    return ((0, first), (first, cols - first)) if first < cols else ((0, cols),)


def attend_kernel(n_seq, heads, gain_ref, whole_ref, *outs):
    inv_root = 1.0 / jnp.sqrt(jnp.float32(HEAD_DIM))
    rows = whole_ref.shape[3]
    for h in range(heads):
        lanes = pl.ds(h * HEAD_DIM, HEAD_DIM)
        q, k, v = (
            jnp.concatenate([whole_ref[c, j, 0, :, lanes] for j in range(n_seq)], axis=0)
            for c in range(3)
        )
        q = head_norm(q, gain_ref[0:1, lanes])
        k = head_norm(k, gain_ref[1:2, lanes])
        scores = lax.dot_general(
            q, k, (((1,), (1,)), ((), ())), preferred_element_type=jnp.float32
        )
        expo = jnp.exp(scores * inv_root)
        probs = (expo / jnp.sum(expo, axis=-1, keepdims=True)).astype(jnp.bfloat16)
        attn = jnp.dot(
            probs, v.astype(jnp.bfloat16), preferred_element_type=jnp.float32
        ).astype(jnp.bfloat16)
        for j, out in enumerate(outs):
            out[0, :, lanes] = attn[j * rows : (j + 1) * rows]


def attend(whole, gain):
    _, n_seq, frames, rows, cols = whole.shape
    heads = cols // HEAD_DIM
    tokens = rows * n_seq
    out = jax.ShapeDtypeStruct((frames, rows, cols), jnp.bfloat16)
    return pl.pallas_call(
        functools.partial(attend_kernel, n_seq, heads),
        grid=(frames,),
        in_specs=[
            pl.BlockSpec((2, cols), lambda f: (0, 0)),
            pl.BlockSpec((3, n_seq, 1, rows, cols), lambda f: (0, 0, f, 0, 0)),
        ],
        out_specs=[pl.BlockSpec((1, rows, cols), lambda f: (f, 0, 0))] * n_seq,
        out_shape=[out] * n_seq,
        cost_estimate=pl.CostEstimate(
            flops=4 * frames * heads * tokens * tokens * HEAD_DIM,
            bytes_accessed=14 * frames * tokens * cols,
            transcendentals=frames * heads * tokens * tokens,
        ),
        compiler_params=pltpu.CompilerParams(vmem_limit_bytes=6 << 20),
        name="attend",
    )(gain, whole)


def spread_kernel(n_tm, states_ref, *outs):
    z, m = lax.axis_index("tm"), lax.axis_index("mp")
    frames, _, width = states_ref.shape
    part, depth = outs[0].shape[1], width // n_tm
    own = pl.ds(pl.multiple_of(m * part, part), part)
    lane = lax.broadcasted_iota(jnp.int32, (part, LANES), 1)
    for f in range(frames):
        field = states_ref[f, own, :].astype(jnp.float32)
        mean = jnp.mean(field, axis=-1, keepdims=True)
        centred = field - mean
        var = jnp.mean(centred * centred, axis=-1, keepdims=True)
        tail = jnp.zeros((part, LANES), jnp.float32)
        for place, rest in enumerate((mean, lax.rsqrt(var + norm_eps))):
            for term in range(3):
                cut = rest.astype(jnp.bfloat16).astype(jnp.float32)
                tail = jnp.where(lane == 3 * place + term, cut, tail)
                rest = rest - cut
        tail = tail.astype(jnp.bfloat16)
        for k, out in enumerate(outs):
            out[f, :, depth:] = tail
            for s in range(n_tm):

                @pl.when(lax.rem(z + k, n_tm) == s)
                def _():
                    out[f, :, :depth] = states_ref[f, own, s * depth : (s + 1) * depth]


def spread(states, n_tm, part):
    frames, _, width = states.shape
    out = jax.ShapeDtypeStruct((frames, part, width // n_tm + LANES), jnp.bfloat16)
    return pl.pallas_call(
        functools.partial(spread_kernel, n_tm),
        in_specs=[pl.BlockSpec(memory_space=pltpu.VMEM)],
        out_specs=[pl.BlockSpec(memory_space=pltpu.VMEM)] * n_tm,
        out_shape=[out] * n_tm,
        cost_estimate=pl.CostEstimate(
            flops=10 * part * width, bytes_accessed=4 * part * width, transcendentals=0
        ),
        compiler_params=pltpu.CompilerParams(vmem_limit_bytes=4 << 20),
        name="spread",
    )(states)


def time_kernel(n_tm, step_ref, proj_ref, *outs):
    z = lax.axis_index("tm")
    freq_rows, wide = proj_ref.shape
    window, depth = outs[0].shape[1:]
    half_freq = FREQ // 2
    index = step_ref[0] + lax.broadcasted_iota(jnp.int32, (window, freq_rows), 0)
    feature = z * freq_rows + lax.broadcasted_iota(jnp.int32, (window, freq_rows), 1)
    late = feature >= half_freq
    rank = jnp.where(late, feature - half_freq, feature).astype(jnp.float32)
    freqs = jnp.exp(-jnp.log(jnp.float32(10000.0)) * rank / jnp.float32(half_freq))
    angles = (1000.0 * sigma_of(index)) * freqs
    emb = jnp.where(late, jnp.sin(angles), jnp.cos(angles)).astype(jnp.bfloat16)
    for k, out in enumerate(outs):
        for s in range(n_tm):

            @pl.when(lax.rem(z + k, n_tm) == s)
            def _():
                for c in range(3):
                    first = c * (wide // 3) + s * depth
                    out[c] = jnp.dot(
                        emb, proj_ref[:, first : first + depth], preferred_element_type=jnp.float32
                    )


def time_shares(start_step, time_proj, n_tm, window):
    freq_rows, wide = time_proj.shape
    out = jax.ShapeDtypeStruct((3, window, wide // (3 * n_tm)), jnp.float32)
    smem, vmem = (pl.BlockSpec(memory_space=space) for space in (pltpu.SMEM, pltpu.VMEM))
    return pl.pallas_call(
        functools.partial(time_kernel, n_tm),
        in_specs=[smem, vmem],
        out_specs=[vmem] * n_tm,
        out_shape=[out] * n_tm,
        cost_estimate=pl.CostEstimate(
            flops=2 * window * freq_rows * wide, bytes_accessed=2 * freq_rows * wide, transcendentals=0
        ),
        compiler_params=pltpu.CompilerParams(vmem_limit_bytes=6 << 20),
        name="time_shares",
    )(start_step, time_proj)


def load_kernel(n_mp, w_ref, *refs):
    outs, sems = refs[:-1], refs[-1]
    copies = []
    for i, out in enumerate(outs):
        rows = out.shape[0]
        share = lax.rem(lax.axis_index("mp") + i, n_mp)
        source = w_ref.at[pl.ds(pl.multiple_of(share * rows, rows), rows)]
        copies.append(pltpu.make_async_copy(source, out, sems.at[i]))
    for copy in copies:
        copy.start()
    for copy in copies:
        copy.wait()


def load_out(weights, n_mp):
    share = jax.ShapeDtypeStruct((weights.shape[0] // n_mp, weights.shape[1]), weights.dtype)
    return pl.pallas_call(
        functools.partial(load_kernel, n_mp),
        in_specs=[pl.BlockSpec(memory_space=pltpu.HBM)],
        out_specs=[pl.BlockSpec(memory_space=pltpu.VMEM)] * n_mp,
        out_shape=[share] * n_mp,
        scratch_shapes=[pltpu.SemaphoreType.DMA((n_mp,))],
        cost_estimate=pl.CostEstimate(flops=0, bytes_accessed=2 * weights.size, transcendentals=0),
        compiler_params=pltpu.CompilerParams(vmem_limit_bytes=8 << 20),
        name="load_out",
    )(weights)


def modulate_kernel(n_tm, n_seq, n_mp, step_ref, *refs):
    sides = n_seq * n_mp
    shares, near, far = refs[:n_tm], refs[n_tm : n_tm + sides], refs[n_tm + sides :][:sides]
    hidden_ref, coef_ref, mod_scr = refs[n_tm + 2 * sides :]
    z, k = lax.axis_index("tm"), pl.program_id(0)
    frames, part, wide = near[0].shape
    depth = wide - LANES

    @pl.when(k == 0)
    def _():
        total = shares[0][...]
        for share in shares[1:]:
            total = total + share[...]
        mod_scr[...] = total

    for f in range(frames):
        step = lax.rem(z - k + n_tm, n_tm) * frames + f
        shift, scale, gate = (mod_scr[c, pl.ds(step, 1), :] for c in range(3))
        index = jnp.full((1, depth), step_ref[0] + step, jnp.int32)
        coef_ref[0, f : f + 1, :] = (sigma_of(index + 1) - sigma_of(index)) * gate

        def modulated(block):
            tail = block[:, depth:].astype(jnp.float32)
            mean = tail[:, 0:1] + tail[:, 1:2] + tail[:, 2:3]
            rstd = tail[:, 3:4] + tail[:, 4:5] + tail[:, 5:6]
            normed = (block[:, :depth].astype(jnp.float32) - mean) * rstd
            return (normed * (1.0 + scale) + shift).astype(jnp.bfloat16)

        for j in range(n_seq):
            for i in range(n_mp):
                to = slice(i * part, (i + 1) * part)

                @pl.when(k == 0)
                def _():
                    hidden_ref[0, j, f, to, :] = modulated(near[j * n_mp + i][f])

                @pl.when(k > 0)
                def _():
                    hidden_ref[0, j, f, to, :] = modulated(far[j * n_mp + i][0, f])


def modulate(start_step, shares, near, far):
    n_tm, n_seq, n_mp = len(shares), len(near), len(near[0])
    frames, part, wide = near[0][0].shape
    depth = wide - LANES
    window = shares[0].shape[1]
    shape = (n_tm, n_seq, frames, n_mp * part, depth)
    return pl.pallas_call(
        functools.partial(modulate_kernel, n_tm, n_seq, n_mp),
        grid=(n_tm,),
        in_specs=[pl.BlockSpec(memory_space=pltpu.SMEM)]
        + [pl.BlockSpec((3, window, depth), lambda k: (0, 0, 0))] * n_tm
        + [pl.BlockSpec((frames, part, wide), lambda k: (0, 0, 0))] * (n_seq * n_mp)
        + [pl.BlockSpec((1, frames, part, wide), lambda k: (jnp.maximum(k - 1, 0), 0, 0, 0))]
        * (n_seq * n_mp),
        out_specs=[
            pl.BlockSpec((1,) + shape[1:], lambda k: (k, 0, 0, 0, 0)),
            pl.BlockSpec((1, frames, depth), lambda k: (k, 0, 0)),
        ],
        scratch_shapes=[
            pltpu.VMEM((3, window, depth), jnp.float32),
        ],
        out_shape=[
            jax.ShapeDtypeStruct(shape, jnp.bfloat16),
            jax.ShapeDtypeStruct((n_tm, frames, depth), jnp.float32),
        ],
        cost_estimate=pl.CostEstimate(
            flops=4 * n_tm * n_seq * frames * n_mp * part * depth,
            bytes_accessed=4 * n_tm * n_seq * frames * n_mp * part * depth,
            transcendentals=0,
        ),
        compiler_params=pltpu.CompilerParams(vmem_limit_bytes=24 << 20),
        name="modulate",
    )(start_step, *shares, *[r for rows in (near, far) for side in rows for r in side])


def project_kernel(dims, widths, coef_ref, *refs):
    n_tm, n_seq, n_mp, frames, part, _ = dims
    n_attn = len(widths) * n_tm * n_mp
    attn_refs = refs[:n_attn]
    w_refs = refs[n_attn : n_attn + n_seq * n_mp]
    outs = refs[n_attn + n_seq * n_mp :]
    own_ref, moved_refs, (rows_scr, sum_scr) = outs[0], outs[1:-2], outs[-2:]
    z, m = lax.axis_index("tm"), lax.axis_index("mp")
    block = n_mp * part
    per = frames * block
    half = own_ref.shape[-1]
    total = None
    for j in range(n_seq):
        for l in range(n_mp):
            at = j * n_mp + l
            for k in range(n_tm):
                for f in range(frames):
                    for i in range(n_mp):
                        first = k * per + f * block + i * part
                        source = (i - l) % n_mp * part
                        for h, (lane, width) in enumerate(widths):
                            piece = attn_refs[(h * n_tm + k) * n_mp + l]
                            rows_scr[at, first : first + part, lane : lane + width] = piece[
                                j, f, source : source + part, :
                            ]
            product = lax.dot_general(
                rows_scr[at],
                w_refs[at][...],
                (((1,), (1,)), ((), ())),
                preferred_element_type=jnp.float32,
            )
            total = product if total is None else total + product
    for k in range(n_tm):
        for f in range(frames):
            first = k * per + f * block
            factor = coef_ref[k, f : f + 1, :half]
            for mm in range(1, n_mp):
                other = coef_ref[k, f : f + 1, mm * half : (mm + 1) * half]
                factor = jnp.where(m == mm, other, factor)
            drift = total[first : first + block] * factor
            sum_scr[lax.rem(z - k + n_tm, n_tm), f] = drift
    for s in range(n_tm):
        for f in range(frames):
            if s or f:
                before = sum_scr[s, f - 1] if f else sum_scr[s - 1, frames - 1]
                sum_scr[s, f] = sum_scr[s, f] + before
    for k in range(n_tm):
        own = lax.rem(z - k + n_tm, n_tm)
        for f in range(frames):
            for i in range(n_mp):
                to = pl.ds(pl.multiple_of(lax.rem(m - i + n_mp, n_mp) * part, part), part)
                piece = sum_scr[own, f, i * part : (i + 1) * part, :]
                moved_refs[k][f, to, :] = piece.astype(jnp.bfloat16)
                if k == 0:
                    own_ref[f, to, :] = piece


def project(attn, weights, coef, dims, widths):
    n_tm, n_seq, n_mp, frames, part, cols = dims
    half = weights[0][0].shape[0]
    tok = n_mp * part
    rows = n_tm * frames * tok
    deep = n_seq * n_mp * cols
    vmem = pl.BlockSpec(memory_space=pltpu.VMEM)
    return pl.pallas_call(
        functools.partial(project_kernel, dims, widths),
        in_specs=[vmem] * (1 + len(widths) * n_tm * n_mp + n_seq * n_mp),
        out_specs=[vmem] * (1 + n_tm),
        scratch_shapes=[
            pltpu.VMEM((n_seq * n_mp, rows, cols), jnp.bfloat16),
            pltpu.VMEM((n_tm, frames, tok, half), jnp.float32),
        ],
        out_shape=[jax.ShapeDtypeStruct((frames, tok, half), jnp.float32)]
        + [jax.ShapeDtypeStruct((frames, tok, half), jnp.bfloat16)] * n_tm,
        cost_estimate=pl.CostEstimate(
            flops=2 * rows * deep * half, bytes_accessed=2 * (rows + half) * deep, transcendentals=0
        ),
        compiler_params=pltpu.CompilerParams(vmem_limit_bytes=24 << 20),
        name="project",
    )(coef, *[a for h in attn for k in h for a in k], *[w for j in weights for w in j])


def finish_kernel(n_tm, n_mp, *refs):
    out = refs[-1]
    z, m = lax.axis_index("tm"), lax.axis_index("mp")
    half = refs[0].shape[-1]
    slices = n_tm // n_mp
    for u in range(slices):
        k_here = lax.rem(m * slices + u - z + n_tm, n_tm)
        for h in range(n_mp):
            first = (u * n_mp + h) * half
            for k in range(n_tm):
                for l in range(n_mp):

                    @pl.when((k_here == k) & (lax.rem(m - h + n_mp, n_mp) == l))
                    def _():
                        out[:, :, first : first + half] = refs[k * n_mp + l][...].astype(
                            jnp.float32
                        )


def finish(blocks):
    n_tm, n_mp = len(blocks), len(blocks[0])
    frames, tok, half = blocks[0][0].shape
    vmem = pl.BlockSpec(memory_space=pltpu.VMEM)
    return pl.pallas_call(
        functools.partial(finish_kernel, n_tm, n_mp),
        in_specs=[vmem] * (n_tm * n_mp),
        out_specs=vmem,
        out_shape=jax.ShapeDtypeStruct((frames, tok, n_tm * half), jnp.float32),
        cost_estimate=pl.CostEstimate(
            flops=0, bytes_accessed=8 * frames * tok * n_tm * half, transcendentals=0
        ),
        compiler_params=pltpu.CompilerParams(vmem_limit_bytes=6 << 20),
        name="finish",
    )(*[b for k in blocks for b in k])


def sweep(states, start_step, w_qkv, qk_gain, w_out, time_proj):
    frames, tok, _ = states.shape
    n_tm, n_seq, n_mp = (lax.axis_size(name) for name in ("tm", "seq", "mp"))
    z = lax.axis_index("tm")
    part = tok // n_mp
    depth, cols = w_qkv.shape[1:]
    window = frames * n_tm

    raw = list(spread(states, n_tm, part))
    for k in range(1, n_tm):
        raw[k] = turn(raw[k], "tm", k)
    near, far = [], []
    for blocks, kept in ((raw[0], near), (jnp.stack(raw[1:]), far)):
        for j in range(n_seq):
            side = turn(blocks, "seq", j) if j else blocks
            kept.append([side] + [turn(side, "mp", i) for i in range(1, n_mp)])

    shares = list(time_shares(start_step, time_proj, n_tm, window))
    for k in range(1, n_tm):
        shares[k] = turn(shares[k], "tm", k)

    shares_out = load_out(w_out, n_mp)
    weights = [turn(share, "mp", i) if i else share for i, share in enumerate(shares_out)]
    weights = [weights]
    for j in range(1, n_seq):
        weights.append([])
        for share in weights[0]:
            weights[j].append(turn(share, "seq", -j))

    groups = head_groups(cols)
    hidden, coef = modulate(start_step, shares, near, far)
    hidden = hidden.reshape(n_tm, n_seq * frames * tok, depth)
    proj = []
    for lane, size in groups:
        proj.append(
            jnp.einsum(
                "krd,cdh->kcrh",
                hidden,
                w_qkv[:, :, lane : lane + size],
                preferred_element_type=jnp.float32,
            )
        )
    even = z % 2 == 0
    ev = [(i, i ^ 1) for i in range(n_tm)]
    od = []
    for i in range(n_tm):
        for c in range(n_mp):
            other = i + 1 if i % 2 else i - 1
            inside = 0 <= other < n_tm
            to = other * n_mp + c if inside else i * n_mp + (c + 1) % n_mp
            od.append((i * n_mp + c, to))

    def incoming(pair):
        first, second = (0.0 if p is None else p.astype(jnp.float32) for p in pair)
        right = jnp.where(z > 0, jnp.where(even, second, first), 0.0)
        return right, jnp.where(z < n_tm - 1, jnp.where(even, first, second), 0.0)

    flows = [(None, None)] * len(groups)
    for t in range(n_tm - 1):
        for h in range(len(groups)):
            right, left = proj[h][(t + 1) % n_tm], proj[h][n_tm - 1 - t]
            if t:
                more_right, more_left = incoming(flows[h])
                right, left = right + more_right, left + more_left
            first = jnp.where(even, right, left).astype(jnp.float16)
            second = jnp.where(even, left, right).astype(jnp.float16)
            first = lax.ppermute(first, "tm", ev)
            if t:
                second = lax.ppermute(second, ("tm", "mp"), od)
                first, second = lax.optimization_barrier((first, second))
            flows[h] = (first, second if t else None)
    gathered = []
    for h, (lane, size) in enumerate(groups):
        right, left = incoming(flows[h])
        total = proj[h][0] + right + left
        total = total.reshape(3, n_seq, frames, tok, size)
        attn = attend(total, qk_gain[:, lane : lane + size])
        attn = jnp.stack([attn[0]] + [turn(attn[j], "seq", -j) for j in range(1, n_seq)])
        pieces = [attn]
        for k in range(1, n_tm):
            pieces.append(turn(attn, "tm", k))
        gathered.append([[g] + [turn(g, "mp", i) for i in range(1, n_mp)] for g in pieces])

    own, *moved = project(
        gathered, weights, coef, (n_tm, n_seq, n_mp, frames, part, cols), groups
    )
    blocks = []
    for k in range(n_tm):
        block = moved[0]
        if k:
            block = turn(moved[k], "tm", -k)
        others = [turn(block, "mp", i) for i in range(1, n_mp)]
        blocks.append([block if k else own] + others)
    return finish(blocks)


def solution(mesh):
    return jax.shard_map(
        sweep,
        mesh=mesh,
        in_specs=(
            P(("group", "tm"), "seq", None),
            P("group"),
            P(None, "tm", ("seq", "mp")),
            P(None, ("seq", "mp")),
            P("tm", ("seq", "mp")),
            P("tm", None),
        ),
        out_specs=P(("group", "tm"), "seq", "mp"),
        check_vma=False,
    )
```

```python
import functools

import jax
import jax.numpy as jnp
from jax import lax
from jax.experimental import pallas as pl
from jax.experimental.pallas import tpu as pltpu
from jax.sharding import PartitionSpec as P


HEAD_DIM = 128
FREQ = 256
STEPS = 100
LANES = 128
DMA_PIECES = 4


sample_shift = 5.0
norm_eps = 1e-06


def sigma_of(index):
    unit = 1.0 - index.astype(jnp.float32) / jnp.float32(STEPS)
    return sample_shift * unit / (1.0 + (sample_shift - 1.0) * unit)


def turn(block, axis, distance):
    size = lax.axis_size(axis)
    return lax.ppermute(block, axis, [(i, (i + distance) % size) for i in range(size)])


def head_norm(values, gain):
    meansq = jnp.mean(values * values, axis=-1, keepdims=True)
    return (values * lax.rsqrt(meansq + norm_eps) * gain).astype(jnp.bfloat16)


def head_groups(cols):
    heads = cols // HEAD_DIM
    first = (heads + 1) // 2 * HEAD_DIM
    return ((0, first), (first, cols - first)) if first < cols else ((0, cols),)


def attend_kernel(n_seq, heads, gain_ref, whole_ref, *outs):
    inv_root = 1.0 / jnp.sqrt(jnp.float32(HEAD_DIM))
    rows = whole_ref.shape[3]
    for h in range(heads):
        lanes = pl.ds(h * HEAD_DIM, HEAD_DIM)
        q, k, v = (
            jnp.concatenate([whole_ref[c, j, 0, :, lanes] for j in range(n_seq)], axis=0)
            for c in range(3)
        )
        q = head_norm(q, gain_ref[0:1, lanes])
        k = head_norm(k, gain_ref[1:2, lanes])
        scores = lax.dot_general(
            q, k, (((1,), (1,)), ((), ())), preferred_element_type=jnp.float32
        )
        expo = jnp.exp(scores * inv_root)
        probs = (expo / jnp.sum(expo, axis=-1, keepdims=True)).astype(jnp.bfloat16)
        attn = jnp.dot(
            probs, v.astype(jnp.bfloat16), preferred_element_type=jnp.float32
        ).astype(jnp.bfloat16)
        for j, out in enumerate(outs):
            out[0, :, lanes] = attn[j * rows : (j + 1) * rows]


def attend(whole, gain):
    _, n_seq, frames, rows, cols = whole.shape
    heads = cols // HEAD_DIM
    tokens = rows * n_seq
    out = jax.ShapeDtypeStruct((frames, rows, cols), jnp.bfloat16)
    return pl.pallas_call(
        functools.partial(attend_kernel, n_seq, heads),
        grid=(frames,),
        in_specs=[
            pl.BlockSpec((2, cols), lambda f: (0, 0)),
            pl.BlockSpec((3, n_seq, 1, rows, cols), lambda f: (0, 0, f, 0, 0)),
        ],
        out_specs=[pl.BlockSpec((1, rows, cols), lambda f: (f, 0, 0))] * n_seq,
        out_shape=[out] * n_seq,
        cost_estimate=pl.CostEstimate(
            flops=4 * frames * heads * tokens * tokens * HEAD_DIM,
            bytes_accessed=14 * frames * tokens * cols,
            transcendentals=frames * heads * tokens * tokens,
        ),
        compiler_params=pltpu.CompilerParams(vmem_limit_bytes=6 << 20),
        name="attend",
    )(gain, whole)


def spread_kernel(n_tm, states_ref, *outs):
    z, m = lax.axis_index("tm"), lax.axis_index("mp")
    frames, _, width = states_ref.shape
    part, depth = outs[0].shape[1], width // n_tm
    own = pl.ds(pl.multiple_of(m * part, part), part)
    lane = lax.broadcasted_iota(jnp.int32, (part, LANES), 1)
    for f in range(frames):
        field = states_ref[f, own, :].astype(jnp.float32)
        mean = jnp.mean(field, axis=-1, keepdims=True)
        centred = field - mean
        var = jnp.mean(centred * centred, axis=-1, keepdims=True)
        tail = jnp.zeros((part, LANES), jnp.float32)
        for place, rest in enumerate((mean, lax.rsqrt(var + norm_eps))):
            for term in range(3):
                cut = rest.astype(jnp.bfloat16).astype(jnp.float32)
                tail = jnp.where(lane == 3 * place + term, cut, tail)
                rest = rest - cut
        tail = tail.astype(jnp.bfloat16)
        for k, out in enumerate(outs):
            out[f, :, depth:] = tail
            for s in range(n_tm):

                @pl.when(lax.rem(z + k, n_tm) == s)
                def _():
                    out[f, :, :depth] = states_ref[f, own, s * depth : (s + 1) * depth]


def spread(states, n_tm, part):
    frames, _, width = states.shape
    out = jax.ShapeDtypeStruct((frames, part, width // n_tm + LANES), jnp.bfloat16)
    return pl.pallas_call(
        functools.partial(spread_kernel, n_tm),
        in_specs=[pl.BlockSpec(memory_space=pltpu.VMEM)],
        out_specs=[pl.BlockSpec(memory_space=pltpu.VMEM)] * n_tm,
        out_shape=[out] * n_tm,
        cost_estimate=pl.CostEstimate(
            flops=10 * part * width, bytes_accessed=4 * part * width, transcendentals=0
        ),
        compiler_params=pltpu.CompilerParams(vmem_limit_bytes=4 << 20),
        name="spread",
    )(states)


def time_kernel(n_tm, step_ref, proj_ref, *outs):
    z = lax.axis_index("tm")
    freq_rows, wide = proj_ref.shape
    window, depth = outs[0].shape[1:]
    half_freq = FREQ // 2
    index = step_ref[0] + lax.broadcasted_iota(jnp.int32, (window, freq_rows), 0)
    feature = z * freq_rows + lax.broadcasted_iota(jnp.int32, (window, freq_rows), 1)
    late = feature >= half_freq
    rank = jnp.where(late, feature - half_freq, feature).astype(jnp.float32)
    freqs = jnp.exp(-jnp.log(jnp.float32(10000.0)) * rank / jnp.float32(half_freq))
    angles = (1000.0 * sigma_of(index)) * freqs
    emb = jnp.where(late, jnp.sin(angles), jnp.cos(angles)).astype(jnp.bfloat16)
    for k, out in enumerate(outs):
        for s in range(n_tm):

            @pl.when(lax.rem(z + k, n_tm) == s)
            def _():
                for c in range(3):
                    first = c * (wide // 3) + s * depth
                    out[c] = jnp.dot(
                        emb, proj_ref[:, first : first + depth], preferred_element_type=jnp.float32
                    )


def time_shares(start_step, time_proj, n_tm, window):
    freq_rows, wide = time_proj.shape
    out = jax.ShapeDtypeStruct((3, window, wide // (3 * n_tm)), jnp.float32)
    smem, vmem = (pl.BlockSpec(memory_space=space) for space in (pltpu.SMEM, pltpu.VMEM))
    return pl.pallas_call(
        functools.partial(time_kernel, n_tm),
        in_specs=[smem, vmem],
        out_specs=[vmem] * n_tm,
        out_shape=[out] * n_tm,
        cost_estimate=pl.CostEstimate(
            flops=2 * window * freq_rows * wide, bytes_accessed=2 * freq_rows * wide, transcendentals=0
        ),
        compiler_params=pltpu.CompilerParams(vmem_limit_bytes=6 << 20),
        name="time_shares",
    )(start_step, time_proj)


def load_kernel(n_mp, w_ref, *refs):
    outs, sems = refs[:-1], refs[-1]
    copies = []
    for i, out in enumerate(outs):
        rows = out.shape[0]
        share = lax.rem(lax.axis_index("mp") + i, n_mp)
        source = w_ref.at[pl.ds(pl.multiple_of(share * rows, rows), rows)]
        copies.append(pltpu.make_async_copy(source, out, sems.at[i]))
    for copy in copies:
        copy.start()
    for copy in copies:
        copy.wait()


def load_out(weights, n_mp):
    share = jax.ShapeDtypeStruct((weights.shape[0] // n_mp, weights.shape[1]), weights.dtype)
    return pl.pallas_call(
        functools.partial(load_kernel, n_mp),
        in_specs=[pl.BlockSpec(memory_space=pltpu.HBM)],
        out_specs=[pl.BlockSpec(memory_space=pltpu.VMEM)] * n_mp,
        out_shape=[share] * n_mp,
        scratch_shapes=[pltpu.SemaphoreType.DMA((n_mp,))],
        cost_estimate=pl.CostEstimate(flops=0, bytes_accessed=2 * weights.size, transcendentals=0),
        compiler_params=pltpu.CompilerParams(vmem_limit_bytes=8 << 20),
        name="load_out",
    )(weights)


def modulate_kernel(n_tm, n_seq, n_mp, step_ref, w_ref, *refs):
    sides = n_seq * n_mp
    shares, near, far = refs[:n_tm], refs[n_tm : n_tm + sides], refs[n_tm + sides :][:sides]
    hidden_ref, coef_ref, w_out, mod_scr, sems = refs[n_tm + 2 * sides :]
    stride = w_ref.shape[1] // DMA_PIECES
    copies = []
    for c in range(w_ref.shape[0]):
        for piece in range(DMA_PIECES):
            at = c, pl.ds(piece * stride, stride)
            copies.append(
                pltpu.make_async_copy(w_ref.at[at], w_out.at[at], sems.at[len(copies)])
            )
    z, k = lax.axis_index("tm"), pl.program_id(0)
    frames, part, wide = near[0].shape
    depth = wide - LANES

    @pl.when(k == 0)
    def _():
        for copy in copies:
            copy.start()
        total = shares[0][...]
        for share in shares[1:]:
            total = total + share[...]
        mod_scr[...] = total

    def write(blocks):
        for f in range(frames):
            step = lax.rem(z - k + n_tm, n_tm) * frames + f
            shift, scale, gate = (mod_scr[c, pl.ds(step, 1), :] for c in range(3))
            index = jnp.full((1, depth), step_ref[0] + step, jnp.int32)
            coef_ref[0, f : f + 1, :] = (sigma_of(index + 1) - sigma_of(index)) * gate
            for j in range(n_seq):
                for i in range(n_mp):
                    block = blocks[j * n_mp + i]
                    tail = block[f, :, depth:].astype(jnp.float32)
                    mean = tail[:, 0:1] + tail[:, 1:2] + tail[:, 2:3]
                    rstd = tail[:, 3:4] + tail[:, 4:5] + tail[:, 5:6]
                    normed = (block[f, :, :depth].astype(jnp.float32) - mean) * rstd
                    hidden_ref[0, j, f, i * part : (i + 1) * part, :] = (
                        normed * (1.0 + scale) + shift
                    ).astype(jnp.bfloat16)

    @pl.when(k == 0)
    def _():
        write(near)

    @pl.when(k > 0)
    def _():
        write([block.at[0] for block in far])

    @pl.when(k == n_tm - 1)
    def _():
        for copy in copies:
            copy.wait()


def modulate(start_step, w_qkv, shares, near, far):
    n_tm, n_seq, n_mp = len(shares), len(near), len(near[0])
    frames, part, wide = near[0][0].shape
    three = w_qkv.shape[0]
    depth = wide - LANES
    window = shares[0].shape[1]
    shape = (n_tm, n_seq, frames, n_mp * part, depth)
    return pl.pallas_call(
        functools.partial(modulate_kernel, n_tm, n_seq, n_mp),
        grid=(n_tm,),
        in_specs=[pl.BlockSpec(memory_space=pltpu.SMEM), pl.BlockSpec(memory_space=pltpu.HBM)]
        + [pl.BlockSpec((3, window, depth), lambda k: (0, 0, 0))] * n_tm
        + [pl.BlockSpec((frames, part, wide), lambda k: (0, 0, 0))] * (n_seq * n_mp)
        + [pl.BlockSpec((1, frames, part, wide), lambda k: (jnp.maximum(k - 1, 0), 0, 0, 0))]
        * (n_seq * n_mp),
        out_specs=[
            pl.BlockSpec((1,) + shape[1:], lambda k: (k, 0, 0, 0, 0)),
            pl.BlockSpec((1, frames, depth), lambda k: (k, 0, 0)),
        ]
        + [pl.BlockSpec(memory_space=pl.ANY)],
        scratch_shapes=[
            pltpu.VMEM((3, window, depth), jnp.float32),
            pltpu.SemaphoreType.DMA((three * DMA_PIECES,)),
        ],
        out_shape=[
            jax.ShapeDtypeStruct(shape, jnp.bfloat16),
            jax.ShapeDtypeStruct((n_tm, frames, depth), jnp.float32),
        ]
        + [jax.ShapeDtypeStruct(w_qkv.shape, w_qkv.dtype)],
        cost_estimate=pl.CostEstimate(
            flops=4 * n_tm * n_seq * frames * n_mp * part * depth,
            bytes_accessed=4 * n_tm * n_seq * frames * n_mp * part * depth,
            transcendentals=0,
        ),
        compiler_params=pltpu.CompilerParams(vmem_limit_bytes=42 << 20),
        name="modulate",
    )(start_step, w_qkv, *shares, *[r for rows in (near, far) for side in rows for r in side])


def project_kernel(dims, widths, coef_ref, *refs):
    n_tm, n_seq, n_mp, frames, part, _ = dims
    n_attn = len(widths) * n_tm * n_mp
    attn_refs = refs[:n_attn]
    w_refs = refs[n_attn : n_attn + n_seq * n_mp]
    outs = refs[n_attn + n_seq * n_mp :]
    own_ref, moved_refs, (rows_scr, sum_scr) = outs[0], outs[1:-2], outs[-2:]
    z, m = lax.axis_index("tm"), lax.axis_index("mp")
    block = n_mp * part
    per = frames * block
    half = own_ref.shape[-1]
    total = None
    for j in range(n_seq):
        for l in range(n_mp):
            at = j * n_mp + l
            for k in range(n_tm):
                for f in range(frames):
                    for i in range(n_mp):
                        first = k * per + f * block + i * part
                        source = (i - l) % n_mp * part
                        for h, (lane, width) in enumerate(widths):
                            piece = attn_refs[(h * n_tm + k) * n_mp + l]
                            rows_scr[at, first : first + part, lane : lane + width] = piece[
                                j, f, source : source + part, :
                            ]
            product = lax.dot_general(
                rows_scr[at],
                w_refs[at][...],
                (((1,), (1,)), ((), ())),
                preferred_element_type=jnp.float32,
            )
            total = product if total is None else total + product
    for k in range(n_tm):
        for f in range(frames):
            first = k * per + f * block
            factor = coef_ref[k, f : f + 1, :half]
            for mm in range(1, n_mp):
                other = coef_ref[k, f : f + 1, mm * half : (mm + 1) * half]
                factor = jnp.where(m == mm, other, factor)
            drift = total[first : first + block] * factor
            sum_scr[lax.rem(z - k + n_tm, n_tm), f] = drift
    for s in range(n_tm):
        for f in range(frames):
            if s or f:
                before = sum_scr[s, f - 1] if f else sum_scr[s - 1, frames - 1]
                sum_scr[s, f] = sum_scr[s, f] + before
    for k in range(n_tm):
        own = lax.rem(z - k + n_tm, n_tm)
        for f in range(frames):
            for i in range(n_mp):
                to = pl.ds(pl.multiple_of(lax.rem(m - i + n_mp, n_mp) * part, part), part)
                piece = sum_scr[own, f, i * part : (i + 1) * part, :]
                moved_refs[k][f, to, :] = piece.astype(jnp.bfloat16)
                if k == 0:
                    own_ref[f, to, :] = piece


def project(attn, weights, coef, dims, widths):
    n_tm, n_seq, n_mp, frames, part, cols = dims
    half = weights[0][0].shape[0]
    tok = n_mp * part
    rows = n_tm * frames * tok
    deep = n_seq * n_mp * cols
    vmem = pl.BlockSpec(memory_space=pltpu.VMEM)
    return pl.pallas_call(
        functools.partial(project_kernel, dims, widths),
        in_specs=[vmem] * (1 + len(widths) * n_tm * n_mp + n_seq * n_mp),
        out_specs=[vmem] * (1 + n_tm),
        scratch_shapes=[
            pltpu.VMEM((n_seq * n_mp, rows, cols), jnp.bfloat16),
            pltpu.VMEM((n_tm, frames, tok, half), jnp.float32),
        ],
        out_shape=[jax.ShapeDtypeStruct((frames, tok, half), jnp.float32)]
        + [jax.ShapeDtypeStruct((frames, tok, half), jnp.bfloat16)] * n_tm,
        cost_estimate=pl.CostEstimate(
            flops=2 * rows * deep * half, bytes_accessed=2 * (rows + half) * deep, transcendentals=0
        ),
        compiler_params=pltpu.CompilerParams(vmem_limit_bytes=24 << 20),
        name="project",
    )(coef, *[a for h in attn for k in h for a in k], *[w for j in weights for w in j])


def finish_kernel(n_tm, n_mp, *refs):
    out = refs[-1]
    z, m = lax.axis_index("tm"), lax.axis_index("mp")
    half = refs[0].shape[-1]
    slices = n_tm // n_mp
    for u in range(slices):
        k_here = lax.rem(m * slices + u - z + n_tm, n_tm)
        for h in range(n_mp):
            first = (u * n_mp + h) * half
            for k in range(n_tm):
                for l in range(n_mp):

                    @pl.when((k_here == k) & (lax.rem(m - h + n_mp, n_mp) == l))
                    def _():
                        out[:, :, first : first + half] = refs[k * n_mp + l][...].astype(
                            jnp.float32
                        )


def finish(blocks):
    n_tm, n_mp = len(blocks), len(blocks[0])
    frames, tok, half = blocks[0][0].shape
    vmem = pl.BlockSpec(memory_space=pltpu.VMEM)
    return pl.pallas_call(
        functools.partial(finish_kernel, n_tm, n_mp),
        in_specs=[vmem] * (n_tm * n_mp),
        out_specs=vmem,
        out_shape=jax.ShapeDtypeStruct((frames, tok, n_tm * half), jnp.float32),
        cost_estimate=pl.CostEstimate(
            flops=0, bytes_accessed=8 * frames * tok * n_tm * half, transcendentals=0
        ),
        compiler_params=pltpu.CompilerParams(vmem_limit_bytes=6 << 20),
        name="finish",
    )(*[b for k in blocks for b in k])


def sweep(states, start_step, w_qkv, qk_gain, w_out, time_proj):
    frames, tok, _ = states.shape
    n_tm, n_seq, n_mp = (lax.axis_size(name) for name in ("tm", "seq", "mp"))
    z = lax.axis_index("tm")
    part = tok // n_mp
    depth, cols = w_qkv.shape[1:]
    window = frames * n_tm

    raw = list(spread(states, n_tm, part))
    for k in range(1, n_tm):
        raw[k] = turn(raw[k], "tm", k)
    near, far = [], []
    for blocks, kept in ((raw[0], near), (jnp.stack(raw[1:]), far)):
        for j in range(n_seq):
            side = turn(blocks, "seq", j) if j else blocks
            kept.append([side] + [turn(side, "mp", i) for i in range(1, n_mp)])

    shares = list(time_shares(start_step, time_proj, n_tm, window))
    for k in range(1, n_tm):
        shares[k] = turn(shares[k], "tm", k)

    shares_out = load_out(w_out, n_mp)
    weights = [turn(share, "mp", i) if i else share for i, share in enumerate(shares_out)]
    weights = [weights]
    for j in range(1, n_seq):
        weights.append([])
        for share in weights[0]:
            weights[j].append(turn(share, "seq", -j))

    groups = head_groups(cols)
    hidden, coef, held_qkv = modulate(start_step, w_qkv, shares, near, far)
    hidden = hidden.reshape(n_tm, n_seq * frames * tok, depth)
    proj = []
    for lane, size in groups:
        proj.append(
            jnp.einsum(
                "krd,cdh->kcrh",
                hidden,
                held_qkv[:, :, lane : lane + size],
                preferred_element_type=jnp.float32,
            )
        )
    even = z % 2 == 0
    ev = [(i, i ^ 1) for i in range(n_tm)]
    od = []
    for i in range(n_tm):
        for c in range(n_mp):
            other = i + 1 if i % 2 else i - 1
            inside = 0 <= other < n_tm
            to = other * n_mp + c if inside else i * n_mp + (c + 1) % n_mp
            od.append((i * n_mp + c, to))

    def incoming(pair):
        first, second = (0.0 if p is None else p.astype(jnp.float32) for p in pair)
        right = jnp.where(z > 0, jnp.where(even, second, first), 0.0)
        return right, jnp.where(z < n_tm - 1, jnp.where(even, first, second), 0.0)

    flows = [(None, None)] * len(groups)
    for t in range(n_tm - 1):
        for h in range(len(groups)):
            right, left = proj[h][(t + 1) % n_tm], proj[h][n_tm - 1 - t]
            if t:
                more_right, more_left = incoming(flows[h])
                right, left = right + more_right, left + more_left
            first = jnp.where(even, right, left).astype(jnp.float16)
            second = jnp.where(even, left, right).astype(jnp.float16)
            first = lax.ppermute(first, "tm", ev)
            if t:
                second = lax.ppermute(second, ("tm", "mp"), od)
                first, second = lax.optimization_barrier((first, second))
            flows[h] = (first, second if t else None)
    gathered = []
    for h, (lane, size) in enumerate(groups):
        right, left = incoming(flows[h])
        total = proj[h][0] + right + left
        total = total.reshape(3, n_seq, frames, tok, size)
        attn = attend(total, qk_gain[:, lane : lane + size])
        attn = jnp.stack([attn[0]] + [turn(attn[j], "seq", -j) for j in range(1, n_seq)])
        pieces = [attn]
        for k in range(1, n_tm):
            pieces.append(turn(attn, "tm", k))
        gathered.append([[g] + [turn(g, "mp", i) for i in range(1, n_mp)] for g in pieces])

    own, *moved = project(
        gathered, weights, coef, (n_tm, n_seq, n_mp, frames, part, cols), groups
    )
    blocks = []
    for k in range(n_tm):
        block = moved[0]
        if k:
            block = turn(moved[k], "tm", -k)
        others = [turn(block, "mp", i) for i in range(1, n_mp)]
        blocks.append([block if k else own] + others)
    return finish(blocks)


def solution(mesh):
    return jax.shard_map(
        sweep,
        mesh=mesh,
        in_specs=(
            P(("group", "tm"), "seq", None),
            P("group"),
            P(None, "tm", ("seq", "mp")),
            P(None, ("seq", "mp")),
            P("tm", ("seq", "mp")),
            P("tm", None),
        ),
        out_specs=P(("group", "tm"), "seq", "mp"),
        check_vma=False,
    )
```

```python
import functools

import jax
import jax.numpy as jnp
from jax import lax
from jax.experimental import pallas as pl
from jax.experimental.pallas import tpu as pltpu
from jax.sharding import PartitionSpec as P


HEAD_DIM = 128
FREQ = 256
STEPS = 100
LANES = 128


sample_shift = 5.0
norm_eps = 1e-06


def sigma_of(index):
    unit = 1.0 - index.astype(jnp.float32) / jnp.float32(STEPS)
    return sample_shift * unit / (1.0 + (sample_shift - 1.0) * unit)


def turn(block, axis, distance):
    size = lax.axis_size(axis)
    return lax.ppermute(block, axis, [(i, (i + distance) % size) for i in range(size)])


def head_norm(values, gain):
    meansq = jnp.mean(values * values, axis=-1, keepdims=True)
    return (values * lax.rsqrt(meansq + norm_eps) * gain).astype(jnp.bfloat16)


def head_groups(cols):
    heads = cols // HEAD_DIM
    first = (heads + 1) // 2 * HEAD_DIM
    return ((0, first), (first, cols - first)) if first < cols else ((0, cols),)


def attend_kernel(n_seq, heads, gain_ref, whole_ref, *outs):
    inv_root = 1.0 / jnp.sqrt(jnp.float32(HEAD_DIM))
    rows = whole_ref.shape[3]
    for h in range(heads):
        lanes = pl.ds(h * HEAD_DIM, HEAD_DIM)
        q, k, v = (
            jnp.concatenate([whole_ref[c, j, 0, :, lanes] for j in range(n_seq)], axis=0)
            for c in range(3)
        )
        q = head_norm(q, gain_ref[0:1, lanes])
        k = head_norm(k, gain_ref[1:2, lanes])
        scores = lax.dot_general(
            q, k, (((1,), (1,)), ((), ())), preferred_element_type=jnp.float32
        )
        expo = jnp.exp(scores * inv_root)
        probs = (expo / jnp.sum(expo, axis=-1, keepdims=True)).astype(jnp.bfloat16)
        attn = jnp.dot(
            probs, v.astype(jnp.bfloat16), preferred_element_type=jnp.float32
        ).astype(jnp.bfloat16)
        for j, out in enumerate(outs):
            out[0, :, lanes] = attn[j * rows : (j + 1) * rows]


def attend(whole, gain):
    _, n_seq, frames, rows, cols = whole.shape
    heads = cols // HEAD_DIM
    tokens = rows * n_seq
    out = jax.ShapeDtypeStruct((frames, rows, cols), jnp.bfloat16)
    return pl.pallas_call(
        functools.partial(attend_kernel, n_seq, heads),
        grid=(frames,),
        in_specs=[
            pl.BlockSpec((2, cols), lambda f: (0, 0)),
            pl.BlockSpec((3, n_seq, 1, rows, cols), lambda f: (0, 0, f, 0, 0)),
        ],
        out_specs=[pl.BlockSpec((1, rows, cols), lambda f: (f, 0, 0))] * n_seq,
        out_shape=[out] * n_seq,
        cost_estimate=pl.CostEstimate(
            flops=4 * frames * heads * tokens * tokens * HEAD_DIM,
            bytes_accessed=14 * frames * tokens * cols,
            transcendentals=frames * heads * tokens * tokens,
        ),
        compiler_params=pltpu.CompilerParams(vmem_limit_bytes=6 << 20),
        name="attend",
    )(gain, whole)


def spread_kernel(n_tm, states_ref, *outs):
    z, m = lax.axis_index("tm"), lax.axis_index("mp")
    frames, _, width = states_ref.shape
    part, depth = outs[0].shape[1], width // n_tm
    own = pl.ds(pl.multiple_of(m * part, part), part)
    lane = lax.broadcasted_iota(jnp.int32, (part, LANES), 1)
    for f in range(frames):
        field = states_ref[f, own, :].astype(jnp.float32)
        mean = jnp.mean(field, axis=-1, keepdims=True)
        centred = field - mean
        var = jnp.mean(centred * centred, axis=-1, keepdims=True)
        tail = jnp.zeros((part, LANES), jnp.float32)
        for place, rest in enumerate((mean, lax.rsqrt(var + norm_eps))):
            for term in range(3):
                cut = rest.astype(jnp.bfloat16).astype(jnp.float32)
                tail = jnp.where(lane == 3 * place + term, cut, tail)
                rest = rest - cut
        tail = tail.astype(jnp.bfloat16)
        for k, out in enumerate(outs):
            out[f, :, depth:] = tail
            for s in range(n_tm):

                @pl.when(lax.rem(z + k, n_tm) == s)
                def _():
                    out[f, :, :depth] = states_ref[f, own, s * depth : (s + 1) * depth]


def spread(states, n_tm, part):
    frames, _, width = states.shape
    out = jax.ShapeDtypeStruct((frames, part, width // n_tm + LANES), jnp.bfloat16)
    return pl.pallas_call(
        functools.partial(spread_kernel, n_tm),
        in_specs=[pl.BlockSpec(memory_space=pltpu.VMEM)],
        out_specs=[pl.BlockSpec(memory_space=pltpu.VMEM)] * n_tm,
        out_shape=[out] * n_tm,
        cost_estimate=pl.CostEstimate(
            flops=10 * part * width, bytes_accessed=4 * part * width, transcendentals=0
        ),
        compiler_params=pltpu.CompilerParams(vmem_limit_bytes=4 << 20),
        name="spread",
    )(states)


def time_kernel(n_tm, step_ref, proj_ref, *outs):
    z = lax.axis_index("tm")
    freq_rows, wide = proj_ref.shape
    window, depth = outs[0].shape[1:]
    half_freq = FREQ // 2
    index = step_ref[0] + lax.broadcasted_iota(jnp.int32, (window, freq_rows), 0)
    feature = z * freq_rows + lax.broadcasted_iota(jnp.int32, (window, freq_rows), 1)
    late = feature >= half_freq
    rank = jnp.where(late, feature - half_freq, feature).astype(jnp.float32)
    freqs = jnp.exp(-jnp.log(jnp.float32(10000.0)) * rank / jnp.float32(half_freq))
    angles = (1000.0 * sigma_of(index)) * freqs
    emb = jnp.where(late, jnp.sin(angles), jnp.cos(angles)).astype(jnp.bfloat16)
    for k, out in enumerate(outs):
        for s in range(n_tm):

            @pl.when(lax.rem(z + k, n_tm) == s)
            def _():
                for c in range(3):
                    first = c * (wide // 3) + s * depth
                    out[c] = jnp.dot(
                        emb, proj_ref[:, first : first + depth], preferred_element_type=jnp.float32
                    )


def time_shares(start_step, time_proj, n_tm, window):
    freq_rows, wide = time_proj.shape
    out = jax.ShapeDtypeStruct((3, window, wide // (3 * n_tm)), jnp.float32)
    smem, vmem = (pl.BlockSpec(memory_space=space) for space in (pltpu.SMEM, pltpu.VMEM))
    return pl.pallas_call(
        functools.partial(time_kernel, n_tm),
        in_specs=[smem, vmem],
        out_specs=[vmem] * n_tm,
        out_shape=[out] * n_tm,
        cost_estimate=pl.CostEstimate(
            flops=2 * window * freq_rows * wide, bytes_accessed=2 * freq_rows * wide, transcendentals=0
        ),
        compiler_params=pltpu.CompilerParams(vmem_limit_bytes=6 << 20),
        name="time_shares",
    )(start_step, time_proj)


def load_kernel(n_mp, w_ref, *refs):
    outs, sems = refs[:-1], refs[-1]
    copies = []
    for i, out in enumerate(outs):
        rows = out.shape[0]
        share = lax.rem(lax.axis_index("mp") + i, n_mp)
        source = w_ref.at[pl.ds(pl.multiple_of(share * rows, rows), rows)]
        copies.append(pltpu.make_async_copy(source, out, sems.at[i]))
    for copy in copies:
        copy.start()
    for copy in copies:
        copy.wait()


def load_out(weights, n_mp):
    share = jax.ShapeDtypeStruct((weights.shape[0] // n_mp, weights.shape[1]), weights.dtype)
    return pl.pallas_call(
        functools.partial(load_kernel, n_mp),
        in_specs=[pl.BlockSpec(memory_space=pltpu.HBM)],
        out_specs=[pl.BlockSpec(memory_space=pltpu.VMEM)] * n_mp,
        out_shape=[share] * n_mp,
        scratch_shapes=[pltpu.SemaphoreType.DMA((n_mp,))],
        cost_estimate=pl.CostEstimate(flops=0, bytes_accessed=2 * weights.size, transcendentals=0),
        compiler_params=pltpu.CompilerParams(vmem_limit_bytes=8 << 20),
        name="load_out",
    )(weights)


def modulate_kernel(n_tm, n_seq, n_mp, step_ref, *refs):
    sides = n_seq * n_mp
    shares, near, far = refs[:n_tm], refs[n_tm : n_tm + sides], refs[n_tm + sides :][:sides]
    hidden_ref, coef_ref, mod_scr = refs[n_tm + 2 * sides :]
    z, k = lax.axis_index("tm"), pl.program_id(0)
    frames, part, wide = near[0].shape
    depth = wide - LANES

    @pl.when(k == 0)
    def _():
        total = shares[0][...]
        for share in shares[1:]:
            total = total + share[...]
        mod_scr[...] = total

    def write(blocks):
        for f in range(frames):
            step = lax.rem(z - k + n_tm, n_tm) * frames + f
            shift, scale, gate = (mod_scr[c, pl.ds(step, 1), :] for c in range(3))
            index = jnp.full((1, depth), step_ref[0] + step, jnp.int32)
            coef_ref[0, f : f + 1, :] = (sigma_of(index + 1) - sigma_of(index)) * gate
            for j in range(n_seq):
                for i in range(n_mp):
                    block = blocks[j * n_mp + i]
                    tail = block[f, :, depth:].astype(jnp.float32)
                    mean = tail[:, 0:1] + tail[:, 1:2] + tail[:, 2:3]
                    rstd = tail[:, 3:4] + tail[:, 4:5] + tail[:, 5:6]
                    normed = (block[f, :, :depth].astype(jnp.float32) - mean) * rstd
                    hidden_ref[0, j, f, i * part : (i + 1) * part, :] = (
                        normed * (1.0 + scale) + shift
                    ).astype(jnp.bfloat16)

    @pl.when(k == 0)
    def _():
        write(near)

    @pl.when(k > 0)
    def _():
        write([block.at[0] for block in far])


def modulate(start_step, shares, near, far):
    n_tm, n_seq, n_mp = len(shares), len(near), len(near[0])
    frames, part, wide = near[0][0].shape
    depth = wide - LANES
    window = shares[0].shape[1]
    shape = (n_tm, n_seq, frames, n_mp * part, depth)
    return pl.pallas_call(
        functools.partial(modulate_kernel, n_tm, n_seq, n_mp),
        grid=(n_tm,),
        in_specs=[pl.BlockSpec(memory_space=pltpu.SMEM)]
        + [pl.BlockSpec((3, window, depth), lambda k: (0, 0, 0))] * n_tm
        + [pl.BlockSpec((frames, part, wide), lambda k: (0, 0, 0))] * (n_seq * n_mp)
        + [pl.BlockSpec((1, frames, part, wide), lambda k: (jnp.maximum(k - 1, 0), 0, 0, 0))]
        * (n_seq * n_mp),
        out_specs=[
            pl.BlockSpec((1,) + shape[1:], lambda k: (k, 0, 0, 0, 0)),
            pl.BlockSpec((1, frames, depth), lambda k: (k, 0, 0)),
        ],
        scratch_shapes=[
            pltpu.VMEM((3, window, depth), jnp.float32),
        ],
        out_shape=[
            jax.ShapeDtypeStruct(shape, jnp.bfloat16),
            jax.ShapeDtypeStruct((n_tm, frames, depth), jnp.float32),
        ],
        cost_estimate=pl.CostEstimate(
            flops=4 * n_tm * n_seq * frames * n_mp * part * depth,
            bytes_accessed=4 * n_tm * n_seq * frames * n_mp * part * depth,
            transcendentals=0,
        ),
        compiler_params=pltpu.CompilerParams(vmem_limit_bytes=24 << 20),
        name="modulate",
    )(start_step, *shares, *[r for rows in (near, far) for side in rows for r in side])


def project_kernel(dims, widths, coef_ref, *refs):
    n_tm, n_seq, n_mp, frames, part, _ = dims
    n_attn = len(widths) * n_tm * n_mp
    attn_refs = refs[:n_attn]
    w_refs = refs[n_attn : n_attn + n_seq * n_mp]
    outs = refs[n_attn + n_seq * n_mp :]
    own_ref, moved_refs, (rows_scr, sum_scr) = outs[0], outs[1:-2], outs[-2:]
    z, m = lax.axis_index("tm"), lax.axis_index("mp")
    block = n_mp * part
    per = frames * block
    half = own_ref.shape[-1]
    total = None
    for j in range(n_seq):
        for l in range(n_mp):
            at = j * n_mp + l
            for k in range(n_tm):
                for f in range(frames):
                    for i in range(n_mp):
                        first = k * per + f * block + i * part
                        source = (i - l) % n_mp * part
                        for h, (lane, width) in enumerate(widths):
                            piece = attn_refs[(h * n_tm + k) * n_mp + l]
                            rows_scr[at, first : first + part, lane : lane + width] = piece[
                                j, f, source : source + part, :
                            ]
            product = lax.dot_general(
                rows_scr[at],
                w_refs[at][...],
                (((1,), (1,)), ((), ())),
                preferred_element_type=jnp.float32,
            )
            total = product if total is None else total + product
    for k in range(n_tm):
        for f in range(frames):
            first = k * per + f * block
            factor = coef_ref[k, f : f + 1, :half]
            for mm in range(1, n_mp):
                other = coef_ref[k, f : f + 1, mm * half : (mm + 1) * half]
                factor = jnp.where(m == mm, other, factor)
            drift = total[first : first + block] * factor
            sum_scr[lax.rem(z - k + n_tm, n_tm), f] = drift
    for s in range(n_tm):
        for f in range(frames):
            if s or f:
                before = sum_scr[s, f - 1] if f else sum_scr[s - 1, frames - 1]
                sum_scr[s, f] = sum_scr[s, f] + before
    for k in range(n_tm):
        own = lax.rem(z - k + n_tm, n_tm)
        for f in range(frames):
            for i in range(n_mp):
                to = pl.ds(pl.multiple_of(lax.rem(m - i + n_mp, n_mp) * part, part), part)
                piece = sum_scr[own, f, i * part : (i + 1) * part, :]
                moved_refs[k][f, to, :] = piece.astype(jnp.bfloat16)
                if k == 0:
                    own_ref[f, to, :] = piece


def project(attn, weights, coef, dims, widths):
    n_tm, n_seq, n_mp, frames, part, cols = dims
    half = weights[0][0].shape[0]
    tok = n_mp * part
    rows = n_tm * frames * tok
    deep = n_seq * n_mp * cols
    vmem = pl.BlockSpec(memory_space=pltpu.VMEM)
    return pl.pallas_call(
        functools.partial(project_kernel, dims, widths),
        in_specs=[vmem] * (1 + len(widths) * n_tm * n_mp + n_seq * n_mp),
        out_specs=[vmem] * (1 + n_tm),
        scratch_shapes=[
            pltpu.VMEM((n_seq * n_mp, rows, cols), jnp.bfloat16),
            pltpu.VMEM((n_tm, frames, tok, half), jnp.float32),
        ],
        out_shape=[jax.ShapeDtypeStruct((frames, tok, half), jnp.float32)]
        + [jax.ShapeDtypeStruct((frames, tok, half), jnp.bfloat16)] * n_tm,
        cost_estimate=pl.CostEstimate(
            flops=2 * rows * deep * half, bytes_accessed=2 * (rows + half) * deep, transcendentals=0
        ),
        compiler_params=pltpu.CompilerParams(vmem_limit_bytes=24 << 20),
        name="project",
    )(coef, *[a for h in attn for k in h for a in k], *[w for j in weights for w in j])


def finish_kernel(n_tm, n_mp, *refs):
    out = refs[-1]
    z, m = lax.axis_index("tm"), lax.axis_index("mp")
    half = refs[0].shape[-1]
    slices = n_tm // n_mp
    for u in range(slices):
        k_here = lax.rem(m * slices + u - z + n_tm, n_tm)
        for h in range(n_mp):
            first = (u * n_mp + h) * half
            for k in range(n_tm):
                for l in range(n_mp):

                    @pl.when((k_here == k) & (lax.rem(m - h + n_mp, n_mp) == l))
                    def _():
                        out[:, :, first : first + half] = refs[k * n_mp + l][...].astype(
                            jnp.float32
                        )


def finish(blocks):
    n_tm, n_mp = len(blocks), len(blocks[0])
    frames, tok, half = blocks[0][0].shape
    vmem = pl.BlockSpec(memory_space=pltpu.VMEM)
    return pl.pallas_call(
        functools.partial(finish_kernel, n_tm, n_mp),
        in_specs=[vmem] * (n_tm * n_mp),
        out_specs=vmem,
        out_shape=jax.ShapeDtypeStruct((frames, tok, n_tm * half), jnp.float32),
        cost_estimate=pl.CostEstimate(
            flops=0, bytes_accessed=8 * frames * tok * n_tm * half, transcendentals=0
        ),
        compiler_params=pltpu.CompilerParams(vmem_limit_bytes=6 << 20),
        name="finish",
    )(*[b for k in blocks for b in k])


def sweep(states, start_step, w_qkv, qk_gain, w_out, time_proj):
    frames, tok, _ = states.shape
    n_tm, n_seq, n_mp = (lax.axis_size(name) for name in ("tm", "seq", "mp"))
    z = lax.axis_index("tm")
    part = tok // n_mp
    depth, cols = w_qkv.shape[1:]
    window = frames * n_tm

    raw = list(spread(states, n_tm, part))
    for k in range(1, n_tm):
        raw[k] = turn(raw[k], "tm", k)
    near, far = [], []
    for blocks, kept in ((raw[0], near), (jnp.stack(raw[1:]), far)):
        for j in range(n_seq):
            side = turn(blocks, "seq", j) if j else blocks
            kept.append([side] + [turn(side, "mp", i) for i in range(1, n_mp)])

    shares = list(time_shares(start_step, time_proj, n_tm, window))
    for k in range(1, n_tm):
        shares[k] = turn(shares[k], "tm", k)

    shares_out = load_out(w_out, n_mp)
    weights = [turn(share, "mp", i) if i else share for i, share in enumerate(shares_out)]
    weights = [weights]
    for j in range(1, n_seq):
        weights.append([])
        for share in weights[0]:
            weights[j].append(turn(share, "seq", -j))

    groups = head_groups(cols)
    hidden, coef = modulate(start_step, shares, near, far)
    hidden = hidden.reshape(n_tm, n_seq * frames * tok, depth)
    proj = []
    for lane, size in groups:
        proj.append(
            jnp.einsum(
                "krd,cdh->kcrh",
                hidden,
                w_qkv[:, :, lane : lane + size],
                preferred_element_type=jnp.float32,
            )
        )
    even = z % 2 == 0
    ev = [(i, i ^ 1) for i in range(n_tm)]
    od = []
    for i in range(n_tm):
        for c in range(n_mp):
            other = i + 1 if i % 2 else i - 1
            inside = 0 <= other < n_tm
            to = other * n_mp + c if inside else i * n_mp + (c + 1) % n_mp
            od.append((i * n_mp + c, to))

    def incoming(pair):
        first, second = (0.0 if p is None else p.astype(jnp.float32) for p in pair)
        right = jnp.where(z > 0, jnp.where(even, second, first), 0.0)
        return right, jnp.where(z < n_tm - 1, jnp.where(even, first, second), 0.0)

    flows = [(None, None)] * len(groups)
    for t in range(n_tm - 1):
        for h in range(len(groups)):
            right, left = proj[h][(t + 1) % n_tm], proj[h][n_tm - 1 - t]
            if t:
                more_right, more_left = incoming(flows[h])
                right, left = right + more_right, left + more_left
            first = jnp.where(even, right, left).astype(jnp.float16)
            second = jnp.where(even, left, right).astype(jnp.float16)
            first = lax.ppermute(first, "tm", ev)
            if t:
                second = lax.ppermute(second, ("tm", "mp"), od)
                first, second = lax.optimization_barrier((first, second))
            flows[h] = (first, second if t else None)
    gathered = []
    for h, (lane, size) in enumerate(groups):
        right, left = incoming(flows[h])
        total = proj[h][0] + right + left
        total = total.reshape(3, n_seq, frames, tok, size)
        attn = attend(total, qk_gain[:, lane : lane + size])
        attn = jnp.stack([attn[0]] + [turn(attn[j], "seq", -j) for j in range(1, n_seq)])
        pieces = [attn]
        for k in range(1, n_tm):
            pieces.append(turn(attn, "tm", k))
        gathered.append([[g] + [turn(g, "mp", i) for i in range(1, n_mp)] for g in pieces])

    own, *moved = project(
        gathered, weights, coef, (n_tm, n_seq, n_mp, frames, part, cols), groups
    )
    blocks = []
    for k in range(n_tm):
        block = moved[0]
        if k:
            block = turn(moved[k], "tm", -k)
        others = [turn(block, "mp", i) for i in range(1, n_mp)]
        blocks.append([block if k else own] + others)
    return finish(blocks)


def solution(mesh):
    return jax.shard_map(
        sweep,
        mesh=mesh,
        in_specs=(
            P(("group", "tm"), "seq", None),
            P("group"),
            P(None, "tm", ("seq", "mp")),
            P(None, ("seq", "mp")),
            P("tm", ("seq", "mp")),
            P("tm", None),
        ),
        out_specs=P(("group", "tm"), "seq", "mp"),
        check_vma=False,
    )
```

```python
import functools

import jax
import jax.numpy as jnp
from jax import lax
from jax.experimental import pallas as pl
from jax.experimental.pallas import tpu as pltpu
from jax.sharding import PartitionSpec as P


HEAD_DIM = 128
FREQ = 256
STEPS = 100
LANES = 128
DMA_PIECES = 4


sample_shift = 5.0
norm_eps = 1e-06


def sigma_of(index):
    unit = 1.0 - index.astype(jnp.float32) / jnp.float32(STEPS)
    return sample_shift * unit / (1.0 + (sample_shift - 1.0) * unit)


def turn(block, axis, distance):
    size = lax.axis_size(axis)
    return lax.ppermute(block, axis, [(i, (i + distance) % size) for i in range(size)])


def head_norm(values, gain):
    meansq = jnp.mean(values * values, axis=-1, keepdims=True)
    return (values * lax.rsqrt(meansq + norm_eps) * gain).astype(jnp.bfloat16)


def head_groups(cols):
    heads = cols // HEAD_DIM
    first = (heads + 1) // 2 * HEAD_DIM
    return ((0, first), (first, cols - first)) if first < cols else ((0, cols),)


def attend_kernel(n_seq, heads, gain_ref, whole_ref, *outs):
    inv_root = 1.0 / jnp.sqrt(jnp.float32(HEAD_DIM))
    rows = whole_ref.shape[3]
    for h in range(heads):
        lanes = pl.ds(h * HEAD_DIM, HEAD_DIM)
        q, k, v = (
            jnp.concatenate([whole_ref[c, j, 0, :, lanes] for j in range(n_seq)], axis=0)
            for c in range(3)
        )
        q = head_norm(q, gain_ref[0:1, lanes])
        k = head_norm(k, gain_ref[1:2, lanes])
        scores = lax.dot_general(
            q, k, (((1,), (1,)), ((), ())), preferred_element_type=jnp.float32
        )
        expo = jnp.exp(scores * inv_root)
        probs = (expo / jnp.sum(expo, axis=-1, keepdims=True)).astype(jnp.bfloat16)
        attn = jnp.dot(
            probs, v.astype(jnp.bfloat16), preferred_element_type=jnp.float32
        ).astype(jnp.bfloat16)
        for j, out in enumerate(outs):
            out[0, :, lanes] = attn[j * rows : (j + 1) * rows]


def attend(whole, gain):
    _, n_seq, frames, rows, cols = whole.shape
    heads = cols // HEAD_DIM
    tokens = rows * n_seq
    out = jax.ShapeDtypeStruct((frames, rows, cols), jnp.bfloat16)
    return pl.pallas_call(
        functools.partial(attend_kernel, n_seq, heads),
        grid=(frames,),
        in_specs=[
            pl.BlockSpec((2, cols), lambda f: (0, 0)),
            pl.BlockSpec((3, n_seq, 1, rows, cols), lambda f: (0, 0, f, 0, 0)),
        ],
        out_specs=[pl.BlockSpec((1, rows, cols), lambda f: (f, 0, 0))] * n_seq,
        out_shape=[out] * n_seq,
        cost_estimate=pl.CostEstimate(
            flops=4 * frames * heads * tokens * tokens * HEAD_DIM,
            bytes_accessed=14 * frames * tokens * cols,
            transcendentals=frames * heads * tokens * tokens,
        ),
        compiler_params=pltpu.CompilerParams(vmem_limit_bytes=6 << 20),
        name="attend",
    )(gain, whole)


def spread_kernel(n_tm, states_ref, *outs):
    z, m = lax.axis_index("tm"), lax.axis_index("mp")
    frames, _, width = states_ref.shape
    part, depth = outs[0].shape[1], width // n_tm
    own = pl.ds(pl.multiple_of(m * part, part), part)
    lane = lax.broadcasted_iota(jnp.int32, (part, LANES), 1)
    for f in range(frames):
        field = states_ref[f, own, :].astype(jnp.float32)
        mean = jnp.mean(field, axis=-1, keepdims=True)
        centred = field - mean
        var = jnp.mean(centred * centred, axis=-1, keepdims=True)
        tail = jnp.zeros((part, LANES), jnp.float32)
        for place, rest in enumerate((mean, lax.rsqrt(var + norm_eps))):
            for term in range(3):
                cut = rest.astype(jnp.bfloat16).astype(jnp.float32)
                tail = jnp.where(lane == 3 * place + term, cut, tail)
                rest = rest - cut
        tail = tail.astype(jnp.bfloat16)
        for k, out in enumerate(outs):
            out[f, :, depth:] = tail
            for s in range(n_tm):

                @pl.when(lax.rem(z + k, n_tm) == s)
                def _():
                    out[f, :, :depth] = states_ref[f, own, s * depth : (s + 1) * depth]


def spread(states, n_tm, part):
    frames, _, width = states.shape
    out = jax.ShapeDtypeStruct((frames, part, width // n_tm + LANES), jnp.bfloat16)
    return pl.pallas_call(
        functools.partial(spread_kernel, n_tm),
        in_specs=[pl.BlockSpec(memory_space=pltpu.VMEM)],
        out_specs=[pl.BlockSpec(memory_space=pltpu.VMEM)] * n_tm,
        out_shape=[out] * n_tm,
        cost_estimate=pl.CostEstimate(
            flops=10 * part * width, bytes_accessed=4 * part * width, transcendentals=0
        ),
        compiler_params=pltpu.CompilerParams(vmem_limit_bytes=4 << 20),
        name="spread",
    )(states)


def time_kernel(n_tm, step_ref, proj_ref, *outs):
    z = lax.axis_index("tm")
    freq_rows, wide = proj_ref.shape
    window, depth = outs[0].shape[1:]
    half_freq = FREQ // 2
    index = step_ref[0] + lax.broadcasted_iota(jnp.int32, (window, freq_rows), 0)
    feature = z * freq_rows + lax.broadcasted_iota(jnp.int32, (window, freq_rows), 1)
    late = feature >= half_freq
    rank = jnp.where(late, feature - half_freq, feature).astype(jnp.float32)
    freqs = jnp.exp(-jnp.log(jnp.float32(10000.0)) * rank / jnp.float32(half_freq))
    angles = (1000.0 * sigma_of(index)) * freqs
    emb = jnp.where(late, jnp.sin(angles), jnp.cos(angles)).astype(jnp.bfloat16)
    for k, out in enumerate(outs):
        for s in range(n_tm):

            @pl.when(lax.rem(z + k, n_tm) == s)
            def _():
                for c in range(3):
                    first = c * (wide // 3) + s * depth
                    out[c] = jnp.dot(
                        emb, proj_ref[:, first : first + depth], preferred_element_type=jnp.float32
                    )


def time_shares(start_step, time_proj, n_tm, window):
    freq_rows, wide = time_proj.shape
    out = jax.ShapeDtypeStruct((3, window, wide // (3 * n_tm)), jnp.float32)
    smem, vmem = (pl.BlockSpec(memory_space=space) for space in (pltpu.SMEM, pltpu.VMEM))
    return pl.pallas_call(
        functools.partial(time_kernel, n_tm),
        in_specs=[smem, vmem],
        out_specs=[vmem] * n_tm,
        out_shape=[out] * n_tm,
        cost_estimate=pl.CostEstimate(
            flops=2 * window * freq_rows * wide, bytes_accessed=2 * freq_rows * wide, transcendentals=0
        ),
        compiler_params=pltpu.CompilerParams(vmem_limit_bytes=6 << 20),
        name="time_shares",
    )(start_step, time_proj)


def load_kernel(n_mp, w_ref, *refs):
    outs, sems = refs[:-1], refs[-1]
    copies = []
    for i, out in enumerate(outs):
        rows = out.shape[0]
        share = lax.rem(lax.axis_index("mp") + i, n_mp)
        source = w_ref.at[pl.ds(pl.multiple_of(share * rows, rows), rows)]
        copies.append(pltpu.make_async_copy(source, out, sems.at[i]))
    for copy in copies:
        copy.start()
    for copy in copies:
        copy.wait()


def load_out(weights, n_mp):
    share = jax.ShapeDtypeStruct((weights.shape[0] // n_mp, weights.shape[1]), weights.dtype)
    return pl.pallas_call(
        functools.partial(load_kernel, n_mp),
        in_specs=[pl.BlockSpec(memory_space=pltpu.HBM)],
        out_specs=[pl.BlockSpec(memory_space=pltpu.VMEM)] * n_mp,
        out_shape=[share] * n_mp,
        scratch_shapes=[pltpu.SemaphoreType.DMA((n_mp,))],
        cost_estimate=pl.CostEstimate(flops=0, bytes_accessed=2 * weights.size, transcendentals=0),
        compiler_params=pltpu.CompilerParams(vmem_limit_bytes=8 << 20),
        name="load_out",
    )(weights)


def modulate_kernel(n_tm, n_seq, n_mp, step_ref, w_ref, *refs):
    sides = n_seq * n_mp
    shares, near, far = refs[:n_tm], refs[n_tm : n_tm + sides], refs[n_tm + sides :][:sides]
    hidden_ref, coef_ref, w_out, mod_scr, sems = refs[n_tm + 2 * sides :]
    stride = w_ref.shape[1] // DMA_PIECES
    copies = []
    for c in range(w_ref.shape[0]):
        for piece in range(DMA_PIECES):
            rows_here = pl.ds(piece * stride, stride)
            copies.append(
                pltpu.make_async_copy(
                    w_ref.at[c, rows_here, pl.ds(0, w_out.shape[2])],
                    w_out.at[c, rows_here],
                    sems.at[len(copies)],
                )
            )
    z, k = lax.axis_index("tm"), pl.program_id(0)
    frames, part, wide = near[0].shape
    depth = wide - LANES

    @pl.when(k == 0)
    def _():
        for copy in copies:
            copy.start()
        total = shares[0][...]
        for share in shares[1:]:
            total = total + share[...]
        mod_scr[...] = total

    def write(blocks):
        for f in range(frames):
            step = lax.rem(z - k + n_tm, n_tm) * frames + f
            shift, scale, gate = (mod_scr[c, pl.ds(step, 1), :] for c in range(3))
            index = jnp.full((1, depth), step_ref[0] + step, jnp.int32)
            coef_ref[0, f : f + 1, :] = (sigma_of(index + 1) - sigma_of(index)) * gate
            for j in range(n_seq):
                for i in range(n_mp):
                    block = blocks[j * n_mp + i]
                    tail = block[f, :, depth:].astype(jnp.float32)
                    mean = tail[:, 0:1] + tail[:, 1:2] + tail[:, 2:3]
                    rstd = tail[:, 3:4] + tail[:, 4:5] + tail[:, 5:6]
                    normed = (block[f, :, :depth].astype(jnp.float32) - mean) * rstd
                    hidden_ref[0, j, f, i * part : (i + 1) * part, :] = (
                        normed * (1.0 + scale) + shift
                    ).astype(jnp.bfloat16)

    @pl.when(k == 0)
    def _():
        write(near)

    @pl.when(k > 0)
    def _():
        write([block.at[0] for block in far])

    @pl.when(k == n_tm - 1)
    def _():
        for copy in copies:
            copy.wait()


def modulate(start_step, w_qkv, held, shares, near, far):
    n_tm, n_seq, n_mp = len(shares), len(near), len(near[0])
    frames, part, wide = near[0][0].shape
    three = w_qkv.shape[0]
    depth = wide - LANES
    window = shares[0].shape[1]
    shape = (n_tm, n_seq, frames, n_mp * part, depth)
    return pl.pallas_call(
        functools.partial(modulate_kernel, n_tm, n_seq, n_mp),
        grid=(n_tm,),
        in_specs=[pl.BlockSpec(memory_space=pltpu.SMEM), pl.BlockSpec(memory_space=pltpu.HBM)]
        + [pl.BlockSpec((3, window, depth), lambda k: (0, 0, 0))] * n_tm
        + [pl.BlockSpec((frames, part, wide), lambda k: (0, 0, 0))] * (n_seq * n_mp)
        + [pl.BlockSpec((1, frames, part, wide), lambda k: (jnp.maximum(k - 1, 0), 0, 0, 0))]
        * (n_seq * n_mp),
        out_specs=[
            pl.BlockSpec((1,) + shape[1:], lambda k: (k, 0, 0, 0, 0)),
            pl.BlockSpec((1, frames, depth), lambda k: (k, 0, 0)),
        ]
        + [pl.BlockSpec(memory_space=pl.ANY)],
        scratch_shapes=[
            pltpu.VMEM((3, window, depth), jnp.float32),
            pltpu.SemaphoreType.DMA((three * DMA_PIECES,)),
        ],
        out_shape=[
            jax.ShapeDtypeStruct(shape, jnp.bfloat16),
            jax.ShapeDtypeStruct((n_tm, frames, depth), jnp.float32),
        ]
        + [jax.ShapeDtypeStruct(w_qkv.shape[:2] + (held,), w_qkv.dtype)],
        cost_estimate=pl.CostEstimate(
            flops=4 * n_tm * n_seq * frames * n_mp * part * depth,
            bytes_accessed=4 * n_tm * n_seq * frames * n_mp * part * depth,
            transcendentals=0,
        ),
        compiler_params=pltpu.CompilerParams(vmem_limit_bytes=46 << 20),
        name="modulate",
    )(start_step, w_qkv, *shares, *[r for rows in (near, far) for side in rows for r in side])


def project_kernel(dims, widths, coef_ref, *refs):
    n_tm, n_seq, n_mp, frames, part, _ = dims
    n_attn = len(widths) * n_tm * n_mp
    attn_refs = refs[:n_attn]
    w_refs = refs[n_attn : n_attn + n_seq * n_mp]
    outs = refs[n_attn + n_seq * n_mp :]
    own_ref, moved_refs, (rows_scr, sum_scr) = outs[0], outs[1:-2], outs[-2:]
    z, m = lax.axis_index("tm"), lax.axis_index("mp")
    block = n_mp * part
    per = frames * block
    half = own_ref.shape[-1]
    total = None
    for j in range(n_seq):
        for l in range(n_mp):
            at = j * n_mp + l
            for k in range(n_tm):
                for f in range(frames):
                    for i in range(n_mp):
                        first = k * per + f * block + i * part
                        source = (i - l) % n_mp * part
                        for h, (lane, width) in enumerate(widths):
                            piece = attn_refs[(h * n_tm + k) * n_mp + l]
                            rows_scr[at, first : first + part, lane : lane + width] = piece[
                                j, f, source : source + part, :
                            ]
            product = lax.dot_general(
                rows_scr[at],
                w_refs[at][...],
                (((1,), (1,)), ((), ())),
                preferred_element_type=jnp.float32,
            )
            total = product if total is None else total + product
    for k in range(n_tm):
        for f in range(frames):
            first = k * per + f * block
            factor = coef_ref[k, f : f + 1, :half]
            for mm in range(1, n_mp):
                other = coef_ref[k, f : f + 1, mm * half : (mm + 1) * half]
                factor = jnp.where(m == mm, other, factor)
            drift = total[first : first + block] * factor
            sum_scr[lax.rem(z - k + n_tm, n_tm), f] = drift
    for s in range(n_tm):
        for f in range(frames):
            if s or f:
                before = sum_scr[s, f - 1] if f else sum_scr[s - 1, frames - 1]
                sum_scr[s, f] = sum_scr[s, f] + before
    for k in range(n_tm):
        own = lax.rem(z - k + n_tm, n_tm)
        for f in range(frames):
            for i in range(n_mp):
                to = pl.ds(pl.multiple_of(lax.rem(m - i + n_mp, n_mp) * part, part), part)
                piece = sum_scr[own, f, i * part : (i + 1) * part, :]
                moved_refs[k][f, to, :] = piece.astype(jnp.bfloat16)
                if k == 0:
                    own_ref[f, to, :] = piece


def project(attn, weights, coef, dims, widths):
    n_tm, n_seq, n_mp, frames, part, cols = dims
    half = weights[0][0].shape[0]
    tok = n_mp * part
    rows = n_tm * frames * tok
    deep = n_seq * n_mp * cols
    vmem = pl.BlockSpec(memory_space=pltpu.VMEM)
    return pl.pallas_call(
        functools.partial(project_kernel, dims, widths),
        in_specs=[vmem] * (1 + len(widths) * n_tm * n_mp + n_seq * n_mp),
        out_specs=[vmem] * (1 + n_tm),
        scratch_shapes=[
            pltpu.VMEM((n_seq * n_mp, rows, cols), jnp.bfloat16),
            pltpu.VMEM((n_tm, frames, tok, half), jnp.float32),
        ],
        out_shape=[jax.ShapeDtypeStruct((frames, tok, half), jnp.float32)]
        + [jax.ShapeDtypeStruct((frames, tok, half), jnp.bfloat16)] * n_tm,
        cost_estimate=pl.CostEstimate(
            flops=2 * rows * deep * half, bytes_accessed=2 * (rows + half) * deep, transcendentals=0
        ),
        compiler_params=pltpu.CompilerParams(vmem_limit_bytes=24 << 20),
        name="project",
    )(coef, *[a for h in attn for k in h for a in k], *[w for j in weights for w in j])


def finish_kernel(n_tm, n_mp, *refs):
    out = refs[-1]
    z, m = lax.axis_index("tm"), lax.axis_index("mp")
    half = refs[0].shape[-1]
    slices = n_tm // n_mp
    for u in range(slices):
        k_here = lax.rem(m * slices + u - z + n_tm, n_tm)
        for h in range(n_mp):
            first = (u * n_mp + h) * half
            for k in range(n_tm):
                for l in range(n_mp):

                    @pl.when((k_here == k) & (lax.rem(m - h + n_mp, n_mp) == l))
                    def _():
                        out[:, :, first : first + half] = refs[k * n_mp + l][...].astype(
                            jnp.float32
                        )


def finish(blocks):
    n_tm, n_mp = len(blocks), len(blocks[0])
    frames, tok, half = blocks[0][0].shape
    vmem = pl.BlockSpec(memory_space=pltpu.VMEM)
    return pl.pallas_call(
        functools.partial(finish_kernel, n_tm, n_mp),
        in_specs=[vmem] * (n_tm * n_mp),
        out_specs=vmem,
        out_shape=jax.ShapeDtypeStruct((frames, tok, n_tm * half), jnp.float32),
        cost_estimate=pl.CostEstimate(
            flops=0, bytes_accessed=8 * frames * tok * n_tm * half, transcendentals=0
        ),
        compiler_params=pltpu.CompilerParams(vmem_limit_bytes=6 << 20),
        name="finish",
    )(*[b for k in blocks for b in k])


def sweep(states, start_step, w_qkv, qk_gain, w_out, time_proj):
    frames, tok, _ = states.shape
    n_tm, n_seq, n_mp = (lax.axis_size(name) for name in ("tm", "seq", "mp"))
    z = lax.axis_index("tm")
    part = tok // n_mp
    depth, cols = w_qkv.shape[1:]
    window = frames * n_tm

    raw = list(spread(states, n_tm, part))
    for k in range(1, n_tm):
        raw[k] = turn(raw[k], "tm", k)
    near, far = [], []
    for blocks, kept in ((raw[0], near), (jnp.stack(raw[1:]), far)):
        for j in range(n_seq):
            side = turn(blocks, "seq", j) if j else blocks
            kept.append([side] + [turn(side, "mp", i) for i in range(1, n_mp)])

    shares = list(time_shares(start_step, time_proj, n_tm, window))
    for k in range(1, n_tm):
        shares[k] = turn(shares[k], "tm", k)

    shares_out = load_out(w_out, n_mp)
    weights = [turn(share, "mp", i) if i else share for i, share in enumerate(shares_out)]
    weights = [weights]
    for j in range(1, n_seq):
        weights.append([])
        for share in weights[0]:
            weights[j].append(turn(share, "seq", -j))

    groups = head_groups(cols)
    hidden, coef, held_qkv = modulate(start_step, w_qkv, groups[0][1], shares, near, far)
    hidden = hidden.reshape(n_tm, n_seq * frames * tok, depth)
    proj = []
    for h, (lane, size) in enumerate(groups):
        proj.append(
            jnp.einsum(
                "krd,cdh->kcrh",
                hidden,
                w_qkv[:, :, lane : lane + size] if h else held_qkv,
                preferred_element_type=jnp.float32,
            )
        )
    even = z % 2 == 0
    ev = [(i, i ^ 1) for i in range(n_tm)]
    od = []
    for i in range(n_tm):
        for c in range(n_mp):
            other = i + 1 if i % 2 else i - 1
            inside = 0 <= other < n_tm
            to = other * n_mp + c if inside else i * n_mp + (c + 1) % n_mp
            od.append((i * n_mp + c, to))

    def incoming(pair):
        first, second = (0.0 if p is None else p.astype(jnp.float32) for p in pair)
        right = jnp.where(z > 0, jnp.where(even, second, first), 0.0)
        return right, jnp.where(z < n_tm - 1, jnp.where(even, first, second), 0.0)

    flows = [(None, None)] * len(groups)
    for t in range(n_tm - 1):
        for h in range(len(groups)):
            right, left = proj[h][(t + 1) % n_tm], proj[h][n_tm - 1 - t]
            if t:
                more_right, more_left = incoming(flows[h])
                right, left = right + more_right, left + more_left
            first = jnp.where(even, right, left).astype(jnp.float16)
            second = jnp.where(even, left, right).astype(jnp.float16)
            first = lax.ppermute(first, "tm", ev)
            if t:
                second = lax.ppermute(second, ("tm", "mp"), od)
                first, second = lax.optimization_barrier((first, second))
            flows[h] = (first, second if t else None)
    gathered = []
    for h, (lane, size) in enumerate(groups):
        right, left = incoming(flows[h])
        total = proj[h][0] + right + left
        total = total.reshape(3, n_seq, frames, tok, size)
        attn = attend(total, qk_gain[:, lane : lane + size])
        attn = jnp.stack([attn[0]] + [turn(attn[j], "seq", -j) for j in range(1, n_seq)])
        pieces = [attn]
        for k in range(1, n_tm):
            pieces.append(turn(attn, "tm", k))
        gathered.append([[g] + [turn(g, "mp", i) for i in range(1, n_mp)] for g in pieces])

    own, *moved = project(
        gathered, weights, coef, (n_tm, n_seq, n_mp, frames, part, cols), groups
    )
    blocks = []
    for k in range(n_tm):
        block = moved[0]
        if k:
            block = turn(moved[k], "tm", -k)
        others = [turn(block, "mp", i) for i in range(1, n_mp)]
        blocks.append([block if k else own] + others)
    return finish(blocks)


def solution(mesh):
    return jax.shard_map(
        sweep,
        mesh=mesh,
        in_specs=(
            P(("group", "tm"), "seq", None),
            P("group"),
            P(None, "tm", ("seq", "mp")),
            P(None, ("seq", "mp")),
            P("tm", ("seq", "mp")),
            P("tm", None),
        ),
        out_specs=P(("group", "tm"), "seq", "mp"),
        check_vma=False,
    )
```
